512 devices in a mesh: pts: 128 (over z, y, core), ch: 4 (over x).
Axes of the slice: x: 4, y: 8, z: 8, core: 2. Of those that a mesh axis runs over, the one named last changes fastest.
Arguments:
- points_in: bfloat16 [65536, 256], P('pts'), may hold values from -6 to 6
- neighbor_offsets: int32 [65536, 16], P('pts'), may hold values from -128 to 128, as said below
- kernel_ids: int32 [65536, 16], P('pts'), may hold values from 0 to 26
- cluster_ids: int32 [65536], P('pts'), may hold values from 0 to 16383, as said below
- owners: int32 [65536], P('pts'), may hold values from 0 to 127, as said below
- conv_weight: bfloat16 [27, 256], replicated, may hold values from -1.5 to 1.5
- norm_gain: float32 [256], replicated, may hold values from 0.1 to 1.9
- norm_bias: float32 [256], replicated, may hold values from -3 to 3
- qkv_weight: bfloat16 [3, 256, 256], P(None, None, 'ch'), may hold values from -20 to 20
- proj_weight: bfloat16 [256, 256], replicated, may hold values from -1.5 to 1.5
- pool_weight: bfloat16 [256, 512], P(None, 'ch'), may hold values from -0.375 to 0.375
Outputs:
- block_out: bfloat16 [65536, 256], P('pts', 'ch')
- pooled: bfloat16 [16384, 512], P('pts', 'ch')
The draws below stay inside these ranges and needn't reach their ends.
Inputs may be any that keep to these rules, and one draw needn't show every extreme that they name: `owners`: each device's points name every owner at most 8 times; in every draw one owner is named exactly 8 times by the points of every device. `cluster_ids`: cluster ids never fall along the points, every cluster holds one or more points, the points of device i belong to clusters i * 128 - 1 .. i * 128 + 127, and only the first 1 to 3 points of a device (none on device 0) lie in cluster i * 128 - 1; some device has exactly 3 such points. `neighbor_offsets`: offsets -128 and 128 both occur.
All inputs are finite; a program needn't handle non-finite values.
Results may differ from the reference program's by a relative error of at most 0.017.
Values may be sent and summed in bfloat16 or wider, within the bound.
No kernel may reach another device: no remote copies, remote signals or barrier semaphores. Data moves between devices by JAX's collectives and lax.ppermute only.
A program may use at most 64 MiB of HBM per device.

```python
import math
import jax
import jax.numpy as jnp
from jax import lax

C = 256
HEADS = 8
HD = 32
PATCH = 1024
P_DEV = 512
POINTS = 65536
CAP = 8
RECV = 1024
NB = 16
K = 27
G = 128
SPILL = 3
M_DEV = 128
M = 16384
N_PTS = 128


def draw_owners(key, part):
    block_count = POINTS // P_DEV
    slot_total = block_count * CAP
    favored = jax.random.randint(jax.random.fold_in(key, 11), (), 0, block_count)
    owner_of = jnp.arange(slot_total, dtype=jnp.int32) // CAP
    slot_ids = jnp.arange(slot_total, dtype=jnp.int32)

    def one_block(block_key):
        bias_key = jax.random.fold_in(block_key, 1)
        score_key = jax.random.fold_in(block_key, 2)
        perm_key = jax.random.fold_in(block_key, 3)
        leaning = jax.random.randint(bias_key, (block_count,), 0, 4)
        noise = jax.random.randint(score_key, (slot_total,), 0, 1 << 14)
        levels = (3 - leaning[owner_of]) * (1 << 14) + noise + 1
        levels = jnp.where(owner_of == favored, 0, levels)
        scores = levels * slot_total + slot_ids
        order = jnp.argsort(scores, stable=True)
        chosen = owner_of[order[:P_DEV]]
        return chosen[jax.random.permutation(perm_key, P_DEV)]
    block_keys = jax.random.split(jax.random.fold_in(key, 12), block_count)
    return jax.vmap(one_block)(block_keys).reshape(POINTS).astype(jnp.int32)


def draw_cluster_ids(key, part):
    block_count = POINTS // P_DEV
    widest = jax.random.randint(jax.random.fold_in(key, 21), (), 1, block_count)
    positions = jnp.arange(P_DEV, dtype=jnp.int32)

    def one_block(block_key, block_index):
        lead_key = jax.random.fold_in(block_key, 1)
        cut_key = jax.random.fold_in(block_key, 2)
        leading = jax.random.randint(lead_key, (), 1, SPILL + 1)
        leading = jnp.where(block_index == widest, SPILL, leading)
        leading = jnp.where(block_index == 0, 0, leading)
        noise = jax.random.randint(cut_key, (P_DEV,), 0, (1 << 30) // P_DEV)
        scores = jnp.where(positions > leading, noise * P_DEV + positions, 2147483647)
        picked = jnp.argsort(scores, stable=True)[:M_DEV - 1]
        cuts = jnp.zeros((P_DEV,), jnp.int32).at[picked].set(1)
        within = jnp.cumsum(cuts)
        return jnp.where(positions < leading, block_index * M_DEV - 1, block_index * M_DEV + within)
    block_keys = jax.random.split(jax.random.fold_in(key, 22), block_count)
    block_ids = jnp.arange(block_count, dtype=jnp.int32)
    return jax.vmap(one_block)(block_keys, block_ids).reshape(POINTS).astype(jnp.int32)


def draw_neighbor_offsets(key, part):
    normal_draw = jax.random.randint(jax.random.fold_in(key, 31), (POINTS, NB), -G, G + 1)
    chosen_rows = jax.random.randint(jax.random.fold_in(key, 32), (2,), 0, POINTS)
    normal_draw = normal_draw.at[chosen_rows[0], 0].set(-G)
    normal_draw = normal_draw.at[chosen_rows[1], 1].set(G)
    return normal_draw.astype(jnp.int32)


def draw_qkv_weight(key, part):
    normal_draw = jax.random.normal(jax.random.fold_in(key, 41), (3, C, C), jnp.float32) * C ** (-0.5)
    normal_draw = jnp.clip(normal_draw, -6.0 * C ** (-0.5), 6.0 * C ** (-0.5))
    return normal_draw.astype(jnp.bfloat16)


def set_ends(array, own_key, least, top_value):
    dims = array.shape
    index_at = [jax.random.randint(jax.random.fold_in(own_key, axis), (), 0, dims[axis]) for axis in range(len(dims))]
    array = array.at[tuple(index_at)].set(least)
    longest = dims.index(max(dims))
    index_at[longest] = (index_at[longest] + 1) % dims[longest]
    return array.at[tuple(index_at)].set(top_value)


def level_of(key, shape, cuts, least, top_value):
    loudness, own = 1.0, jax.random.fold_in(key, 6)
    for axis_at, blocks in cuts:
        heights = jnp.exp(jax.random.uniform(jax.random.fold_in(own, axis_at), (blocks,), jnp.float32, least / len(cuts), top_value / len(cuts)))
        loudness = loudness * jnp.repeat(heights, shape[axis_at] // blocks).reshape([-1 if axis == axis_at else 1 for axis in range(len(shape))])
    return loudness


def bell_draw(rng, shape, scale, most, cuts=(), kind=jnp.bfloat16):
    values = jax.random.normal(rng, shape, jnp.float32) * scale
    if len(cuts) > 0:
        values = level_of(rng, shape, cuts, -0.22, 0.18) * values
    return jnp.clip(values, min=-most, max=most).astype(kind)


def setup_inputs(seed: int = 0) -> dict:
    splits = jax.random.split(jax.random.key(seed), 12)
    return {
        "points_in": bell_draw(splits[0], (POINTS, C), 1.0, 6.0, ((0, 128),)),
        "neighbor_offsets": draw_neighbor_offsets(jax.random.fold_in(splits[11], 71), 0),
        "kernel_ids": set_ends(jax.random.randint(splits[2], (POINTS, NB), 0, K), jax.random.fold_in(splits[2], 1), 0, K - 1).astype(jnp.int32),
        "cluster_ids": draw_cluster_ids(jax.random.fold_in(splits[11], 71), 0),
        "owners": draw_owners(jax.random.fold_in(splits[11], 71), 0),
        "conv_weight": bell_draw(splits[5], (K, C), 0.25, 1.5),
        "norm_gain": jnp.clip(1.0 + 0.18 * jax.random.normal(splits[6], (C,), jnp.float32), 0.1, 1.9),
        "norm_bias": bell_draw(splits[7], (C,), 0.5, 3.0, (), jnp.float32),
        "qkv_weight": draw_qkv_weight(jax.random.fold_in(splits[11], 71), 0),
        "proj_weight": bell_draw(splits[9], (C, C), (C // 16) ** -0.5, 1.5),
        "pool_weight": bell_draw(splits[10], (C, 2 * C), C ** -0.5, 0.375, ((1, 4),)),
    }


def attend_owner(rows_three, live_rows):
    patch_count = RECV // PATCH
    cube = rows_three.astype(jnp.float32).reshape(3, patch_count, PATCH, HEADS, HD)
    queries, key_rows, value_rows = (cube[0], cube[1], cube[2])
    score_scale = 1.0 / math.sqrt(HD)
    scores = jnp.einsum('pqhd,pkhd->phqk', queries, key_rows) * score_scale
    alive_keys = live_rows.reshape(patch_count, 1, 1, PATCH)
    scores = jnp.where(alive_keys, scores, -1e+30)
    row_max = lax.optimization_barrier(jnp.max(scores, axis=-1, keepdims=True))
    weights_f = jnp.exp(scores - row_max)
    denominator = lax.optimization_barrier(jnp.sum(weights_f, axis=-1))
    soft_weights = weights_f.astype(jnp.bfloat16).astype(jnp.float32)
    summed = jnp.einsum('phqk,pkhd->pqhd', soft_weights, value_rows)
    attended = summed / jnp.transpose(denominator, (0, 2, 1))[:, :, :, None]
    return attended.astype(jnp.bfloat16).reshape(RECV, C)

def reference(points_in, neighbor_offsets, kernel_ids, cluster_ids, owners, conv_weight, norm_gain, norm_bias, qkv_weight, proj_weight, pool_weight):
    point_total = points_in.shape[0]
    padded = jnp.pad(points_in, ((G, G), (0, 0)))
    offsets_base = jnp.arange(point_total, dtype=jnp.int32) + G
    kind_ids = jnp.arange(K, dtype=jnp.int32)
    conv = jnp.zeros((point_total, C), jnp.float32)
    for neighbor_slot in range(NB):
        selector = (kernel_ids[:, neighbor_slot][:, None] == kind_ids[None, :]).astype(jnp.bfloat16)
        weights_here = jnp.dot(selector, conv_weight, preferred_element_type=jnp.float32)
        picked = padded[offsets_base + neighbor_offsets[:, neighbor_slot]].astype(jnp.float32)
        conv = conv + weights_here * picked
    residual_rows = (points_in.astype(jnp.float32) + conv).astype(jnp.bfloat16)
    features = residual_rows.astype(jnp.float32)
    average = lax.optimization_barrier(jnp.mean(features, axis=1, keepdims=True))
    centered = features - average
    variance = lax.optimization_barrier(jnp.mean(centered * centered, axis=1, keepdims=True))
    normed_rows = (centered / jnp.sqrt(variance + 1e-05) * norm_gain + norm_bias).astype(jnp.bfloat16)
    qkv = jnp.stack([jnp.dot(normed_rows, qkv_weight[index_t], preferred_element_type=jnp.float32) for index_t in range(3)]).astype(jnp.bfloat16)
    block_count = point_total // P_DEV
    owner_blocks = owners.reshape(block_count, P_DEV)
    peer_ids = jnp.arange(N_PTS, dtype=jnp.int32)
    dest_marks = (owner_blocks[:, :, None] == peer_ids[None, None, :]).astype(jnp.int32)
    earlier_count = jnp.cumsum(dest_marks, axis=1) - dest_marks
    slot_index = lax.optimization_barrier(jnp.sum(earlier_count * dest_marks, axis=2)).reshape(point_total)
    block_ids = jnp.arange(point_total, dtype=jnp.int32) // P_DEV
    position = owners * RECV + block_ids * CAP + slot_index
    source_of = jnp.full((N_PTS * RECV,), point_total, jnp.int32).at[position].set(jnp.arange(point_total, dtype=jnp.int32))
    qkv_ext = jnp.concatenate([qkv, jnp.zeros((3, 1, C), jnp.bfloat16)], axis=1)

    def per_owner(owner_index):
        ids = lax.dynamic_slice_in_dim(source_of, owner_index * RECV, RECV)
        rows_three = qkv_ext[:, ids, :]
        return attend_owner(rows_three, ids < point_total)
    attended = lax.map(per_owner, jnp.arange(N_PTS, dtype=jnp.int32))
    returned = attended.reshape(N_PTS * RECV, C)[position]
    block_out = (residual_rows.astype(jnp.float32) + jnp.dot(returned, proj_weight, preferred_element_type=jnp.float32)).astype(jnp.bfloat16)
    lifted = jnp.dot(block_out, pool_weight, preferred_element_type=jnp.float32)
    cluster_sums = jax.ops.segment_sum(lifted, cluster_ids, num_segments=M)
    cluster_counts = jax.ops.segment_sum(jnp.ones((point_total,), jnp.float32), cluster_ids, num_segments=M)
    pooled = jax.nn.gelu(cluster_sums / cluster_counts[:, None], approximate=False).astype(jnp.bfloat16)
    return (block_out, pooled)
```

```python
import functools
import math

import jax
import jax.numpy as jnp
from jax import lax
from jax.experimental import pallas as pl
from jax.experimental.pallas import tpu as pltpu
from jax.sharding import PartitionSpec as P

HD = 32
G = 128
ROWS = 128
HALF_SLOTS = 4
DEAD = -1e30
BF = jnp.bfloat16
F32 = jnp.float32
VMEM_BYTES = 24 * 1024 * 1024


def call(body, outs, scratch=(), flops=0, nbytes=0, name=None):
    def run(*args):
        return pl.pallas_call(
            body,
            out_shape=outs,
            in_specs=[pl.BlockSpec(memory_space=pltpu.VMEM)] * len(args),
            out_specs=jax.tree.map(lambda _: pl.BlockSpec(memory_space=pltpu.VMEM), outs),
            scratch_shapes=list(scratch),
            compiler_params=pltpu.CompilerParams(vmem_limit_bytes=VMEM_BYTES),
            cost_estimate=pl.CostEstimate(flops=flops, bytes_accessed=nbytes, transcendentals=0),
            name=name,
        )(*args)

    return run


def iota(shape, dim):
    return lax.broadcasted_iota(jnp.int32, shape, dim)


def hot(mask):
    return jnp.where(mask, 1.0, 0.0).astype(BF)


def dot(a, b):
    return lax.dot_general(a, b, (((1,), (0,)), ((), ())), preferred_element_type=F32)


def dot_t(a, b):
    return lax.dot_general(a, b, (((1,), (1,)), ((), ())), preferred_element_type=F32)


def conv_norm_block(points, window, offsets, kinds, weights, gain, bias):
    rows, span = points.shape[0], window.shape[0]
    target = offsets + iota(offsets.shape, 0) + G
    conv = jnp.zeros(points.shape, F32)
    group = 4
    for first in range(0, offsets.shape[1], group):
        picks = [hot(target[:, n : n + 1] == iota((rows, span), 1)) for n in range(first, first + group)]
        marks = [
            hot(kinds[:, n : n + 1] == iota((rows, weights.shape[0]), 1))
            for n in range(first, first + group)
        ]
        picked = dot(jnp.concatenate(picks, axis=0), window)
        scale = dot(jnp.concatenate(marks, axis=0), weights)
        part = picked * scale
        for n in range(group):
            conv = conv + part[n * rows : (n + 1) * rows]
    residual = (points.astype(F32) + conv).astype(BF)
    features = residual.astype(F32)
    average = jnp.mean(features, axis=1, keepdims=True)
    centered = features - average
    variance = jnp.mean(centered * centered, axis=1, keepdims=True)
    normed = (centered * lax.rsqrt(variance + 1e-05) * gain + bias).astype(BF)
    return residual, normed


def padded_weights(conv_weight):
    kinds = conv_weight.shape[0]
    fill = jnp.zeros((32 - kinds, conv_weight.shape[1]), F32)
    return jnp.concatenate([conv_weight.astype(F32), fill], axis=0).astype(BF)


def front_inner(points, offsets, kinds, owners, conv_weight, gain, bias, residual, normed, place, fetch, dead):
    total = points.shape[0]
    weights = padded_weights(conv_weight[...])
    for block in range(1, total // ROWS - 1):
        rows = slice(block * ROWS, (block + 1) * ROWS)
        window = points[block * ROWS - G : (block + 1) * ROWS + G, :]
        res, nor = conv_norm_block(
            points[rows, :], window, offsets[rows, :], kinds[rows, :], weights, gain[...], bias[...]
        )
        out = slice((block - 1) * ROWS, block * ROWS)
        residual[out, :] = res
        normed[out, :] = nor
    peers = place.shape[0] // HALF_SLOTS
    own = owners[...]
    match = iota((peers, total), 0) == own
    marks = hot(match)
    before = hot(iota((total, total), 0) < iota((total, total), 1))
    earlier = dot(marks, before)
    slot = jnp.sum(jnp.where(match, earlier, 0.0), axis=0, keepdims=True).astype(jnp.int32)
    low = own * HALF_SLOTS + (slot & (HALF_SLOTS - 1))
    high = slot >= HALF_SLOTS
    rows = place.shape[0]
    ups = iota((rows, total), 0)
    place_a = jnp.where(ups == jnp.where(high, -1, low), 1.0, 0.0)
    place_b = jnp.where(ups == jnp.where(high, low, -1), 1.0, 0.0)
    place[:, :total] = place_a.astype(BF)
    place[:, total:] = place_b.astype(BF)
    live_a = jnp.sum(place_a, axis=1, keepdims=True)
    live_b = jnp.sum(place_b, axis=1, keepdims=True)
    lane = iota((rows, 128), 1)
    dead[...] = jnp.where(jnp.where(lane < 64, live_a, live_b) > 0.5, 0.0, DEAD)
    spot = jnp.where(high, low + rows, low).astype(F32)
    column = jnp.transpose(jnp.broadcast_to(spot, (8, total)))[:, 0:1]
    fetch[...] = hot(column.astype(jnp.int32) == iota((total, 2 * rows), 1))


def front_edges(
    above, points, below, offsets, kinds, conv_weight, gain, bias, qkv_weight, inner, place, dead, residual, out, normed
):
    total = points.shape[0]
    weights = padded_weights(conv_weight[...])
    last = total - ROWS
    for start, window in (
        (0, jnp.concatenate([above[...], points[0 : ROWS + G, :]], axis=0)),
        (last, jnp.concatenate([points[last - G :, :], below[...]], axis=0)),
    ):
        rows = slice(start, start + ROWS)
        res, nor = conv_norm_block(
            points[rows, :], window, offsets[rows, :], kinds[rows, :], weights, gain[...], bias[...]
        )
        residual[(0 if start == 0 else ROWS) : (ROWS if start == 0 else 2 * ROWS), :] = res
        normed[rows, :] = nor
    normed[ROWS:last, :] = inner[...]
    q, k, v = (qkv_weight[t] for t in range(3))
    none = jnp.zeros(q.shape, BF)
    left = jnp.concatenate([q, none, k, none, v, none], axis=1)
    right = jnp.concatenate([none, q, none, k, none, v], axis=1)
    rows_in = normed[...]
    stacked = jnp.concatenate(
        [dot(rows_in, left).astype(BF), dot(rows_in, right).astype(BF)], axis=0
    )
    packed = dot(place[...], stacked)
    out[:, 0:128] = (packed[:, 0:128] + dead[...]).astype(BF)
    out[:, 128:] = packed[:, 128:].astype(BF)


def swap_halves(value):
    return jnp.concatenate([value[:, 64:], value[:, :64]], axis=1)


def attend(packed, out, keys, queries, values):
    half = packed.shape[0]
    lane = iota((half, 128), 1)
    q = packed[:, 0:128]
    k = packed[:, 128:256]
    v = packed[:, 256:384]
    qs, ks, vs = (swap_halves(x) for x in (q, k, v))
    zero = jnp.zeros((half, 128), F32)

    def dead_bias(x):
        return jnp.where(x.astype(F32) < 0.1 * DEAD, DEAD, 0.0)

    for part, (qq, kk, vv, flag) in enumerate(((q, k, v, qs), (qs, ks, vs, q))):
        rows = slice(part * half, (part + 1) * half)
        qf, kf, vf = (x.astype(F32) for x in (qq, kk, vv))
        keys[rows, :] = jnp.where(lane < 64, kf, jnp.where(lane == 64, dead_bias(flag), 0.0)).astype(BF)
        extra = jnp.where(lane == 64, 1.0, zero)
        for head in range(2):
            mine = (lane >= head * HD) & (lane < (head + 1) * HD)
            queries[head, rows, :] = jnp.where(mine, qf, extra).astype(BF)
            values[head, rows, :] = jnp.where(mine, vf, extra).astype(BF)
    factor = math.log2(math.e) / math.sqrt(HD)
    step = 128

    def one(index):
        base = pl.multiple_of(index * step, step)
        halves = []
        for part in range(2):
            results = []
            for head in range(2):
                mine = queries[head, pl.ds(part * half + base, step), :]
                scores = dot_t(mine, keys[...])
                top = jnp.max(scores, axis=1, keepdims=True)
                soft = jnp.exp2((scores - top) * factor).astype(BF)
                summed = dot(soft, values[head])
                results.append(summed / summed[:, 64:65])
            block_lane = iota((step, 128), 1)
            halves.append(jnp.where(block_lane < HD, results[0], results[1]))
        moved = jnp.concatenate([halves[1][:, 64:], halves[1][:, :64]], axis=1)
        block_lane = iota((step, 128), 1)
        out[pl.ds(base, step), :] = jnp.where(block_lane < 64, halves[0], moved).astype(BF)

    pl.loop(0, half // step)(one)


def fetch_rows(returned, fetch, out):
    half = returned.shape[0]
    value = returned[...]
    lane = iota((half, 128), 1)
    zero = jnp.zeros((half, 128), BF)
    moved = swap_halves(value)
    left = jnp.concatenate([jnp.where(lane < 64, value, zero), jnp.where(lane < 64, moved, zero)], axis=0)
    right = jnp.concatenate([jnp.where(lane < 64, zero, moved), jnp.where(lane < 64, zero, value)], axis=0)
    points = fetch.shape[0] // 2
    rows = (dot(fetch[:points, :], left) + dot(fetch[points:, :], right)).astype(BF)
    for peer in range(out.shape[0]):
        out[peer] = rows


def finish(gathered, edge_res, inner_res, proj_weight, clusters, block_out, sums, block):
    channels = gathered.shape[0]
    width = proj_weight.shape[1]
    part = width // channels
    wide = jnp.concatenate([gathered[c] for c in range(channels)], axis=1)
    proj = proj_weight[...]
    none = jnp.zeros((part, width), BF)
    low, high = [], []
    for c in range(channels):
        piece = proj[c * part : (c + 1) * part, :]
        low += [piece, none]
        high += [none, piece]
    points = block.shape[0] // 2
    last = 2 * points - ROWS
    first = dot(wide, jnp.concatenate(low, axis=0))
    second = dot(wide, jnp.concatenate(high, axis=0))
    block[0:ROWS, :] = (edge_res[0:ROWS, :].astype(F32) + first[0:ROWS]).astype(BF)
    block[ROWS:points, :] = (inner_res[0 : points - ROWS, :].astype(F32) + first[ROWS:]).astype(BF)
    block[points:last, :] = (inner_res[points - ROWS :, :].astype(F32) + second[: last - points]).astype(BF)
    block[last:, :] = (edge_res[ROWS:, :].astype(F32) + second[last - points :]).astype(BF)
    full = block[...]
    channel = lax.axis_index("ch")
    pick = hot(iota((width, part), 0) == iota((width, part), 1) + channel * part)
    block_out[...] = dot(full, pick).astype(BF)
    count = 2 * points // 4
    base = lax.axis_index("pts") * count - 1
    rows = sums.shape[0]
    member = jnp.where(iota((rows, 2 * points), 0) == clusters[...] - base, 1.0, 0.0)
    sums[:, :width] = dot(member.astype(BF), full)
    sums[:, width:] = jnp.broadcast_to(jnp.sum(member, axis=1, keepdims=True), (rows, 128))


def pool(sums, spill, pool_weight, out):
    count = out.shape[0]
    width = pool_weight.shape[0]
    own = sums[1 : count + 1, :]
    total = jnp.where(iota(own.shape, 0) == count - 1, own + spill[0:1, :], own)
    value = total[:, :width]
    high = value.astype(BF)
    low = (value - high.astype(F32)).astype(BF)
    weight = pool_weight[...]
    lifted = dot(high, weight) + dot(low, weight)
    mean = lifted / total[:, width:]
    out[...] = (mean * (1.0 + lax.erf(mean * math.sqrt(0.5))) * 0.5).astype(BF)


def shape(dims, kind=BF):
    return jax.ShapeDtypeStruct(dims, kind)


def shards(
    points_in,
    neighbor_offsets,
    kernel_ids,
    cluster_ids,
    owners,
    conv_weight,
    norm_gain,
    norm_bias,
    qkv_weight,
    proj_weight,
    pool_weight,
):
    total, width = points_in.shape
    nodes = lax.axis_size("pts")
    channels = lax.axis_size("ch")
    up = [(i, i + 1) for i in range(nodes - 1)]
    down = [(j, i) for i, j in up]
    above = lax.ppermute(points_in[total - G :], "pts", up)
    below = lax.ppermute(points_in[:G], "pts", down)
    gain, bias = norm_gain.reshape(1, width), norm_bias.reshape(1, width)
    slots = nodes * HALF_SLOTS
    inner_rows = total - 2 * ROWS
    inner_res, inner_normed, place, fetch, dead = call(
        front_inner,
        (
            shape((inner_rows, width)),
            shape((inner_rows, width)),
            shape((slots, 2 * total)),
            shape((total, 2 * slots)),
            shape((slots, 128), F32),
        ),
        flops=10**9,
        nbytes=4 * 10**6,
        name="front_inner",
    )(points_in, neighbor_offsets, kernel_ids, owners.reshape(1, total), conv_weight, gain, bias)
    edge_res, packed = call(
        front_edges,
        (shape((2 * ROWS, width)), shape((slots, 384))),
        scratch=(pltpu.VMEM((total, width), BF),),
        flops=10**9,
        nbytes=4 * 10**6,
        name="front_edges",
    )(
        above,
        points_in,
        below,
        neighbor_offsets,
        kernel_ids,
        conv_weight,
        gain,
        bias,
        qkv_weight,
        inner_normed,
        place,
        dead,
    )
    arrived = lax.all_to_all(
        packed.reshape(nodes, HALF_SLOTS, 384), "pts", split_axis=0, concat_axis=0, tiled=True
    ).reshape(slots, 384)
    attended = call(
        attend,
        shape((slots, 128)),
        scratch=(
            pltpu.VMEM((2 * slots, 128), BF),
            pltpu.VMEM((2, 2 * slots, 128), BF),
            pltpu.VMEM((2, 2 * slots, 128), BF),
        ),
        flops=10**9,
        nbytes=10**6,
        name="attend",
    )(arrived)
    returned = lax.all_to_all(
        attended.reshape(nodes, HALF_SLOTS, 128), "pts", split_axis=0, concat_axis=0, tiled=True
    ).reshape(slots, 128)
    rows = call(
        fetch_rows, shape((channels, total // 2, 128)), flops=10**8, nbytes=10**6, name="fetch_rows"
    )(returned, fetch)
    gathered = lax.all_to_all(rows, "ch", split_axis=0, concat_axis=0, tiled=True)
    clusters = total // 4
    block_out, sums = call(
        finish,
        (shape((total, width // channels)), shape((clusters + 8, width + 128), F32)),
        scratch=(pltpu.VMEM((total, width), BF),),
        flops=10**8,
        nbytes=10**6,
        name="finish",
    )(gathered, edge_res, inner_res, proj_weight, cluster_ids.reshape(1, total))
    spill = lax.ppermute(sums[:8], "pts", down)
    pooled = call(pool, shape((clusters, pool_weight.shape[1])), flops=10**7, nbytes=10**5, name="pool")(
        sums, spill, pool_weight
    )
    return block_out, pooled


def solution(mesh):
    return jax.shard_map(
        shards,
        mesh=mesh,
        in_specs=(
            P("pts", None),
            P("pts", None),
            P("pts", None),
            P("pts"),
            P("pts"),
            P(),
            P(),
            P(),
            P(None, None, "ch"),
            P(),
            P(None, "ch"),
        ),
        out_specs=(P("pts", "ch"), P("pts", "ch")),
        check_vma=False,
    )
```

```python
import functools
import math

import jax
import jax.numpy as jnp
from jax import lax
from jax.experimental import pallas as pl
from jax.experimental.pallas import tpu as pltpu
from jax.sharding import PartitionSpec as P

HD = 32
G = 128
ROWS = 128
HALF_SLOTS = 4
DEAD = -1e30
BF = jnp.bfloat16
F32 = jnp.float32
VMEM_BYTES = 24 * 1024 * 1024


def call(body, outs, scratch=(), flops=0, nbytes=0, name=None):
    def run(*args):
        return pl.pallas_call(
            body,
            out_shape=outs,
            in_specs=[pl.BlockSpec(memory_space=pltpu.VMEM)] * len(args),
            out_specs=jax.tree.map(lambda _: pl.BlockSpec(memory_space=pltpu.VMEM), outs),
            scratch_shapes=list(scratch),
            compiler_params=pltpu.CompilerParams(vmem_limit_bytes=VMEM_BYTES),
            cost_estimate=pl.CostEstimate(flops=flops, bytes_accessed=nbytes, transcendentals=0),
            name=name,
        )(*args)

    return run


def iota(shape, dim):
    return lax.broadcasted_iota(jnp.int32, shape, dim)


def hot(mask):
    return jnp.where(mask, 1.0, 0.0).astype(BF)


def dot(a, b):
    return lax.dot_general(a, b, (((1,), (0,)), ((), ())), preferred_element_type=F32)


def dot_t(a, b):
    return lax.dot_general(a, b, (((1,), (1,)), ((), ())), preferred_element_type=F32)


def stage(count):
    def body(*refs):
        sources, targets, sems = refs[:count], refs[count:-1], refs[-1]
        pairs = list(zip(sources, targets[:count], strict=True))
        points = sources[0]
        pairs.append((points.at[pl.ds(points.shape[0] - G, G), :], targets[count]))
        pairs.append((points.at[pl.ds(0, G), :], targets[count + 1]))
        copies = [pltpu.make_async_copy(a, b, sems.at[n]) for n, (a, b) in enumerate(pairs)]
        for copy in copies:
            copy.start()
        for copy in copies:
            copy.wait()

    def run(*args):
        outs = [jax.ShapeDtypeStruct(a.shape, a.dtype) for a in args]
        outs += [jax.ShapeDtypeStruct((G, args[0].shape[1]), args[0].dtype)] * 2
        return pl.pallas_call(
            body,
            out_shape=outs,
            in_specs=[pl.BlockSpec(memory_space=pltpu.HBM)] * count,
            out_specs=[pl.BlockSpec(memory_space=pltpu.VMEM)] * (count + 2),
            scratch_shapes=[pltpu.SemaphoreType.DMA((count + 2,))],
            compiler_params=pltpu.CompilerParams(vmem_limit_bytes=VMEM_BYTES),
            name="stage",
        )(*(pltpu.with_memory_space_constraint(a, pltpu.HBM) for a in args))

    return run


def conv_norm_block(points, window, offsets, kinds, weights, gain, bias):
    rows, span = points.shape[0], window.shape[0]
    offsets, kinds = jnp.transpose(offsets), jnp.transpose(kinds)
    target = offsets + iota(offsets.shape, 0) + G
    conv = jnp.zeros(points.shape, F32)
    group = 4
    for first in range(0, offsets.shape[1], group):
        picks = [hot(target[:, n : n + 1] == iota((rows, span), 1)) for n in range(first, first + group)]
        marks = [
            hot(kinds[:, n : n + 1] == iota((rows, weights.shape[0]), 1))
            for n in range(first, first + group)
        ]
        picked = dot(jnp.concatenate(picks, axis=0), window)
        scale = dot(jnp.concatenate(marks, axis=0), weights)
        part = picked * scale
        for n in range(group):
            conv = conv + part[n * rows : (n + 1) * rows]
    residual = (points.astype(F32) + conv).astype(BF)
    features = residual.astype(F32)
    average = jnp.mean(features, axis=1, keepdims=True)
    centered = features - average
    variance = jnp.mean(centered * centered, axis=1, keepdims=True)
    normed = (centered * lax.rsqrt(variance + 1e-05) * gain + bias).astype(BF)
    return residual, normed


def padded_weights(conv_weight):
    kinds = conv_weight.shape[0]
    fill = jnp.zeros((32 - kinds, conv_weight.shape[1]), F32)
    return jnp.concatenate([conv_weight.astype(F32), fill], axis=0).astype(BF)


def front_inner(points, offsets, kinds, owners, conv_weight, gain, bias, residual, normed, place, fetch, dead):
    total = points.shape[0]
    weights = padded_weights(conv_weight[...])
    for block in range(1, total // ROWS - 1):
        rows = slice(block * ROWS, (block + 1) * ROWS)
        window = points[block * ROWS - G : (block + 1) * ROWS + G, :]
        res, nor = conv_norm_block(
            points[rows, :], window, offsets[:, rows], kinds[:, rows], weights, gain[...], bias[...]
        )
        out = slice((block - 1) * ROWS, block * ROWS)
        residual[out, :] = res
        normed[out, :] = nor
    peers = place.shape[0] // HALF_SLOTS
    own = owners[...]
    match = iota((peers, total), 0) == own
    marks = hot(match)
    before = hot(iota((total, total), 0) < iota((total, total), 1))
    earlier = dot(marks, before)
    slot = jnp.sum(jnp.where(match, earlier, 0.0), axis=0, keepdims=True).astype(jnp.int32)
    low = own * HALF_SLOTS + (slot & (HALF_SLOTS - 1))
    high = slot >= HALF_SLOTS
    rows = place.shape[0]
    ups = iota((rows, total), 0)
    place_a = jnp.where(ups == jnp.where(high, -1, low), 1.0, 0.0)
    place_b = jnp.where(ups == jnp.where(high, low, -1), 1.0, 0.0)
    place[:, :total] = place_a.astype(BF)
    place[:, total:] = place_b.astype(BF)
    live_a = jnp.sum(place_a, axis=1, keepdims=True)
    live_b = jnp.sum(place_b, axis=1, keepdims=True)
    lane = iota((rows, 128), 1)
    dead[...] = jnp.where(jnp.where(lane < 64, live_a, live_b) > 0.5, 0.0, DEAD)
    spot = jnp.where(high, low + rows, low).astype(F32)
    column = jnp.transpose(jnp.broadcast_to(spot, (8, total)))[:, 0:1]
    fetch[...] = hot(column.astype(jnp.int32) == iota((total, 2 * rows), 1))


def front_edges(
    above, points, below, offsets, kinds, conv_weight, gain, bias, qkv_weight, inner, place, dead, residual, out, normed
):
    total = points.shape[0]
    weights = padded_weights(conv_weight[...])
    last = total - ROWS
    for start, window in (
        (0, jnp.concatenate([above[...], points[0 : ROWS + G, :]], axis=0)),
        (last, jnp.concatenate([points[last - G :, :], below[...]], axis=0)),
    ):
        rows = slice(start, start + ROWS)
        res, nor = conv_norm_block(
            points[rows, :], window, offsets[:, rows], kinds[:, rows], weights, gain[...], bias[...]
        )
        residual[(0 if start == 0 else ROWS) : (ROWS if start == 0 else 2 * ROWS), :] = res
        normed[rows, :] = nor
    normed[ROWS:last, :] = inner[...]
    q, k, v = (qkv_weight[t] for t in range(3))
    none = jnp.zeros(q.shape, BF)
    left = jnp.concatenate([q, none, k, none, v, none], axis=0)
    right = jnp.concatenate([none, q, none, k, none, v], axis=0)
    rows_in = normed[...]
    stacked = jnp.concatenate(
        [dot_t(rows_in, left).astype(BF), dot_t(rows_in, right).astype(BF)], axis=0
    )
    packed = dot(place[...], stacked)
    out[:, 0:128] = (packed[:, 0:128] + dead[...]).astype(BF)
    out[:, 128:] = packed[:, 128:].astype(BF)


def swap_halves(value):
    return jnp.concatenate([value[:, 64:], value[:, :64]], axis=1)


def attend(packed, out, keys, queries, values):
    half = packed.shape[0]
    lane = iota((half, 128), 1)
    q = packed[:, 0:128]
    k = packed[:, 128:256]
    v = packed[:, 256:384]
    qs, ks, vs = (swap_halves(x) for x in (q, k, v))
    zero = jnp.zeros((half, 128), F32)

    def dead_bias(x):
        return jnp.where(x.astype(F32) < 0.1 * DEAD, DEAD, 0.0)

    step = 128
    for part, (qq, kk, vv, flag) in enumerate(((q, k, v, qs), (qs, ks, vs, q))):
        rows = slice(part * half, (part + 1) * half)
        qf, kf, vf = (x.astype(F32) for x in (qq, kk, vv))
        keys[rows, :] = jnp.where(lane < 64, kf, jnp.where(lane == 64, dead_bias(flag), 0.0)).astype(BF)
        extra = jnp.where(lane == 64, 1.0, zero)
        values[rows, :] = jnp.where(lane < 64, vf, extra).astype(BF)
        for head in range(2):
            mine = (lane >= head * HD) & (lane < (head + 1) * HD)
            query = jnp.where(mine, qf, extra).astype(BF)
            for index in range(half // step):
                start = (index * 4 + part * 2 + head) * step
                queries[start : start + step, :] = query[index * step : (index + 1) * step, :]
    factor = math.log2(math.e) / math.sqrt(HD)

    def one(index):
        mine = queries[pl.ds(pl.multiple_of(index * 4 * step, 4 * step), 4 * step), :]
        scores = dot_t(mine, keys[...])
        top = jnp.max(scores, axis=1, keepdims=True)
        soft = jnp.exp2((scores - top) * factor).astype(BF)
        summed = dot(soft, values[...])
        result = summed / summed[:, 64:65]
        pieces = [result[n * step : (n + 1) * step] for n in range(4)]
        block_lane = iota((step, 128), 1)
        first = jnp.where(block_lane < HD, pieces[0], pieces[1])
        second = jnp.where(block_lane < HD, pieces[2], pieces[3])
        moved = jnp.concatenate([second[:, 64:], second[:, :64]], axis=1)
        rows = pl.ds(pl.multiple_of(index * step, step), step)
        out[rows, :] = jnp.where(block_lane < 64, first, moved).astype(BF)

    pl.loop(0, half // step)(one)


def fetch_rows(returned, fetch, out):
    half = returned.shape[0]
    value = returned[...]
    lane = iota((half, 128), 1)
    zero = jnp.zeros((half, 128), BF)
    moved = swap_halves(value)
    left = jnp.concatenate([jnp.where(lane < 64, value, zero), jnp.where(lane < 64, moved, zero)], axis=0)
    right = jnp.concatenate([jnp.where(lane < 64, zero, moved), jnp.where(lane < 64, zero, value)], axis=0)
    points = fetch.shape[0] // 2
    rows = (dot(fetch[:points, :], left) + dot(fetch[points:, :], right)).astype(BF)
    for peer in range(out.shape[0]):
        out[peer] = rows


def finish(gathered, edge_res, inner_res, proj_weight, clusters, block_out, sums, block):
    channels = gathered.shape[0]
    width = proj_weight.shape[1]
    part = width // channels
    wide = jnp.concatenate([gathered[c] for c in range(channels)], axis=1)
    proj = proj_weight[...]
    none = jnp.zeros((part, width), BF)
    low, high = [], []
    for c in range(channels):
        piece = proj[c * part : (c + 1) * part, :]
        low += [piece, none]
        high += [none, piece]
    points = block.shape[0] // 2
    last = 2 * points - ROWS
    first = dot(wide, jnp.concatenate(low, axis=0))
    second = dot(wide, jnp.concatenate(high, axis=0))
    block[0:ROWS, :] = (edge_res[0:ROWS, :].astype(F32) + first[0:ROWS]).astype(BF)
    block[ROWS:points, :] = (inner_res[0 : points - ROWS, :].astype(F32) + first[ROWS:]).astype(BF)
    block[points:last, :] = (inner_res[points - ROWS :, :].astype(F32) + second[: last - points]).astype(BF)
    block[last:, :] = (edge_res[ROWS:, :].astype(F32) + second[last - points :]).astype(BF)
    full = block[...]
    channel = lax.axis_index("ch")
    pick = hot(iota((part, width), 1) == iota((part, width), 0) + channel * part)
    block_out[...] = dot_t(pick, full).astype(BF)
    count = 2 * points // 4
    base = lax.axis_index("pts") * count - 1
    rows = sums.shape[0]
    member = jnp.where(iota((rows, 2 * points), 0) == clusters[...] - base, 1.0, 0.0)
    sums[:, :width] = dot(member.astype(BF), full)
    sums[:, width:] = jnp.broadcast_to(jnp.sum(member, axis=1, keepdims=True), (rows, 128))


def pool(sums, spill, pool_weight, out):
    count = out.shape[0]
    width = pool_weight.shape[0]
    own = sums[1 : count + 1, :]
    total = jnp.where(iota(own.shape, 0) == count - 1, own + spill[0:1, :], own)
    value = total[:, :width]
    high = value.astype(BF)
    low = (value - high.astype(F32)).astype(BF)
    weight = pool_weight[...]
    lifted = dot(high, weight) + dot(low, weight)
    mean = lifted / total[:, width:]
    out[...] = (mean * (1.0 + lax.erf(mean * math.sqrt(0.5))) * 0.5).astype(BF)


def shape(dims, kind=BF):
    return jax.ShapeDtypeStruct(dims, kind)


def shards(
    points_in,
    neighbor_offsets,
    kernel_ids,
    cluster_ids,
    owners,
    conv_weight,
    norm_gain,
    norm_bias,
    qkv_weight,
    proj_weight,
    pool_weight,
):
    total, width = points_in.shape
    nodes = lax.axis_size("pts")
    channels = lax.axis_size("ch")
    up = [(i, i + 1) for i in range(nodes - 1)]
    down = [(j, i) for i, j in up]
    offsets, kinds = jnp.transpose(neighbor_offsets), jnp.transpose(kernel_ids)
    args = (
        points_in,
        offsets,
        kinds,
        owners.reshape(1, total),
        conv_weight,
        norm_gain.reshape(1, width),
        norm_bias.reshape(1, width),
        jnp.transpose(qkv_weight, (0, 2, 1)),
        proj_weight,
        pool_weight,
        cluster_ids.reshape(1, total),
    )
    staged = stage(len(args))(*args)
    points, offsets, kinds, own, conv_weight, gain, bias, qkv_weight, proj_weight, pool_weight = staged[:10]
    clusters_here, tail, head = staged[10:]
    above = lax.ppermute(tail, "pts", up)
    below = lax.ppermute(head, "pts", down)
    slots = nodes * HALF_SLOTS
    inner_rows = total - 2 * ROWS
    inner_res, inner_normed, place, fetch, dead = call(
        front_inner,
        (
            shape((inner_rows, width)),
            shape((inner_rows, width)),
            shape((slots, 2 * total)),
            shape((total, 2 * slots)),
            shape((slots, 128), F32),
        ),
        flops=10**9,
        nbytes=4 * 10**6,
        name="front_inner",
    )(points, offsets, kinds, own, conv_weight, gain, bias)
    edge_res, packed = call(
        front_edges,
        (shape((2 * ROWS, width)), shape((slots, 384))),
        scratch=(pltpu.VMEM((total, width), BF),),
        flops=10**9,
        nbytes=4 * 10**6,
        name="front_edges",
    )(
        above,
        points,
        below,
        offsets,
        kinds,
        conv_weight,
        gain,
        bias,
        qkv_weight,
        inner_normed,
        place,
        dead,
    )
    arrived = lax.all_to_all(
        packed.reshape(nodes, HALF_SLOTS, 384), "pts", split_axis=0, concat_axis=0, tiled=True
    ).reshape(slots, 384)
    attended = call(
        attend,
        shape((slots, 128)),
        scratch=(
            pltpu.VMEM((2 * slots, 128), BF),
            pltpu.VMEM((4 * slots, 128), BF),
            pltpu.VMEM((2 * slots, 128), BF),
        ),
        flops=10**9,
        nbytes=10**6,
        name="attend",
    )(arrived)
    returned = lax.all_to_all(
        attended.reshape(nodes, HALF_SLOTS, 128), "pts", split_axis=0, concat_axis=0, tiled=True
    ).reshape(slots, 128)
    rows = call(
        fetch_rows, shape((channels, total // 2, 128)), flops=10**8, nbytes=10**6, name="fetch_rows"
    )(returned, fetch)
    gathered = lax.all_to_all(rows, "ch", split_axis=0, concat_axis=0, tiled=True)
    clusters = total // 4
    block_out, sums = call(
        finish,
        (shape((width // channels, total)), shape((clusters + 8, width + 128), F32)),
        scratch=(pltpu.VMEM((total, width), BF),),
        flops=10**8,
        nbytes=10**6,
        name="finish",
    )(gathered, edge_res, inner_res, proj_weight, clusters_here)
    spill = lax.ppermute(sums[:8], "pts", down)
    pooled = call(pool, shape((clusters, pool_weight.shape[1])), flops=10**7, nbytes=10**5, name="pool")(
        sums, spill, pool_weight
    )
    return jnp.transpose(block_out), pooled


def solution(mesh):
    return jax.shard_map(
        shards,
        mesh=mesh,
        in_specs=(
            P("pts", None),
            P("pts", None),
            P("pts", None),
            P("pts"),
            P("pts"),
            P(),
            P(),
            P(),
            P(None, None, "ch"),
            P(),
            P(None, "ch"),
        ),
        out_specs=(P("pts", "ch"), P("pts", "ch")),
        check_vma=False,
    )
```

```python
import functools
import math

import jax
import jax.numpy as jnp
from jax import lax
from jax.experimental import pallas as pl
from jax.experimental.pallas import tpu as pltpu
from jax.sharding import PartitionSpec as P

HD = 32
G = 128
ROWS = 128
HALF_SLOTS = 4
DEAD = -1e30
SHIFT_BITS = 10
SHIFT = 1 << SHIFT_BITS
BF = jnp.bfloat16
F32 = jnp.float32
VMEM_BYTES = 24 * 1024 * 1024


def call(body, outs, scratch=(), flops=0, nbytes=0, name=None):
    def run(*args):
        return pl.pallas_call(
            body,
            out_shape=outs,
            in_specs=[pl.BlockSpec(memory_space=pltpu.VMEM)] * len(args),
            out_specs=jax.tree.map(lambda _: pl.BlockSpec(memory_space=pltpu.VMEM), outs),
            scratch_shapes=list(scratch),
            compiler_params=pltpu.CompilerParams(vmem_limit_bytes=VMEM_BYTES),
            cost_estimate=pl.CostEstimate(flops=flops, bytes_accessed=nbytes, transcendentals=0),
            name=name,
        )(*args)

    return run


def iota(shape, dim):
    return lax.broadcasted_iota(jnp.int32, shape, dim)


def hot(mask):
    return jnp.where(mask, 1.0, 0.0).astype(BF)


def dot(a, b):
    return lax.dot_general(a, b, (((1,), (0,)), ((), ())), preferred_element_type=F32)


def dot_t(a, b):
    return lax.dot_general(a, b, (((1,), (1,)), ((), ())), preferred_element_type=F32)


def stage(count):
    def body(*refs):
        sources, targets, sems = refs[:count], refs[count:-1], refs[-1]
        pairs = list(zip(sources, targets[:count], strict=True))
        points = sources[0]
        pairs.append((points.at[pl.ds(points.shape[0] - G, G), :], targets[count]))
        pairs.append((points.at[pl.ds(0, G), :], targets[count + 1]))
        copies = [pltpu.make_async_copy(a, b, sems.at[n]) for n, (a, b) in enumerate(pairs)]
        for copy in copies:
            copy.start()
        for copy in copies:
            copy.wait()

    def run(*args):
        outs = [jax.ShapeDtypeStruct(a.shape, a.dtype) for a in args]
        outs += [jax.ShapeDtypeStruct((G, args[0].shape[1]), args[0].dtype)] * 2
        return pl.pallas_call(
            body,
            out_shape=outs,
            in_specs=[pl.BlockSpec(memory_space=pltpu.HBM)] * count,
            out_specs=[pl.BlockSpec(memory_space=pltpu.VMEM)] * (count + 2),
            scratch_shapes=[pltpu.SemaphoreType.DMA((count + 2,))],
            compiler_params=pltpu.CompilerParams(vmem_limit_bytes=VMEM_BYTES),
            name="stage",
        )(*(pltpu.with_memory_space_constraint(a, pltpu.HBM) for a in args))

    return run


def conv_norm_block(points, window, offsets, kinds, weights, gain, bias, between=()):
    rows, span = points.shape[0], window.shape[0]
    between = list(between)
    target = jnp.transpose(offsets + jnp.transpose(jnp.broadcast_to(iota((rows, 1), 0), (rows, offsets.shape[0]))) + G)
    code = target + jnp.transpose(kinds) * SHIFT
    conv = jnp.zeros(points.shape, F32)
    group = 4
    for first in range(0, offsets.shape[0], group):
        picks, marks = [], []
        for n in range(first, first + group):
            value = jnp.broadcast_to(code[:, n : n + 1], (rows, 128))
            place, kind = value & (SHIFT - 1), lax.shift_right_logical(value, SHIFT_BITS)
            wide = jnp.concatenate([hot(place == iota((rows, 128), 1) + lanes) for lanes in range(0, span, 128)], axis=1)
            picks.append(wide)
            marks.append(hot(kind == iota((rows, 128), 1)))
        picked = dot(jnp.concatenate(picks, axis=0), window)
        scale = dot(jnp.concatenate(marks, axis=0), weights)
        part = picked * scale
        for n in range(group):
            conv = conv + part[n * rows : (n + 1) * rows]
        if between:
            between.pop(0)()
    for step in between:
        step()
    residual = (points.astype(F32) + conv).astype(BF)
    features = residual.astype(F32)
    average = jnp.mean(features, axis=1, keepdims=True)
    centered = features - average
    variance = jnp.mean(centered * centered, axis=1, keepdims=True)
    normed = (centered * lax.rsqrt(variance + 1e-05) * gain + bias).astype(BF)
    return residual, normed


def padded_weights(conv_weight):
    kinds = conv_weight.shape[0]
    fill = jnp.zeros((128 - kinds, conv_weight.shape[1]), F32)
    return jnp.concatenate([conv_weight.astype(F32), fill], axis=0).astype(BF)


def front_inner(points, offsets, kinds, owners, conv_weight, gain, bias, residual, normed, place, fetch, dead):
    total = points.shape[0]
    weights = padded_weights(conv_weight[...])
    slots = place.shape[0] // 2
    peers = slots // HALF_SLOTS
    own = owners[...]
    match = iota((peers, total), 0) == own
    before = hot(iota((total, total), 0) < iota((total, total), 1))
    earlier = dot(hot(match), before)
    slot = jnp.sum(jnp.where(match, earlier, 0.0), axis=0, keepdims=True).astype(jnp.int32)
    low = own * HALF_SLOTS + (slot & (HALF_SLOTS - 1))
    spot = jnp.where(slot >= HALF_SLOTS, low + slots, low)
    column = jnp.transpose(jnp.broadcast_to(spot, (8, total)))[:, 0:1]

    def build_place(start):
        lane = iota((ROWS, 128), 1)
        rows = slice(start, start + ROWS)
        live = []
        for half in range(2):
            here = slice(half * slots + start, half * slots + start + ROWS)
            mask = jnp.where(iota((ROWS, total), 0) + (half * slots + start) == spot, 1.0, 0.0)
            place[here, :] = mask.astype(BF)
            live.append(jnp.sum(mask, axis=1, keepdims=True))
        dead[rows, :] = jnp.where(jnp.where(lane < 64, live[0], live[1]) > 0.5, 0.0, DEAD)

    def build_fetch(start):
        rows = slice(start, start + ROWS)
        here = jnp.broadcast_to(column[rows, :], (ROWS, 128))
        for lanes in range(0, 2 * slots, 128):
            fetch[rows, lanes : lanes + 128] = hot(here == iota((ROWS, 128), 1) + lanes)

    pieces = [functools.partial(build_place, n) for n in range(0, slots, ROWS)]
    pieces += [functools.partial(build_fetch, n) for n in range(0, total, ROWS)]
    blocks = range(1, total // ROWS - 1)
    share = len(pieces) // len(blocks)
    for block in blocks:
        rows = slice(block * ROWS, (block + 1) * ROWS)
        window = points[block * ROWS - G : (block + 1) * ROWS + G, :]
        res, nor = conv_norm_block(
            points[rows, :],
            window,
            offsets[:, rows],
            kinds[:, rows],
            weights,
            gain[...],
            bias[...],
            pieces[(block - 1) * share : block * share],
        )
        out = slice((block - 1) * ROWS, block * ROWS)
        residual[out, :] = res
        normed[out, :] = nor


def front_edges(
    above, points, below, offsets, kinds, conv_weight, gain, bias, qkv_weight, inner, place, dead, residual, out, normed
):
    total = points.shape[0]
    weights = padded_weights(conv_weight[...])
    last = total - ROWS
    for start, window in (
        (0, jnp.concatenate([above[...], points[0 : ROWS + G, :]], axis=0)),
        (last, jnp.concatenate([points[last - G :, :], below[...]], axis=0)),
    ):
        rows = slice(start, start + ROWS)
        res, nor = conv_norm_block(
            points[rows, :], window, offsets[:, rows], kinds[:, rows], weights, gain[...], bias[...]
        )
        residual[(0 if start == 0 else ROWS) : (ROWS if start == 0 else 2 * ROWS), :] = res
        normed[rows, :] = nor
    normed[ROWS:last, :] = inner[...]
    q, k, v = (qkv_weight[t] for t in range(3))
    none = jnp.zeros(q.shape, BF)
    left = jnp.concatenate([q, none, k, none, v, none], axis=0)
    right = jnp.concatenate([none, q, none, k, none, v], axis=0)
    placed = dot(place[...], normed[...]).astype(BF)
    slots = out.shape[0]
    packed = dot_t(
        jnp.concatenate([placed[:slots], placed[slots:]], axis=1), jnp.concatenate([left, right], axis=1)
    )
    out[:, 0:128] = (packed[:, 0:128] + dead[...]).astype(BF)
    out[:, 128:] = packed[:, 128:].astype(BF)


def swap_halves(value):
    return jnp.concatenate([value[:, 64:], value[:, :64]], axis=1)


def attend(packed, out, keys, queries, values):
    half = packed.shape[0]
    lane = iota((half, 128), 1)
    q = packed[:, 0:128]
    k = packed[:, 128:256]
    v = packed[:, 256:384]
    qs, ks, vs = (swap_halves(x) for x in (q, k, v))
    zero = jnp.zeros((half, 128), F32)

    def dead_bias(x):
        return jnp.where(x.astype(F32) < 0.1 * DEAD, DEAD, 0.0)

    step = 128
    for part, (qq, kk, vv, flag) in enumerate(((q, k, v, qs), (qs, ks, vs, q))):
        rows = slice(part * half, (part + 1) * half)
        qf, kf, vf = (x.astype(F32) for x in (qq, kk, vv))
        keys[rows, :] = jnp.where(lane < 64, kf, jnp.where(lane == 64, dead_bias(flag), 0.0)).astype(BF)
        extra = jnp.where(lane == 64, 1.0, zero)
        values[rows, :] = jnp.where(lane < 64, vf, extra).astype(BF)
        for head in range(2):
            mine = (lane >= head * HD) & (lane < (head + 1) * HD)
            query = jnp.where(mine, qf, extra).astype(BF)
            for index in range(half // step):
                start = (index * 4 + part * 2 + head) * step
                queries[start : start + step, :] = query[index * step : (index + 1) * step, :]
    factor = math.log2(math.e) / math.sqrt(HD)
    block_lane = iota((step, 128), 1)

    def scores_of(chunk):
        return dot_t(queries[chunk * 2 * step : (chunk + 1) * 2 * step, :], keys[...])

    def attended_of(scores):
        top = jnp.max(scores, axis=1, keepdims=True)
        soft = jnp.exp2((scores - top) * factor).astype(BF)
        summed = dot(soft, values[...])
        result = summed / summed[:, 64:65]
        return jnp.where(block_lane < HD, result[:step], result[step:])

    chunks = 2 * half // step
    ahead = [scores_of(0)]
    done = []
    for chunk in range(chunks):
        if chunk + 1 < chunks:
            ahead.append(scores_of(chunk + 1))
        done.append(attended_of(ahead.pop(0)))
        if len(done) == 2:
            first, second = done
            done = []
            moved = jnp.concatenate([second[:, 64:], second[:, :64]], axis=1)
            rows = slice((chunk // 2) * step, (chunk // 2 + 1) * step)
            out[rows, :] = jnp.where(block_lane < 64, first, moved).astype(BF)


def fetch_rows(returned, fetch, out):
    half = returned.shape[0]
    value = returned[...]
    lane = iota((half, 128), 1)
    zero = jnp.zeros((half, 128), BF)
    moved = swap_halves(value)
    left = jnp.concatenate([jnp.where(lane < 64, value, zero), jnp.where(lane < 64, moved, zero)], axis=0)
    right = jnp.concatenate([jnp.where(lane < 64, zero, moved), jnp.where(lane < 64, zero, value)], axis=0)
    points = fetch.shape[0] // 2
    rows = (dot(fetch[:points, :], left) + dot(fetch[points:, :], right)).astype(BF)
    for peer in range(out.shape[0]):
        out[peer] = rows


def finish(gathered, edge_res, inner_res, proj_weight, clusters, block_out, sums, block):
    channels = gathered.shape[0]
    width = proj_weight.shape[1]
    part = width // channels
    wide = jnp.concatenate([gathered[c] for c in range(channels)], axis=1)
    proj = proj_weight[...]
    none = jnp.zeros((part, width), BF)
    low, high = [], []
    for c in range(channels):
        piece = proj[c * part : (c + 1) * part, :]
        low += [piece, none]
        high += [none, piece]
    points = block.shape[0] // 2
    last = 2 * points - ROWS
    first = dot(wide, jnp.concatenate(low, axis=0))
    second = dot(wide, jnp.concatenate(high, axis=0))
    block[0:ROWS, :] = (edge_res[0:ROWS, :].astype(F32) + first[0:ROWS]).astype(BF)
    block[ROWS:points, :] = (inner_res[0 : points - ROWS, :].astype(F32) + first[ROWS:]).astype(BF)
    block[points:last, :] = (inner_res[points - ROWS :, :].astype(F32) + second[: last - points]).astype(BF)
    block[last:, :] = (edge_res[ROWS:, :].astype(F32) + second[last - points :]).astype(BF)
    full = block[...]
    channel = lax.axis_index("ch")
    pick = hot(iota((part, width), 1) == iota((part, width), 0) + channel * part)
    block_out[...] = dot_t(pick, full).astype(BF)
    count = 2 * points // 4
    base = lax.axis_index("pts") * count - 1
    rows = sums.shape[0]
    member = jnp.where(iota((rows, 2 * points), 0) == clusters[...] - base, 1.0, 0.0)
    sums[:, :width] = dot(member.astype(BF), full)
    sums[:, width:] = jnp.broadcast_to(jnp.sum(member, axis=1, keepdims=True), (rows, 128))


def pool(sums, spill, pool_weight, out):
    count = out.shape[0]
    width = pool_weight.shape[0]
    own = sums[1 : count + 1, :]
    total = jnp.where(iota(own.shape, 0) == count - 1, own + spill[0:1, :], own)
    value = total[:, :width]
    high = value.astype(BF)
    low = (value - high.astype(F32)).astype(BF)
    weight = pool_weight[...]
    lifted = dot(high, weight) + dot(low, weight)
    mean = lifted / total[:, width:]
    out[...] = (mean * (1.0 + lax.erf(mean * math.sqrt(0.5))) * 0.5).astype(BF)


def shape(dims, kind=BF):
    return jax.ShapeDtypeStruct(dims, kind)


def shards(
    points_in,
    neighbor_offsets,
    kernel_ids,
    cluster_ids,
    owners,
    conv_weight,
    norm_gain,
    norm_bias,
    qkv_weight,
    proj_weight,
    pool_weight,
):
    total, width = points_in.shape
    nodes = lax.axis_size("pts")
    channels = lax.axis_size("ch")
    up = [(i, i + 1) for i in range(nodes - 1)]
    down = [(j, i) for i, j in up]
    offsets, kinds = jnp.transpose(neighbor_offsets), jnp.transpose(kernel_ids)
    args = (
        points_in,
        offsets,
        kinds,
        owners.reshape(1, total),
        conv_weight,
        norm_gain.reshape(1, width),
        norm_bias.reshape(1, width),
        jnp.transpose(qkv_weight, (0, 2, 1)),
        proj_weight,
        pool_weight,
        cluster_ids.reshape(1, total),
    )
    staged = stage(len(args))(*args)
    points, offsets, kinds, own, conv_weight, gain, bias, qkv_weight, proj_weight, pool_weight = staged[:10]
    clusters_here, tail, head = staged[10:]
    above = lax.ppermute(tail, "pts", up)
    below = lax.ppermute(head, "pts", down)
    slots = nodes * HALF_SLOTS
    inner_rows = total - 2 * ROWS
    inner_res, inner_normed, place, fetch, dead = call(
        front_inner,
        (
            shape((inner_rows, width)),
            shape((inner_rows, width)),
            shape((2 * slots, total)),
            shape((total, 2 * slots)),
            shape((slots, 128), F32),
        ),
        flops=10**9,
        nbytes=4 * 10**6,
        name="front_inner",
    )(points, offsets, kinds, own, conv_weight, gain, bias)
    edge_res, packed = call(
        front_edges,
        (shape((2 * ROWS, width)), shape((slots, 384))),
        scratch=(pltpu.VMEM((total, width), BF),),
        flops=10**9,
        nbytes=4 * 10**6,
        name="front_edges",
    )(
        above,
        points,
        below,
        offsets,
        kinds,
        conv_weight,
        gain,
        bias,
        qkv_weight,
        inner_normed,
        place,
        dead,
    )
    arrived = lax.all_to_all(
        packed.reshape(nodes, HALF_SLOTS, 384), "pts", split_axis=0, concat_axis=0, tiled=True
    ).reshape(slots, 384)
    attended = call(
        attend,
        shape((slots, 128)),
        scratch=(
            pltpu.VMEM((2 * slots, 128), BF),
            pltpu.VMEM((4 * slots, 128), BF),
            pltpu.VMEM((2 * slots, 128), BF),
        ),
        flops=10**9,
        nbytes=10**6,
        name="attend",
    )(arrived)
    returned = lax.all_to_all(
        attended.reshape(nodes, HALF_SLOTS, 128), "pts", split_axis=0, concat_axis=0, tiled=True
    ).reshape(slots, 128)
    rows = call(
        fetch_rows, shape((channels, total // 2, 128)), flops=10**8, nbytes=10**6, name="fetch_rows"
    )(returned, fetch)
    gathered = lax.all_to_all(rows, "ch", split_axis=0, concat_axis=0, tiled=True)
    clusters = total // 4
    block_out, sums = call(
        finish,
        (shape((width // channels, total)), shape((clusters + 8, width + 128), F32)),
        scratch=(pltpu.VMEM((total, width), BF),),
        flops=10**8,
        nbytes=10**6,
        name="finish",
    )(gathered, edge_res, inner_res, proj_weight, clusters_here)
    spill = lax.ppermute(sums[:8], "pts", down)
    pooled = call(pool, shape((clusters, pool_weight.shape[1])), flops=10**7, nbytes=10**5, name="pool")(
        sums, spill, pool_weight
    )
    return jnp.transpose(block_out), pooled


def solution(mesh):
    return jax.shard_map(
        shards,
        mesh=mesh,
        in_specs=(
            P("pts", None),
            P("pts", None),
            P("pts", None),
            P("pts"),
            P("pts"),
            P(),
            P(),
            P(),
            P(None, None, "ch"),
            P(),
            P(None, "ch"),
        ),
        out_specs=(P("pts", "ch"), P("pts", "ch")),
        check_vma=False,
    )
```

```python
import functools
import math

import jax
import jax.numpy as jnp
from jax import lax
from jax.experimental import pallas as pl
from jax.experimental.pallas import tpu as pltpu
from jax.sharding import PartitionSpec as P

HD = 32
G = 128
ROWS = 128
HALF_SLOTS = 4
DEAD = -1e30
SHIFT_BITS = 10
SHIFT = 1 << SHIFT_BITS
LEAD = 8
HALO = G + 2 * LEAD
EXTRA = 16
BF = jnp.bfloat16
F32 = jnp.float32
VMEM_BYTES = 24 * 1024 * 1024


def call(body, outs, scratch=(), flops=0, nbytes=0, name=None):
    def run(*args):
        return pl.pallas_call(
            body,
            out_shape=outs,
            in_specs=[pl.BlockSpec(memory_space=pltpu.VMEM)] * len(args),
            out_specs=jax.tree.map(lambda _: pl.BlockSpec(memory_space=pltpu.VMEM), outs),
            scratch_shapes=list(scratch),
            compiler_params=pltpu.CompilerParams(vmem_limit_bytes=VMEM_BYTES),
            cost_estimate=pl.CostEstimate(flops=flops, bytes_accessed=nbytes, transcendentals=0),
            name=name,
        )(*args)

    return run


def iota(shape, dim):
    return lax.broadcasted_iota(jnp.int32, shape, dim)


def hot(mask):
    return jnp.where(mask, 1.0, 0.0).astype(BF)


def dot(a, b):
    return lax.dot_general(a, b, (((1,), (0,)), ((), ())), preferred_element_type=F32)


def dot_t(a, b):
    return lax.dot_general(a, b, (((1,), (1,)), ((), ())), preferred_element_type=F32)


def lead_facts(offsets, kinds, owners, clusters, first_cluster):
    own = owners[:, :128]
    lane = iota(own.shape, 1)
    slot = jnp.zeros(own.shape, F32)
    for back in (1, 2):
        same = (own == jnp.concatenate([own[:, 128 - back :], own[:, : 128 - back]], axis=1)) & (lane >= back)
        slot = slot + jnp.where(same, 1.0, 0.0)
    lead = jnp.where(clusters[:, :128] < first_cluster, 1.0, 0.0)
    lines = [
        offsets[:, :128].astype(F32),
        kinds[:, :128].astype(F32),
        jnp.broadcast_to(own.astype(F32), (8, 128)),
        jnp.broadcast_to(slot, (8, 128)),
        jnp.broadcast_to(lead, (8, 128)),
        jnp.zeros((72, 128), F32),
    ]
    return jnp.transpose(jnp.concatenate(lines, axis=0))[:LEAD, :]


def stage(count):
    def body(*refs):
        sources, targets = refs[:count], refs[count : 2 * count]
        first, second, sems = refs[2 * count :]
        copies = [
            pltpu.make_async_copy(a, b, sems.at[n]) for n, (a, b) in enumerate(zip(sources, targets, strict=True))
        ]
        for copy in copies:
            copy.start()
        for copy in copies:
            copy.wait()
        points, offsets, kinds, owners = targets[:4]
        clusters = targets[-1]
        total, width = points.shape
        index = lax.axis_index("pts")
        even = lax.rem(index, 2) == 0
        facts = lead_facts(offsets[...], kinds[...], owners[...], clusters[...], index * (total // 4))
        facts = jnp.concatenate([facts, jnp.zeros((LEAD, width - 128), F32)], axis=1)
        head = jnp.concatenate([points[0:G, :].astype(F32), points[G : G + LEAD, :].astype(F32), facts], axis=0)
        tail = jnp.concatenate([points[total - G :, :].astype(F32), jnp.zeros((2 * LEAD, width), F32)], axis=0)
        first[...] = jnp.where(even, tail, head).astype(BF)
        second[...] = jnp.where(even, head, tail).astype(BF)

    def run(*args):
        outs = [jax.ShapeDtypeStruct(a.shape, a.dtype) for a in args]
        outs += [jax.ShapeDtypeStruct((HALO, args[0].shape[1]), args[0].dtype)] * 2
        return pl.pallas_call(
            body,
            out_shape=outs,
            in_specs=[pl.BlockSpec(memory_space=pltpu.HBM)] * count,
            out_specs=[pl.BlockSpec(memory_space=pltpu.VMEM)] * (count + 2),
            scratch_shapes=[pltpu.SemaphoreType.DMA((count,))],
            compiler_params=pltpu.CompilerParams(vmem_limit_bytes=VMEM_BYTES),
            name="stage",
        )(*(pltpu.with_memory_space_constraint(a, pltpu.HBM) for a in args))

    return run


def codes(offsets, kinds):
    rows = offsets.shape[1]
    target = jnp.transpose(offsets) + iota((rows, offsets.shape[0]), 0) + G
    return target + jnp.transpose(kinds) * SHIFT


def conv_norm_block(points, window, code, weights, gain, bias, between=()):
    rows, span = points.shape[0], window.shape[0]
    between = list(between)
    conv = jnp.zeros(points.shape, F32)
    group = 4
    for first in range(0, code.shape[1], group):
        picks, marks = [], []
        for n in range(first, first + group):
            value = jnp.broadcast_to(code[:, n : n + 1], (rows, 128))
            place, kind = value & (SHIFT - 1), lax.shift_right_logical(value, SHIFT_BITS)
            wide = jnp.concatenate([hot(place == iota((rows, 128), 1) + lanes) for lanes in range(0, span, 128)], axis=1)
            picks.append(wide)
            marks.append(hot(kind == iota((rows, 128), 1)))
        picked = dot(jnp.concatenate(picks, axis=0), window)
        scale = dot(jnp.concatenate(marks, axis=0), weights)
        part = picked * scale
        for n in range(group):
            conv = conv + part[n * rows : (n + 1) * rows]
        if between:
            between.pop(0)()
    for step in between:
        step()
    residual = (points.astype(F32) + conv).astype(BF)
    features = residual.astype(F32)
    average = jnp.mean(features, axis=1, keepdims=True)
    centered = features - average
    variance = jnp.mean(centered * centered, axis=1, keepdims=True)
    normed = (centered * lax.rsqrt(variance + 1e-05) * gain + bias).astype(BF)
    return residual, normed


def padded_weights(conv_weight):
    kinds = conv_weight.shape[0]
    fill = jnp.zeros((128 - kinds, conv_weight.shape[1]), F32)
    return jnp.concatenate([conv_weight.astype(F32), fill], axis=0).astype(BF)


def front_inner(points, offsets, kinds, owners, conv_weight, gain, bias, residual, normed, place, fetch, dead):
    total = points.shape[0]
    weights = padded_weights(conv_weight[...])
    slots = place.shape[0] // 2
    peers = slots // HALF_SLOTS
    own = owners[...]
    match = iota((peers, total), 0) == own
    before = hot(iota((total, total), 0) < iota((total, total), 1))
    earlier = dot(hot(match), before)
    slot = jnp.sum(jnp.where(match, earlier, 0.0), axis=0, keepdims=True).astype(jnp.int32)
    low = own * HALF_SLOTS + (slot & (HALF_SLOTS - 1))
    spot = jnp.where(slot >= HALF_SLOTS, low + slots, low)
    column = jnp.transpose(jnp.broadcast_to(spot, (8, total)))[:, 0:1]

    def build_place(start):
        lane = iota((ROWS, 128), 1)
        rows = slice(start, start + ROWS)
        live = []
        for half in range(2):
            here = slice(half * slots + start, half * slots + start + ROWS)
            mask = jnp.where(iota((ROWS, total), 0) + (half * slots + start) == spot, 1.0, 0.0)
            place[here, :] = mask.astype(BF)
            live.append(jnp.sum(mask, axis=1, keepdims=True))
        dead[rows, :] = jnp.where(jnp.where(lane < 64, live[0], live[1]) > 0.5, 0.0, DEAD)

    def build_fetch(start):
        rows = slice(start, start + ROWS)
        here = jnp.broadcast_to(column[rows, :], (ROWS, 128))
        for lanes in range(0, 2 * slots, 128):
            fetch[rows, lanes : lanes + 128] = hot(here == iota((ROWS, 128), 1) + lanes)

    pieces = [functools.partial(build_place, n) for n in range(0, slots, ROWS)]
    pieces += [functools.partial(build_fetch, n) for n in range(0, total, ROWS)]
    blocks = range(1, total // ROWS - 1)
    share = len(pieces) // len(blocks)
    for block in blocks:
        rows = slice(block * ROWS, (block + 1) * ROWS)
        window = points[block * ROWS - G : (block + 1) * ROWS + G, :]
        res, nor = conv_norm_block(
            points[rows, :],
            window,
            codes(offsets[:, rows], kinds[:, rows]),
            weights,
            gain[...],
            bias[...],
            pieces[(block - 1) * share : block * share],
        )
        out = slice((block - 1) * ROWS, block * ROWS)
        residual[out, :] = res
        normed[out, :] = nor


def front_edges(
    got_first,
    got_second,
    points,
    offsets,
    kinds,
    conv_weight,
    gain,
    bias,
    qkv_weight,
    inner,
    place,
    dead,
    residual,
    out,
    extra_res,
    extra_fetch,
    extra_lead,
    normed,
):
    total, width = points.shape
    weights = padded_weights(conv_weight[...])
    last = total - ROWS
    even = lax.rem(lax.axis_index("pts"), 2) == 0
    one, two = got_first[...].astype(F32), got_second[...].astype(F32)
    above = jnp.where(even, two[:G], one[:G]).astype(BF)
    below = jnp.where(even, one, two)
    facts = below[G + LEAD :, :128]
    window = jnp.concatenate([above, points[0 : ROWS + G, :]], axis=0)
    res, nor = conv_norm_block(
        points[0:ROWS, :], window, codes(offsets[:, :ROWS], kinds[:, :ROWS]), weights, gain[...], bias[...]
    )
    residual[0:ROWS, :] = res
    normed[0:ROWS, :] = nor
    normed[ROWS:last, :] = inner[...]
    near = offsets.shape[0]
    facts_int = facts.astype(jnp.int32)
    extra_code = facts_int[:, :near] + iota((LEAD, near), 0) + ROWS + G + facts_int[:, near : 2 * near] * SHIFT
    blank = jnp.zeros((EXTRA - LEAD, near), jnp.int32)
    code = jnp.concatenate([codes(offsets[:, last:], kinds[:, last:]), extra_code, blank], axis=0)
    reach = below[: G + LEAD]
    fill = jnp.zeros((512 - 2 * ROWS - G - LEAD, width), F32)
    window = jnp.concatenate([points[last - G :, :], jnp.concatenate([reach, fill], axis=0).astype(BF)], axis=0)
    more = jnp.concatenate([reach[:LEAD], jnp.zeros((EXTRA - LEAD, width), F32)], axis=0).astype(BF)
    res, nor = conv_norm_block(
        jnp.concatenate([points[last:, :], more], axis=0), window, code, weights, gain[...], bias[...]
    )
    residual[ROWS:, :] = res[:ROWS]
    normed[last:, :] = nor[:ROWS]
    extra_res[...] = res[ROWS:]
    slots = out.shape[0]
    full = jnp.concatenate([facts, jnp.zeros((EXTRA - LEAD, 128), F32)], axis=0)
    owner, slot, lead = (full[:, 2 * near + 8 * n : 2 * near + 8 * n + 1] for n in range(3))
    spot = (owner * HALF_SLOTS + slot).astype(jnp.int32)
    extra_fetch[...] = hot(spot == iota((EXTRA, slots), 1))
    extra_lead[...] = jnp.broadcast_to(lead, (EXTRA, 128))
    q, k, v = (qkv_weight[t] for t in range(3))
    none = jnp.zeros(q.shape, BF)
    left = jnp.concatenate([q, none, k, none, v, none], axis=0)
    right = jnp.concatenate([none, q, none, k, none, v], axis=0)
    placed = dot(place[...], normed[...]).astype(BF)
    packed = dot_t(
        jnp.concatenate([placed[:slots], placed[slots:]], axis=1), jnp.concatenate([left, right], axis=1)
    )
    out[:, 0:128] = (packed[:, 0:128] + dead[...]).astype(BF)
    out[:, 128:] = packed[:, 128:].astype(BF)


def swap_halves(value):
    return jnp.concatenate([value[:, 64:], value[:, :64]], axis=1)


def attend(packed, out, keys, queries, values, kept):
    half = packed.shape[0]
    lane = iota((half, 128), 1)
    q = packed[:, 0:128]
    k = packed[:, 128:256]
    v = packed[:, 256:384]
    qs, ks, vs = (swap_halves(x) for x in (q, k, v))
    zero = jnp.zeros((half, 128), F32)

    def dead_bias(x):
        return jnp.where(x.astype(F32) < 0.1 * DEAD, DEAD, 0.0)

    step = 128
    for part, (qq, kk, vv, flag) in enumerate(((q, k, v, qs), (qs, ks, vs, q))):
        rows = slice(part * half, (part + 1) * half)
        qf, kf, vf = (x.astype(F32) for x in (qq, kk, vv))
        keys[rows, :] = jnp.where(lane < 64, kf, jnp.where(lane == 64, dead_bias(flag), 0.0)).astype(BF)
        extra = jnp.where(lane == 64, 1.0, zero)
        values[rows, :] = jnp.where(lane < 64, vf, extra).astype(BF)
        for head in range(2):
            mine = (lane >= head * HD) & (lane < (head + 1) * HD)
            query = jnp.where(mine, qf, extra).astype(BF)
            for index in range(half // step):
                start = (index * 4 + part * 2 + head) * step
                queries[start : start + step, :] = query[index * step : (index + 1) * step, :]
    factor = math.log2(math.e) / math.sqrt(HD)
    block_lane = iota((step, 128), 1)

    def scores_of(chunk):
        return dot_t(queries[chunk * 2 * step : (chunk + 1) * 2 * step, :], keys[...])

    def attended_of(scores):
        top = jnp.max(scores, axis=1, keepdims=True)
        soft = jnp.exp2((scores - top) * factor).astype(BF)
        summed = dot(soft, values[...])
        result = summed / summed[:, 64:65]
        return jnp.where(block_lane < HD, result[:step], result[step:])

    chunks = 2 * half // step
    ahead = [scores_of(0)]
    done = []
    for chunk in range(chunks):
        if chunk + 1 < chunks:
            ahead.append(scores_of(chunk + 1))
        done.append(attended_of(ahead.pop(0)))
        if len(done) == 2:
            first, second = done
            done = []
            moved = jnp.concatenate([second[:, 64:], second[:, :64]], axis=1)
            rows = slice((chunk // 2) * step, (chunk // 2 + 1) * step)
            both = jnp.where(block_lane < 64, first, moved)
            out[rows, :128] = both.astype(BF)
            kept[rows, :] = both
    kept[half:, :] = jnp.zeros((8, 128), F32)
    out[:, 128:] = kept[HALF_SLOTS : half + HALF_SLOTS, :].astype(BF)


def fetch_rows(returned, fetch, extra_fetch, out):
    half = returned.shape[0]
    value = returned[:, :128]
    lane = iota((half, 128), 1)
    zero = jnp.zeros((half, 128), BF)
    moved = swap_halves(value)
    left = jnp.concatenate([jnp.where(lane < 64, value, zero), jnp.where(lane < 64, moved, zero)], axis=0)
    right = jnp.concatenate([jnp.where(lane < 64, zero, moved), jnp.where(lane < 64, zero, value)], axis=0)
    points = fetch.shape[0] // 2
    rows = (dot(fetch[:points, :], left) + dot(fetch[points:, :], right)).astype(BF)
    extra = dot(extra_fetch[...], returned[:, 128:]).astype(BF)
    for peer in range(out.shape[0]):
        out[peer, :points, :] = rows
        out[peer, points:, :] = extra


def finish(
    gathered,
    edge_res,
    inner_res,
    extra_res,
    extra_lead,
    proj_weight,
    pool_weight,
    clusters,
    block_out,
    pooled,
    block,
):
    channels = gathered.shape[0]
    width = proj_weight.shape[1]
    part = width // channels
    wide = jnp.concatenate([gathered[c] for c in range(channels)], axis=1)
    proj = proj_weight[...]
    none = jnp.zeros((part, width), BF)
    low, high = [], []
    for c in range(channels):
        piece = proj[c * part : (c + 1) * part, :]
        low += [piece, none]
        high += [none, piece]
    points = block.shape[0] // 2
    last = 2 * points - ROWS
    first = dot(wide, jnp.concatenate(low, axis=0))
    second = dot(wide[:points], jnp.concatenate(high, axis=0))
    block[0:ROWS, :] = (edge_res[0:ROWS, :].astype(F32) + first[0:ROWS]).astype(BF)
    block[ROWS:points, :] = (inner_res[0 : points - ROWS, :].astype(F32) + first[ROWS:points]).astype(BF)
    block[points:last, :] = (inner_res[points - ROWS :, :].astype(F32) + second[: last - points]).astype(BF)
    block[last:, :] = (edge_res[ROWS:, :].astype(F32) + second[last - points :]).astype(BF)
    extra = (extra_res[...].astype(F32) + first[points:]).astype(BF).astype(F32)
    lead = extra_lead[...]
    spill = jnp.sum(jnp.where(lead[:, 0:1] > 0.5, extra, 0.0), axis=0, keepdims=True)
    spill_count = jnp.sum(lead, axis=0, keepdims=True)
    full = block[...]
    channel = lax.axis_index("ch")
    pick = hot(iota((part, width), 1) == iota((part, width), 0) + channel * part)
    block_out[...] = dot_t(pick, full).astype(BF)
    count = pooled.shape[0]
    base = lax.axis_index("pts") * count
    member = jnp.where(iota((count, 2 * points), 0) == clusters[...] - base, 1.0, 0.0)
    final = iota((count, 1), 0) == count - 1
    value = dot(member.astype(BF), full) + jnp.where(final, spill, 0.0)
    number = jnp.sum(member, axis=1, keepdims=True) + jnp.where(final, spill_count, 0.0)
    upper = value.astype(BF)
    lower = (value - upper.astype(F32)).astype(BF)
    weight = pool_weight[...]
    mean = (dot(upper, weight) + dot(lower, weight)) / number
    pooled[...] = (mean * (1.0 + lax.erf(mean * math.sqrt(0.5))) * 0.5).astype(BF)


def shape(dims, kind=BF):
    return jax.ShapeDtypeStruct(dims, kind)


def shards(
    points_in,
    neighbor_offsets,
    kernel_ids,
    cluster_ids,
    owners,
    conv_weight,
    norm_gain,
    norm_bias,
    qkv_weight,
    proj_weight,
    pool_weight,
):
    total, width = points_in.shape
    nodes = lax.axis_size("pts")
    channels = lax.axis_size("ch")
    inside = [(i, i ^ 1) for i in range(nodes)]
    across = [(i, ((i + 1) ^ 1) - 1) for i in range(1, nodes - 1)]
    offsets, kinds = jnp.transpose(neighbor_offsets), jnp.transpose(kernel_ids)
    args = (
        points_in,
        offsets,
        kinds,
        owners.reshape(1, total),
        conv_weight,
        norm_gain.reshape(1, width),
        norm_bias.reshape(1, width),
        jnp.transpose(qkv_weight, (0, 2, 1)),
        proj_weight,
        pool_weight,
        cluster_ids.reshape(1, total),
    )
    staged = stage(len(args))(*args)
    points, offsets, kinds, own, conv_weight, gain, bias, qkv_weight, proj_weight, pool_weight = staged[:10]
    clusters_here, first, second = staged[10:]
    got_first = lax.ppermute(first, "pts", inside)
    got_second = lax.ppermute(second, "pts", across)
    slots = nodes * HALF_SLOTS
    inner_rows = total - 2 * ROWS
    inner_res, inner_normed, place, fetch, dead = call(
        front_inner,
        (
            shape((inner_rows, width)),
            shape((inner_rows, width)),
            shape((2 * slots, total)),
            shape((total, 2 * slots)),
            shape((slots, 128), F32),
        ),
        flops=10**9,
        nbytes=4 * 10**6,
        name="front_inner",
    )(points, offsets, kinds, own, conv_weight, gain, bias)
    edge_res, packed, extra_res, extra_fetch, extra_lead = call(
        front_edges,
        (
            shape((2 * ROWS, width)),
            shape((slots, 384)),
            shape((EXTRA, width)),
            shape((EXTRA, slots)),
            shape((EXTRA, 128), F32),
        ),
        scratch=(pltpu.VMEM((total, width), BF),),
        flops=10**9,
        nbytes=4 * 10**6,
        name="front_edges",
    )(
        got_first,
        got_second,
        points,
        offsets,
        kinds,
        conv_weight,
        gain,
        bias,
        qkv_weight,
        inner_normed,
        place,
        dead,
    )
    arrived = lax.all_to_all(
        packed.reshape(nodes, HALF_SLOTS, 384), "pts", split_axis=0, concat_axis=0, tiled=True
    ).reshape(slots, 384)
    attended = call(
        attend,
        shape((slots, 256)),
        scratch=(
            pltpu.VMEM((2 * slots, 128), BF),
            pltpu.VMEM((4 * slots, 128), BF),
            pltpu.VMEM((2 * slots, 128), BF),
            pltpu.VMEM((slots + 8, 128), F32),
        ),
        flops=10**9,
        nbytes=10**6,
        name="attend",
    )(arrived)
    returned = lax.all_to_all(
        attended.reshape(nodes, HALF_SLOTS, 256), "pts", split_axis=0, concat_axis=0, tiled=True
    ).reshape(slots, 256)
    rows = call(
        fetch_rows, shape((channels, total // 2 + EXTRA, 128)), flops=10**8, nbytes=10**6, name="fetch_rows"
    )(returned, fetch, extra_fetch)
    gathered = lax.all_to_all(rows, "ch", split_axis=0, concat_axis=0, tiled=True)
    block_out, pooled = call(
        finish,
        (shape((width // channels, total)), shape((total // 4, pool_weight.shape[1]))),
        scratch=(pltpu.VMEM((total, width), BF),),
        flops=10**8,
        nbytes=10**6,
        name="finish",
    )(gathered, edge_res, inner_res, extra_res, extra_lead, proj_weight, pool_weight, clusters_here)
    return jnp.transpose(block_out), pooled


def solution(mesh):
    return jax.shard_map(
        shards,
        mesh=mesh,
        in_specs=(
            P("pts", None),
            P("pts", None),
            P("pts", None),
            P("pts"),
            P("pts"),
            P(),
            P(),
            P(),
            P(None, None, "ch"),
            P(),
            P(None, "ch"),
        ),
        out_specs=(P("pts", "ch"), P("pts", "ch")),
        check_vma=False,
    )
```

```python
import functools
import math

import jax
import jax.numpy as jnp
from jax import lax
from jax.experimental import pallas as pl
from jax.experimental.pallas import tpu as pltpu
from jax.sharding import PartitionSpec as P

HD = 32
G = 128
ROWS = 128
HALF_SLOTS = 4
DEAD = -1e30
SHIFT_BITS = 10
SHIFT = 1 << SHIFT_BITS
LEAD = 8
HALO = G + 2 * LEAD
EXTRA = 16
GROUP = 4
BF = jnp.bfloat16
F32 = jnp.float32
VMEM_BYTES = 24 * 1024 * 1024


def call(body, outs, scratch=(), flops=0, nbytes=0, name=None):
    def run(*args):
        return pl.pallas_call(
            body,
            out_shape=outs,
            in_specs=[pl.BlockSpec(memory_space=pltpu.VMEM)] * len(args),
            out_specs=jax.tree.map(lambda _: pl.BlockSpec(memory_space=pltpu.VMEM), outs),
            scratch_shapes=list(scratch),
            compiler_params=pltpu.CompilerParams(vmem_limit_bytes=VMEM_BYTES),
            cost_estimate=pl.CostEstimate(flops=flops, bytes_accessed=nbytes, transcendentals=0),
            name=name,
        )(*args)

    return run


def iota(shape, dim):
    return lax.broadcasted_iota(jnp.int32, shape, dim)


def hot(mask):
    return jnp.where(mask, 1.0, 0.0).astype(BF)


def dot(a, b):
    return lax.dot_general(a, b, (((1,), (0,)), ((), ())), preferred_element_type=F32)


def dot_t(a, b):
    return lax.dot_general(a, b, (((1,), (1,)), ((), ())), preferred_element_type=F32)


def lead_facts(offsets, kinds, owners, clusters, first_cluster):
    own = owners[:, :128]
    lane = iota(own.shape, 1)
    slot = jnp.zeros(own.shape, F32)
    for back in (1, 2):
        same = (own == jnp.concatenate([own[:, 128 - back :], own[:, : 128 - back]], axis=1)) & (lane >= back)
        slot = slot + jnp.where(same, 1.0, 0.0)
    lead = jnp.where(clusters[:, :128] < first_cluster, 1.0, 0.0)
    lines = [
        offsets[:, :128].astype(F32),
        kinds[:, :128].astype(F32),
        jnp.broadcast_to(own.astype(F32), (8, 128)),
        jnp.broadcast_to(slot, (8, 128)),
        jnp.broadcast_to(lead, (8, 128)),
        jnp.zeros((72, 128), F32),
    ]
    return jnp.transpose(jnp.concatenate(lines, axis=0))[:LEAD, :]


def stage(count):
    def body(*refs):
        sources, targets = refs[:count], refs[count : 2 * count]
        first, second, sems = refs[2 * count :]
        copies = [
            pltpu.make_async_copy(a, b, sems.at[n]) for n, (a, b) in enumerate(zip(sources, targets, strict=True))
        ]
        for copy in copies:
            copy.start()
        for copy in copies:
            copy.wait()
        points, offsets, kinds, owners = targets[:4]
        clusters = targets[-1]
        total, width = points.shape
        index = lax.axis_index("pts")
        even = lax.rem(index, 2) == 0
        facts = lead_facts(offsets[...], kinds[...], owners[...], clusters[...], index * (total // 4))
        facts = jnp.concatenate([facts, jnp.zeros((LEAD, width - 128), F32)], axis=1)
        head = jnp.concatenate([points[0:G, :].astype(F32), points[G : G + LEAD, :].astype(F32), facts], axis=0)
        tail = jnp.concatenate([points[total - G :, :].astype(F32), jnp.zeros((2 * LEAD, width), F32)], axis=0)
        first[...] = jnp.where(even, tail, head).astype(BF)
        second[...] = jnp.where(even, head, tail).astype(BF)

    def run(*args):
        outs = [jax.ShapeDtypeStruct(a.shape, a.dtype) for a in args]
        outs += [jax.ShapeDtypeStruct((HALO, args[0].shape[1]), args[0].dtype)] * 2
        return pl.pallas_call(
            body,
            out_shape=outs,
            in_specs=[pl.BlockSpec(memory_space=pltpu.HBM)] * count,
            out_specs=[pl.BlockSpec(memory_space=pltpu.VMEM)] * (count + 2),
            scratch_shapes=[pltpu.SemaphoreType.DMA((count,))],
            compiler_params=pltpu.CompilerParams(vmem_limit_bytes=VMEM_BYTES),
            name="stage",
        )(*(pltpu.with_memory_space_constraint(a, pltpu.HBM) for a in args))

    return run


def codes(offsets, kinds=None):
    rows = offsets.shape[1]
    target = jnp.transpose(offsets) + iota((rows, offsets.shape[0]), 0) + G
    return target if kinds is None else target + jnp.transpose(kinds) * SHIFT


def windowed_sum(code, shift, window, scale_of, between=()):
    rows, span = code.shape[0], window.shape[0]
    between = list(between)
    conv = jnp.zeros((rows, window.shape[1]), F32)
    for first in range(0, code.shape[1], GROUP):
        picks, kinds = [], []
        for n in range(first, first + GROUP):
            place = jnp.broadcast_to(code[:, n : n + 1], (rows, 128))
            if scale_of.marked:
                kinds.append(lax.shift_right_logical(place, SHIFT_BITS))
                place = place & (SHIFT - 1)
            lane = iota((rows, 128), 1) + shift
            picks.append(jnp.concatenate([hot(place == lane + lanes) for lanes in range(0, span, 128)], axis=1))
        picked = dot(jnp.concatenate(picks, axis=0), window)
        part = picked * scale_of(first // GROUP, kinds)
        for n in range(GROUP):
            conv = conv + part[n * rows : (n + 1) * rows]
        if between:
            between.pop(0)()
    for step in between:
        step()
    return conv


def scale_by(weights, keep=None):
    def scale_of(group, kinds):
        marks = [hot(kind == iota(kind.shape, 1)) for kind in kinds]
        scale = dot(jnp.concatenate(marks, axis=0), weights)
        if keep is not None:
            keep[group] = scale.astype(BF)
        return scale

    scale_of.marked = True
    return scale_of


def kept_scale(kept):
    def scale_of(group, kinds):
        return kept[group].astype(F32)

    scale_of.marked = False
    return scale_of


def normalize(points, conv, gain, bias):
    residual = (points.astype(F32) + conv).astype(BF)
    features = residual.astype(F32)
    average = jnp.mean(features, axis=1, keepdims=True)
    centered = features - average
    variance = jnp.mean(centered * centered, axis=1, keepdims=True)
    normed = (centered * lax.rsqrt(variance + 1e-05) * gain + bias).astype(BF)
    return residual, normed


def padded_weights(conv_weight):
    kinds = conv_weight.shape[0]
    fill = jnp.zeros((128 - kinds, conv_weight.shape[1]), F32)
    return jnp.concatenate([conv_weight.astype(F32), fill], axis=0).astype(BF)


def front_inner(
    points,
    offsets,
    kinds,
    owners,
    conv_weight,
    gain,
    bias,
    residual,
    normed,
    place,
    fetch,
    dead,
    partial,
    top_scale,
    end_scale,
):
    total = points.shape[0]
    weights = padded_weights(conv_weight[...])
    slots = place.shape[0] // 2
    peers = slots // HALF_SLOTS
    own = owners[...]
    match = iota((peers, total), 0) == own
    before = hot(iota((total, total), 0) < iota((total, total), 1))
    earlier = dot(hot(match), before)
    slot = jnp.sum(jnp.where(match, earlier, 0.0), axis=0, keepdims=True).astype(jnp.int32)
    low = own * HALF_SLOTS + (slot & (HALF_SLOTS - 1))
    spot = jnp.where(slot >= HALF_SLOTS, low + slots, low)
    quarter = (slot >> 2) * 2 + (slot & 1)
    back = quarter * (2 * peers) + own * 2 + ((slot & (HALF_SLOTS - 1)) >> 1)
    column = jnp.transpose(jnp.broadcast_to(back, (8, total)))[:, 0:1]

    def build_place(start):
        lane = iota((ROWS, 128), 1)
        rows = slice(start, start + ROWS)
        live = []
        for half in range(2):
            here = slice(half * slots + start, half * slots + start + ROWS)
            mask = jnp.where(iota((ROWS, total), 0) + (half * slots + start) == spot, 1.0, 0.0)
            place[here, :] = mask.astype(BF)
            live.append(jnp.sum(mask, axis=1, keepdims=True))
        dead[rows, :] = jnp.where(jnp.where(lane < 64, live[0], live[1]) > 0.5, 0.0, DEAD)

    def build_fetch(start):
        rows = slice(start, start + ROWS)
        here = jnp.broadcast_to(column[rows, :], (ROWS, 128))
        for lanes in range(0, 2 * slots, 128):
            fetch[rows, lanes : lanes + 128] = hot(here == iota((ROWS, 128), 1) + lanes)

    pieces = [functools.partial(build_place, n) for n in range(0, slots, ROWS)]
    pieces += [functools.partial(build_fetch, n) for n in range(0, total, ROWS)]
    blocks = range(1, total // ROWS - 1)
    share = len(pieces) // (len(blocks) + 2)
    for block in blocks:
        rows = slice(block * ROWS, (block + 1) * ROWS)
        window = points[block * ROWS - G : (block + 1) * ROWS + G, :]
        conv = windowed_sum(
            codes(offsets[:, rows], kinds[:, rows]),
            0,
            window,
            scale_by(weights),
            pieces[(block - 1) * share : block * share],
        )
        res, nor = normalize(points[rows, :], conv, gain[...], bias[...])
        out = slice((block - 1) * ROWS, block * ROWS)
        residual[out, :] = res
        normed[out, :] = nor
    last = total - ROWS
    partial[0:ROWS, :] = windowed_sum(
        codes(offsets[:, :ROWS], kinds[:, :ROWS]),
        G,
        points[0 : ROWS + G, :],
        scale_by(weights, top_scale),
        pieces[2 * share : 3 * share],
    )
    partial[ROWS:, :] = windowed_sum(
        codes(offsets[:, last:], kinds[:, last:]),
        0,
        points[last - G :, :],
        scale_by(weights, end_scale),
        pieces[3 * share :],
    )


def front_edges(
    got_first,
    got_second,
    points,
    offsets,
    kinds,
    conv_weight,
    gain,
    bias,
    qkv_weight,
    inner,
    place,
    dead,
    partial,
    top_scale,
    end_scale,
    residual,
    out,
    extra_res,
    extra_fetch,
    extra_lead,
    normed,
):
    total, width = points.shape
    weights = padded_weights(conv_weight[...])
    last = total - ROWS
    even = lax.rem(lax.axis_index("pts"), 2) == 0
    one, two = got_first[...].astype(F32), got_second[...].astype(F32)
    above = jnp.where(even, two[:G], one[:G]).astype(BF)
    below = jnp.where(even, one, two)
    facts = below[G + LEAD :, :128]
    conv = partial[0:ROWS, :] + windowed_sum(
        codes(offsets[:, :ROWS]), 0, above, kept_scale(top_scale)
    )
    res, nor = normalize(points[0:ROWS, :], conv, gain[...], bias[...])
    residual[0:ROWS, :] = res
    normed[0:ROWS, :] = nor
    normed[ROWS:last, :] = inner[...]
    conv = partial[ROWS:, :] + windowed_sum(
        codes(offsets[:, last:]),
        ROWS + G,
        below[:G].astype(BF),
        kept_scale(end_scale),
    )
    res, nor = normalize(points[last:, :], conv, gain[...], bias[...])
    residual[ROWS:, :] = res
    normed[last:, :] = nor
    near = offsets.shape[0]
    facts_int = facts.astype(jnp.int32)
    extra_code = facts_int[:, :near] + iota((LEAD, near), 0) + G + facts_int[:, near : 2 * near] * SHIFT
    blank = jnp.zeros((EXTRA - LEAD, near), jnp.int32)
    reach = below[: G + LEAD]
    fill = jnp.zeros((256 - G - LEAD, width), F32)
    window = jnp.concatenate([points[last:, :], jnp.concatenate([reach, fill], axis=0).astype(BF)], axis=0)
    more = jnp.concatenate([reach[:LEAD], jnp.zeros((EXTRA - LEAD, width), F32)], axis=0)
    conv = windowed_sum(jnp.concatenate([extra_code, blank], axis=0), 0, window, scale_by(weights))
    extra_res[...] = (more + conv).astype(BF)
    slots = out.shape[0]
    full = jnp.concatenate([facts, jnp.zeros((EXTRA - LEAD, 128), F32)], axis=0)
    owner, slot, lead = (full[:, 2 * near + 8 * n : 2 * near + 8 * n + 1] for n in range(3))
    index = slot.astype(jnp.int32)
    spot = (index & 1) * (slots // 2) + owner.astype(jnp.int32) * 2 + (index >> 1)
    extra_fetch[...] = hot(spot == iota((EXTRA, slots), 1))
    extra_lead[...] = jnp.broadcast_to(lead, (EXTRA, 128))
    q, k, v = (qkv_weight[t] for t in range(3))
    none = jnp.zeros(q.shape, BF)
    left = jnp.concatenate([q, none, k, none, v, none], axis=0)
    right = jnp.concatenate([none, q, none, k, none, v], axis=0)
    placed = dot(place[...], normed[...]).astype(BF)
    packed = dot_t(
        jnp.concatenate([placed[:slots], placed[slots:]], axis=1), jnp.concatenate([left, right], axis=1)
    )
    out[:, 0:128] = (packed[:, 0:128] + dead[...]).astype(BF)
    out[:, 128:] = packed[:, 128:].astype(BF)


def swap_halves(value):
    return jnp.concatenate([value[:, 64:], value[:, :64]], axis=1)


def attend(packed, out, keys, queries, values, kept):
    half = packed.shape[0]
    lane = iota((half, 128), 1)
    q = packed[:, 0:128]
    k = packed[:, 128:256]
    v = packed[:, 256:384]
    qs, ks, vs = (swap_halves(x) for x in (q, k, v))
    zero = jnp.zeros((half, 128), F32)

    def dead_bias(x):
        return jnp.where(x.astype(F32) < 0.1 * DEAD, DEAD, 0.0)

    step = 128
    for part, (qq, kk, vv, flag) in enumerate(((q, k, v, qs), (qs, ks, vs, q))):
        rows = slice(part * half, (part + 1) * half)
        qf, kf, vf = (x.astype(F32) for x in (qq, kk, vv))
        keys[rows, :] = jnp.where(lane < 64, kf, jnp.where(lane == 64, dead_bias(flag), 0.0)).astype(BF)
        extra = jnp.where(lane == 64, 1.0, zero)
        values[rows, :] = jnp.where(lane < 64, vf, extra).astype(BF)
        for head in range(2):
            mine = (lane >= head * HD) & (lane < (head + 1) * HD)
            query = jnp.where(mine, qf, extra).astype(BF)
            for index in range(half // step):
                start = (index * 4 + part * 2 + head) * step
                queries[start : start + step, :] = query[index * step : (index + 1) * step, :]
    factor = math.log2(math.e) / math.sqrt(HD)
    block_lane = iota((step, 128), 1)

    def scores_of(chunk):
        return dot_t(queries[chunk * 2 * step : (chunk + 1) * 2 * step, :], keys[...])

    def attended_of(scores):
        top = jnp.max(scores, axis=1, keepdims=True)
        soft = jnp.exp2((scores - top) * factor).astype(BF)
        summed = dot(soft, values[...])
        result = summed / summed[:, 64:65]
        return jnp.where(block_lane < HD, result[:step], result[step:])

    chunks = 2 * half // step
    ahead = [scores_of(0)]
    done = []
    for chunk in range(chunks):
        if chunk + 1 < chunks:
            ahead.append(scores_of(chunk + 1))
        done.append(attended_of(ahead.pop(0)))
        if len(done) == 2:
            first, second = done
            done = []
            moved = jnp.concatenate([second[:, 64:], second[:, :64]], axis=1)
            rows = slice((chunk // 2) * step, (chunk // 2 + 1) * step)
            both = jnp.where(block_lane < 64, first, moved)
            kept[rows, :] = both
    kept[half:, :] = jnp.zeros((8, 128), F32)
    pairs = half // 2
    lane = iota((pairs, 128), 1)
    out[:, :128] = kept[pl.ds(0, pairs, stride=2), :].astype(BF)
    out[:, 128:256] = kept[pl.ds(1, pairs, stride=2), :].astype(BF)
    near, far = kept[pl.ds(HALF_SLOTS, pairs, stride=2), :], kept[pl.ds(HALF_SLOTS + 1, pairs, stride=2), :]
    out[:, 256:] = jnp.where(lane < 64, near, swap_halves(far)).astype(BF)


def fetch_rows(returned, fetch, extra_fetch, out):
    tiles = [returned[:, n * 128 : (n + 1) * 128] for n in range(3)]
    lane = iota(tiles[0].shape, 1)
    zero = jnp.zeros(tiles[0].shape, BF)
    moved = [swap_halves(tile) for tile in tiles]
    order = [tiles[0], tiles[1], moved[0], moved[1]]
    other = [moved[0], moved[1], tiles[0], tiles[1]]
    left = jnp.concatenate([jnp.where(lane < 64, tile, zero) for tile in order], axis=0)
    right = jnp.concatenate([jnp.where(lane < 64, zero, tile) for tile in other], axis=0)
    points = fetch.shape[0] // 2
    rows = (dot(fetch[:points, :], left) + dot(fetch[points:, :], right)).astype(BF)
    extra = dot(extra_fetch[...], jnp.concatenate([tiles[2], moved[2]], axis=0)).astype(BF)
    for peer in range(out.shape[0]):
        out[peer, :points, :] = rows
        out[peer, points:, :] = extra


def finish(
    gathered,
    edge_res,
    inner_res,
    extra_res,
    extra_lead,
    proj_weight,
    pool_weight,
    clusters,
    block_out,
    pooled,
    block,
):
    channels = gathered.shape[0]
    width = proj_weight.shape[1]
    part = width // channels
    wide = jnp.concatenate([gathered[c] for c in range(channels)], axis=1)
    proj = proj_weight[...]
    none = jnp.zeros((part, width), BF)
    low, high = [], []
    for c in range(channels):
        piece = proj[c * part : (c + 1) * part, :]
        low += [piece, none]
        high += [none, piece]
    points = block.shape[0] // 2
    last = 2 * points - ROWS
    first = dot(wide, jnp.concatenate(low, axis=0))
    second = dot(wide[:points], jnp.concatenate(high, axis=0))
    block[0:ROWS, :] = (edge_res[0:ROWS, :].astype(F32) + first[0:ROWS]).astype(BF)
    block[ROWS:points, :] = (inner_res[0 : points - ROWS, :].astype(F32) + first[ROWS:points]).astype(BF)
    block[points:last, :] = (inner_res[points - ROWS :, :].astype(F32) + second[: last - points]).astype(BF)
    block[last:, :] = (edge_res[ROWS:, :].astype(F32) + second[last - points :]).astype(BF)
    extra = (extra_res[...].astype(F32) + first[points:]).astype(BF).astype(F32)
    lead = extra_lead[...]
    spill = jnp.sum(jnp.where(lead[:, 0:1] > 0.5, extra, 0.0), axis=0, keepdims=True)
    spill_count = jnp.sum(lead, axis=0, keepdims=True)
    full = block[...]
    channel = lax.axis_index("ch")
    pick = hot(iota((part, width), 1) == iota((part, width), 0) + channel * part)
    block_out[...] = dot_t(pick, full).astype(BF)
    count = pooled.shape[0]
    base = lax.axis_index("pts") * count
    member = jnp.where(iota((count, 2 * points), 0) == clusters[...] - base, 1.0, 0.0)
    final = iota((count, 1), 0) == count - 1
    value = dot(member.astype(BF), full) + jnp.where(final, spill, 0.0)
    number = jnp.sum(member, axis=1, keepdims=True) + jnp.where(final, spill_count, 0.0)
    upper = value.astype(BF)
    lower = (value - upper.astype(F32)).astype(BF)
    weight = pool_weight[...]
    mean = (dot(upper, weight) + dot(lower, weight)) / number
    pooled[...] = (mean * (1.0 + lax.erf(mean * math.sqrt(0.5))) * 0.5).astype(BF)


def shape(dims, kind=BF):
    return jax.ShapeDtypeStruct(dims, kind)


def shards(
    points_in,
    neighbor_offsets,
    kernel_ids,
    cluster_ids,
    owners,
    conv_weight,
    norm_gain,
    norm_bias,
    qkv_weight,
    proj_weight,
    pool_weight,
):
    total, width = points_in.shape
    entries = neighbor_offsets.shape[1]
    nodes = lax.axis_size("pts")
    channels = lax.axis_size("ch")
    inside = [(i, i ^ 1) for i in range(nodes)]
    across = [(i, ((i + 1) ^ 1) - 1) for i in range(1, nodes - 1)]
    offsets, kinds = jnp.transpose(neighbor_offsets), jnp.transpose(kernel_ids)
    args = (
        points_in,
        offsets,
        kinds,
        owners.reshape(1, total),
        conv_weight,
        norm_gain.reshape(1, width),
        norm_bias.reshape(1, width),
        jnp.transpose(qkv_weight, (0, 2, 1)),
        proj_weight,
        pool_weight,
        cluster_ids.reshape(1, total),
    )
    staged = stage(len(args))(*args)
    points, offsets, kinds, own, conv_weight, gain, bias, qkv_weight, proj_weight, pool_weight = staged[:10]
    clusters_here, first, second = staged[10:]
    got_first = lax.ppermute(first, "pts", inside)
    got_second = lax.ppermute(second, "pts", across)
    slots = nodes * HALF_SLOTS
    inner_rows = total - 2 * ROWS
    inner_res, inner_normed, place, fetch, dead, partial, top_scale, end_scale = call(
        front_inner,
        (
            shape((inner_rows, width)),
            shape((inner_rows, width)),
            shape((2 * slots, total)),
            shape((total, 2 * slots)),
            shape((slots, 128), F32),
            shape((2 * ROWS, width), F32),
            shape((entries // GROUP, GROUP * ROWS, width)),
            shape((entries // GROUP, GROUP * ROWS, width)),
        ),
        flops=10**9,
        nbytes=4 * 10**6,
        name="front_inner",
    )(points, offsets, kinds, own, conv_weight, gain, bias)
    edge_res, packed, extra_res, extra_fetch, extra_lead = call(
        front_edges,
        (
            shape((2 * ROWS, width)),
            shape((slots, 384)),
            shape((EXTRA, width)),
            shape((EXTRA, slots)),
            shape((EXTRA, 128), F32),
        ),
        scratch=(pltpu.VMEM((total, width), BF),),
        flops=10**9,
        nbytes=4 * 10**6,
        name="front_edges",
    )(
        got_first,
        got_second,
        points,
        offsets,
        kinds,
        conv_weight,
        gain,
        bias,
        qkv_weight,
        inner_normed,
        place,
        dead,
        partial,
        top_scale,
        end_scale,
    )
    arrived = lax.all_to_all(
        packed.reshape(nodes, HALF_SLOTS, 384), "pts", split_axis=0, concat_axis=0, tiled=True
    ).reshape(slots, 384)
    attended = call(
        attend,
        shape((slots // 2, 384)),
        scratch=(
            pltpu.VMEM((2 * slots, 128), BF),
            pltpu.VMEM((4 * slots, 128), BF),
            pltpu.VMEM((2 * slots, 128), BF),
            pltpu.VMEM((slots + 8, 128), F32),
        ),
        flops=10**9,
        nbytes=10**6,
        name="attend",
    )(arrived)
    returned = lax.all_to_all(
        attended.reshape(nodes, 2, 384), "pts", split_axis=0, concat_axis=0, tiled=True
    ).reshape(slots // 2, 384)
    rows = call(
        fetch_rows, shape((channels, total // 2 + EXTRA, 128)), flops=10**8, nbytes=10**6, name="fetch_rows"
    )(returned, fetch, extra_fetch)
    gathered = lax.all_to_all(rows, "ch", split_axis=0, concat_axis=0, tiled=True)
    block_out, pooled = call(
        finish,
        (shape((width // channels, total)), shape((total // 4, pool_weight.shape[1]))),
        scratch=(pltpu.VMEM((total, width), BF),),
        flops=10**8,
        nbytes=10**6,
        name="finish",
    )(gathered, edge_res, inner_res, extra_res, extra_lead, proj_weight, pool_weight, clusters_here)
    return jnp.transpose(block_out), pooled


def solution(mesh):
    return jax.shard_map(
        shards,
        mesh=mesh,
        in_specs=(
            P("pts", None),
            P("pts", None),
            P("pts", None),
            P("pts"),
            P("pts"),
            P(),
            P(),
            P(),
            P(None, None, "ch"),
            P(),
            P(None, "ch"),
        ),
        out_specs=(P("pts", "ch"), P("pts", "ch")),
        check_vma=False,
    )
```

```python
import functools
import math

import jax
import jax.numpy as jnp
from jax import lax
from jax.experimental import pallas as pl
from jax.experimental.pallas import tpu as pltpu
from jax.sharding import PartitionSpec as P

HD = 32
G = 128
ROWS = 128
HALF_SLOTS = 4
DEAD = -1e30
LEAD = 8
HALO = G + 2 * LEAD
EXTRA = 16
GROUP = 4
BF = jnp.bfloat16
F32 = jnp.float32
VMEM_BYTES = 24 * 1024 * 1024


def call(body, outs, scratch=(), flops=0, nbytes=0, name=None):
    def run(*args):
        return pl.pallas_call(
            body,
            out_shape=outs,
            in_specs=[pl.BlockSpec(memory_space=pltpu.VMEM)] * len(args),
            out_specs=jax.tree.map(lambda _: pl.BlockSpec(memory_space=pltpu.VMEM), outs),
            scratch_shapes=list(scratch),
            compiler_params=pltpu.CompilerParams(vmem_limit_bytes=VMEM_BYTES),
            cost_estimate=pl.CostEstimate(flops=flops, bytes_accessed=nbytes, transcendentals=0),
            name=name,
        )(*args)

    return run


def iota(shape, dim):
    return lax.broadcasted_iota(jnp.int32, shape, dim)


def hot(mask):
    return jnp.where(mask, 1.0, 0.0).astype(BF)


def dot(a, b):
    return lax.dot_general(a, b, (((1,), (0,)), ((), ())), preferred_element_type=F32)


def dot_t(a, b):
    return lax.dot_general(a, b, (((1,), (1,)), ((), ())), preferred_element_type=F32)


def lead_facts(offsets, kinds, owners, clusters, first_cluster):
    own = owners[:, :128]
    lane = iota(own.shape, 1)
    slot = jnp.zeros(own.shape, F32)
    for back in (1, 2):
        same = (own == jnp.concatenate([own[:, 128 - back :], own[:, : 128 - back]], axis=1)) & (lane >= back)
        slot = slot + jnp.where(same, 1.0, 0.0)
    lead = jnp.where(clusters[:, :128] < first_cluster, 1.0, 0.0)
    lines = [
        offsets[:, :128].astype(F32),
        kinds[:, :128].astype(F32),
        jnp.broadcast_to(own.astype(F32), (8, 128)),
        jnp.broadcast_to(slot, (8, 128)),
        jnp.broadcast_to(lead, (8, 128)),
        jnp.zeros((72, 128), F32),
    ]
    return jnp.transpose(jnp.concatenate(lines, axis=0))[:LEAD, :]


def stage(count):
    def body(*refs):
        sources, targets = refs[:count], refs[count : 2 * count]
        first, second, sems = refs[2 * count :]
        copies = [
            pltpu.make_async_copy(a, b, sems.at[n]) for n, (a, b) in enumerate(zip(sources, targets, strict=True))
        ]
        for copy in copies:
            copy.start()
        for copy in copies:
            copy.wait()
        points, offsets, kinds, owners = targets[:4]
        clusters = targets[-1]
        total, width = points.shape
        index = lax.axis_index("pts")
        even = lax.rem(index, 2) == 0
        facts = lead_facts(offsets[...], kinds[...], owners[...], clusters[...], index * (total // 4))
        facts = jnp.concatenate([facts, jnp.zeros((LEAD, width - 128), F32)], axis=1)
        head = jnp.concatenate([points[0:G, :].astype(F32), points[G : G + LEAD, :].astype(F32), facts], axis=0)
        tail = jnp.concatenate([points[total - G :, :].astype(F32), jnp.zeros((2 * LEAD, width), F32)], axis=0)
        first[...] = jnp.where(even, tail, head).astype(BF)
        second[...] = jnp.where(even, head, tail).astype(BF)

    def run(*args):
        outs = [jax.ShapeDtypeStruct(a.shape, a.dtype) for a in args]
        outs += [jax.ShapeDtypeStruct((HALO, args[0].shape[1]), args[0].dtype)] * 2
        return pl.pallas_call(
            body,
            out_shape=outs,
            in_specs=[pl.BlockSpec(memory_space=pltpu.HBM)] * count,
            out_specs=[pl.BlockSpec(memory_space=pltpu.VMEM)] * (count + 2),
            scratch_shapes=[pltpu.SemaphoreType.DMA((count,))],
            compiler_params=pltpu.CompilerParams(vmem_limit_bytes=VMEM_BYTES),
            name="stage",
        )(*(pltpu.with_memory_space_constraint(a, pltpu.HBM) for a in args))

    return run


def codes(offsets):
    return jnp.transpose(offsets.astype(F32)) + iota((offsets.shape[1], offsets.shape[0]), 0).astype(F32)


def columns(kinds):
    return jnp.transpose(kinds.astype(F32))


def marks_of(values, n, first, span):
    value = jnp.broadcast_to(values[:, n : n + 1], (values.shape[0], 128)).astype(BF)
    lane = iota(value.shape, 1).astype(F32)
    one, none = jnp.ones(value.shape, BF), jnp.zeros(value.shape, BF)
    tiles = [jnp.where(value == (lane + (first + lanes)).astype(BF), one, none) for lanes in range(0, span, 128)]
    return tiles[0] if len(tiles) == 1 else jnp.concatenate(tiles, axis=1)


def windowed_sum(code, first_row, window, scale_of, between=()):
    rows, span = code.shape[0], window.shape[0]
    between = list(between)
    conv = jnp.zeros((rows, window.shape[1]), F32)
    for first in range(0, code.shape[1], GROUP):
        picks = [marks_of(code, n, first_row - G, span) for n in range(first, first + GROUP)]
        picked = dot(jnp.concatenate(picks, axis=0), window)
        part = picked * scale_of(first // GROUP)
        for n in range(GROUP):
            conv = conv + part[n * rows : (n + 1) * rows]
        if between:
            between.pop(0)()
    for step in between:
        step()
    return conv


def scale_by(weights, kinds, keep=None):
    def scale_of(group):
        marks = [marks_of(kinds, n, 0, 128) for n in range(group * GROUP, (group + 1) * GROUP)]
        scale = dot(jnp.concatenate(marks, axis=0), weights)
        if keep is not None:
            keep[group] = scale.astype(BF)
        return scale

    return scale_of


def kept_scale(kept):
    return lambda group: kept[group].astype(F32)


def normalize(points, conv, gain, bias):
    residual = (points.astype(F32) + conv).astype(BF)
    features = residual.astype(F32)
    average = jnp.mean(features, axis=1, keepdims=True)
    centered = features - average
    variance = jnp.mean(centered * centered, axis=1, keepdims=True)
    normed = (centered * lax.rsqrt(variance + 1e-05) * gain + bias).astype(BF)
    return residual, normed


def padded_weights(conv_weight):
    kinds = conv_weight.shape[0]
    fill = jnp.zeros((128 - kinds, conv_weight.shape[1]), F32)
    return jnp.concatenate([conv_weight.astype(F32), fill], axis=0).astype(BF)


def projection(qkv_weight):
    q, k, v = (qkv_weight[t] for t in range(3))
    return jnp.concatenate([q, k, v, jnp.zeros(q.shape, BF)], axis=0)


def projected(rows, qkv_weight):
    value = dot_t(rows, projection(qkv_weight))
    return jnp.where(iota(value.shape, 1) == value.shape[1] - 64, 1.0, value).astype(BF)


def front_inner(
    points,
    offsets,
    kinds,
    owners,
    conv_weight,
    gain,
    bias,
    qkv_weight,
    residual,
    base,
    place,
    fetch,
    partial,
    top_scale,
    end_scale,
    normed,
    place_inner,
):
    total = points.shape[0]
    weights = padded_weights(conv_weight[...])
    slots = place.shape[0] // 2
    peers = slots // HALF_SLOTS
    own = owners[...]
    match = iota((peers, total), 0) == own
    before = hot(iota((total, total), 0) < iota((total, total), 1))
    earlier = dot(hot(match), before)
    slot = jnp.sum(jnp.where(match, earlier, 0.0), axis=0, keepdims=True).astype(jnp.int32)
    low = own * HALF_SLOTS + (slot & (HALF_SLOTS - 1))
    spot = jnp.where(slot >= HALF_SLOTS, low + slots, low)
    quarter = (slot >> 2) * 2 + (slot & 1)
    back = quarter * (2 * peers) + own * 2 + ((slot & (HALF_SLOTS - 1)) >> 1)
    column = jnp.transpose(jnp.broadcast_to(back, (8, total)))[:, 0:1]
    one, none = jnp.ones((ROWS, 128), BF), jnp.zeros((ROWS, 128), BF)
    tile_row = jnp.broadcast_to((spot >> 7).astype(F32), (ROWS, total)).astype(BF)
    mark_row = hot(iota((ROWS, total), 0) == (spot & 127))
    blank_row = jnp.zeros((ROWS, total), BF)

    def build_place(start):
        for tile in (start // ROWS, (start + slots) // ROWS):
            here = slice(tile * ROWS, (tile + 1) * ROWS)
            mask = jnp.where(tile_row == jnp.full((ROWS, total), tile, BF), mark_row, blank_row)
            place[here, :ROWS] = mask[:, :ROWS]
            place_inner[here, :] = mask[:, ROWS : total - ROWS]
            place[here, ROWS:] = mask[:, total - ROWS :]

    def build_fetch(start):
        rows = slice(start, start + ROWS)
        value = jnp.broadcast_to(column[rows, :], (ROWS, 128))
        mark = jnp.where((value & 127).astype(F32).astype(BF) == iota((ROWS, 128), 1).astype(F32).astype(BF), one, none)
        tile_of = (value >> 7).astype(F32).astype(BF)
        for tile in range(2 * slots // 128):
            fetch[rows, tile * 128 : (tile + 1) * 128] = jnp.where(
                tile_of == jnp.full((ROWS, 128), tile, BF), mark, none
            )

    pieces = [functools.partial(build_place, n) for n in range(0, slots, ROWS)]
    pieces += [functools.partial(build_fetch, n) for n in range(0, total, ROWS)]
    blocks = range(1, total // ROWS - 1)
    share = len(pieces) // (len(blocks) + 2)
    for block in blocks:
        rows = slice(block * ROWS, (block + 1) * ROWS)
        window = points[block * ROWS - G : (block + 1) * ROWS + G, :]
        conv = windowed_sum(
            codes(offsets[:, rows]),
            0,
            window,
            scale_by(weights, columns(kinds[:, rows])),
            pieces[(block - 1) * share : block * share],
        )
        res, nor = normalize(points[rows, :], conv, gain[...], bias[...])
        out = slice((block - 1) * ROWS, block * ROWS)
        residual[out, :] = res
        normed[out, :] = nor
    last = total - ROWS
    partial[0:ROWS, :] = windowed_sum(
        codes(offsets[:, :ROWS]),
        G,
        points[0 : ROWS + G, :],
        scale_by(weights, columns(kinds[:, :ROWS]), top_scale),
        pieces[2 * share : 3 * share],
    )
    partial[ROWS:, :] = windowed_sum(
        codes(offsets[:, last:]),
        0,
        points[last - G :, :],
        scale_by(weights, columns(kinds[:, last:]), end_scale),
        pieces[3 * share :],
    )
    base[...] = dot(place_inner[...], projected(normed[...], qkv_weight)).astype(BF)


def front_edges(
    got_first,
    got_second,
    points,
    offsets,
    kinds,
    conv_weight,
    gain,
    bias,
    qkv_weight,
    base,
    place,
    partial,
    top_scale,
    end_scale,
    residual,
    out,
    extra_res,
    extra_fetch,
    extra_lead,
):
    total, width = points.shape
    weights = padded_weights(conv_weight[...])
    last = total - ROWS
    even = lax.rem(lax.axis_index("pts"), 2) == 0
    one, two = got_first[...].astype(F32), got_second[...].astype(F32)
    above = jnp.where(even, two[:G], one[:G]).astype(BF)
    below = jnp.where(even, one, two)
    facts = below[G + LEAD :, :128]
    conv = partial[0:ROWS, :] + windowed_sum(
        codes(offsets[:, :ROWS]), 0, above, kept_scale(top_scale)
    )
    res, top = normalize(points[0:ROWS, :], conv, gain[...], bias[...])
    residual[0:ROWS, :] = res
    conv = partial[ROWS:, :] + windowed_sum(
        codes(offsets[:, last:]),
        ROWS + G,
        below[:G].astype(BF),
        kept_scale(end_scale),
    )
    res, end = normalize(points[last:, :], conv, gain[...], bias[...])
    residual[ROWS:, :] = res
    slots = out.shape[0]
    placed = dot(place[...], projected(jnp.concatenate([top, end], axis=0), qkv_weight)) + base[...].astype(F32)
    near_half, far_half = placed[:slots], placed[slots:]
    lane = iota((slots, 128), 1)
    near_moved, far_moved = swap_halves(near_half[:, :128]), swap_halves(far_half[:, :128])
    query = jnp.where(lane < 64, near_half[:, :128], far_moved)
    live = jnp.where(lane < 64, near_half[:, 192:193], far_half[:, 192:193])
    out[:, 0:128] = jnp.where(live > 0.5, query, DEAD).astype(BF)
    out[:, 128:256] = jnp.where(lane < 64, near_moved, far_half[:, :128]).astype(BF)
    out[:, 256:] = jnp.where(lane < 64, near_half[:, 128:], swap_halves(far_half[:, 128:])).astype(BF)
    near = offsets.shape[0]
    padded = jnp.concatenate([facts, jnp.zeros((EXTRA - LEAD, 128), F32)], axis=0)
    code = padded[:, :near] + jnp.where(iota((EXTRA, near), 0) < LEAD, iota((EXTRA, near), 0), 0).astype(F32)
    reach = below[: G + LEAD]
    fill = jnp.zeros((256 - G - LEAD, width), F32)
    window = jnp.concatenate([points[last:, :], jnp.concatenate([reach, fill], axis=0).astype(BF)], axis=0)
    more = jnp.concatenate([reach[:LEAD], jnp.zeros((EXTRA - LEAD, width), F32)], axis=0)
    conv = windowed_sum(code, 0, window, scale_by(weights, padded[:, near : 2 * near]))
    extra_res[...] = (more + conv).astype(BF)
    full = jnp.concatenate([facts, jnp.zeros((EXTRA - LEAD, 128), F32)], axis=0)
    owner, slot, lead = (full[:, 2 * near + 8 * n : 2 * near + 8 * n + 1] for n in range(3))
    index = slot.astype(jnp.int32)
    spot = (index & 1) * (slots // 2) + owner.astype(jnp.int32) * 2 + (index >> 1)
    extra_fetch[...] = hot(spot == iota((EXTRA, slots), 1))
    extra_lead[...] = jnp.broadcast_to(lead, (EXTRA, 128))


def swap_halves(value):
    return jnp.concatenate([value[:, 64:], value[:, :64]], axis=1)


def attend(packed, out, keys, values, kept):
    half = packed.shape[0]
    lane = iota((half, 128), 1)
    q = packed[:, 0:128]
    k = packed[:, 128:256]
    v = packed[:, 256:384]
    qs, ks, vs = (swap_halves(x) for x in (q, k, v))
    zero = jnp.zeros((half, 128), F32)

    def dead_bias(x):
        return jnp.where(x.astype(F32) < 0.1 * DEAD, DEAD, 0.0)

    step = 128
    extra = jnp.where(lane == 64, 1.0, zero)
    for part, (kk, flag) in enumerate(((k, qs), (ks, q))):
        rows = slice(part * half, (part + 1) * half)
        keys[rows, :] = jnp.where(lane < 64, kk.astype(F32), jnp.where(lane == 64, dead_bias(flag), 0.0)).astype(BF)

    def fill_values():
        for part, vv in enumerate((v, vs)):
            rows = slice(part * half, (part + 1) * half)
            values[rows, :] = jnp.where(lane < 64, vv.astype(F32), extra).astype(BF)

    factor = math.log2(math.e) / math.sqrt(HD)
    block_lane = iota((step, 128), 1)

    def scores_of(chunk):
        rows = slice((chunk // 2) * step, (chunk // 2 + 1) * step)
        mine = (q, qs)[chunk % 2][rows].astype(F32)
        pair = []
        for head in range(2):
            inside = (block_lane >= head * HD) & (block_lane < (head + 1) * HD)
            pair.append(jnp.where(inside, mine, extra[:step]).astype(BF))
        return dot_t(jnp.concatenate(pair, axis=0), keys[...])

    def attended_of(scores):
        top = jnp.max(scores, axis=1, keepdims=True)
        soft = jnp.exp2((scores - top) * factor).astype(BF)
        summed = dot(soft, values[...])
        result = summed / summed[:, 64:65]
        return jnp.where(block_lane < HD, result[:step], result[step:])

    chunks = 2 * half // step
    ahead = [scores_of(0)]
    fill_values()
    done = []
    for chunk in range(chunks):
        if chunk + 1 < chunks:
            ahead.append(scores_of(chunk + 1))
        done.append(attended_of(ahead.pop(0)))
        if len(done) == 2:
            first, second = done
            done = []
            moved = jnp.concatenate([second[:, 64:], second[:, :64]], axis=1)
            rows = slice((chunk // 2) * step, (chunk // 2 + 1) * step)
            both = jnp.where(block_lane < 64, first, moved)
            kept[rows, :] = both
    kept[half:, :] = jnp.zeros((8, 128), F32)
    pairs = half // 2
    lane = iota((pairs, 128), 1)
    out[:, :128] = kept[pl.ds(0, pairs, stride=2), :].astype(BF)
    out[:, 128:256] = kept[pl.ds(1, pairs, stride=2), :].astype(BF)
    near, far = kept[pl.ds(HALF_SLOTS, pairs, stride=2), :], kept[pl.ds(HALF_SLOTS + 1, pairs, stride=2), :]
    out[:, 256:] = jnp.where(lane < 64, near, swap_halves(far)).astype(BF)


def fetch_rows(returned, fetch, extra_fetch, out):
    tiles = [returned[:, n * 128 : (n + 1) * 128] for n in range(3)]
    lane = iota(tiles[0].shape, 1)
    zero = jnp.zeros(tiles[0].shape, BF)
    moved = [swap_halves(tile) for tile in tiles]
    order = [tiles[0], tiles[1], moved[0], moved[1]]
    other = [moved[0], moved[1], tiles[0], tiles[1]]
    left = jnp.concatenate([jnp.where(lane < 64, tile, zero) for tile in order], axis=0)
    right = jnp.concatenate([jnp.where(lane < 64, zero, tile) for tile in other], axis=0)
    points = fetch.shape[0] // 2
    rows = (dot(fetch[:points, :], left) + dot(fetch[points:, :], right)).astype(BF)
    extra = dot(extra_fetch[...], jnp.concatenate([tiles[2], moved[2]], axis=0)).astype(BF)
    for peer in range(out.shape[0]):
        out[peer, :points, :] = rows
        out[peer, points:, :] = extra


def finish(
    gathered,
    edge_res,
    inner_res,
    extra_res,
    extra_lead,
    proj_weight,
    pool_weight,
    clusters,
    block_out,
    pooled,
    block,
):
    channels = gathered.shape[0]
    width = proj_weight.shape[1]
    part = width // channels
    wide = jnp.concatenate([gathered[c] for c in range(channels)], axis=1)
    proj = proj_weight[...]
    none = jnp.zeros((part, width), BF)
    low, high = [], []
    for c in range(channels):
        piece = proj[c * part : (c + 1) * part, :]
        low += [piece, none]
        high += [none, piece]
    points = block.shape[0] // 2
    last = 2 * points - ROWS
    first = dot(wide, jnp.concatenate(low, axis=0))
    second = dot(wide[:points], jnp.concatenate(high, axis=0))
    block[0:ROWS, :] = (edge_res[0:ROWS, :].astype(F32) + first[0:ROWS]).astype(BF)
    block[ROWS:points, :] = (inner_res[0 : points - ROWS, :].astype(F32) + first[ROWS:points]).astype(BF)
    block[points:last, :] = (inner_res[points - ROWS :, :].astype(F32) + second[: last - points]).astype(BF)
    block[last:, :] = (edge_res[ROWS:, :].astype(F32) + second[last - points :]).astype(BF)
    extra = (extra_res[...].astype(F32) + first[points:]).astype(BF).astype(F32)
    lead = extra_lead[...]
    spill = jnp.sum(jnp.where(lead[:, 0:1] > 0.5, extra, 0.0), axis=0, keepdims=True)
    spill_count = jnp.sum(lead, axis=0, keepdims=True)
    full = block[...]
    channel = lax.axis_index("ch")
    pick = hot(iota((part, width), 1) == iota((part, width), 0) + channel * part)
    block_out[...] = dot_t(pick, full).astype(BF)
    count = pooled.shape[0]
    base = lax.axis_index("pts") * count
    member = jnp.where(iota((count, 2 * points), 0) == clusters[...] - base, 1.0, 0.0)
    final = iota((count, 1), 0) == count - 1
    value = dot(member.astype(BF), full) + jnp.where(final, spill, 0.0)
    number = jnp.sum(member, axis=1, keepdims=True) + jnp.where(final, spill_count, 0.0)
    upper = value.astype(BF)
    lower = (value - upper.astype(F32)).astype(BF)
    weight = pool_weight[...]
    mean = (dot(upper, weight) + dot(lower, weight)) / number
    pooled[...] = (mean * (1.0 + lax.erf(mean * math.sqrt(0.5))) * 0.5).astype(BF)


def shape(dims, kind=BF):
    return jax.ShapeDtypeStruct(dims, kind)


def shards(
    points_in,
    neighbor_offsets,
    kernel_ids,
    cluster_ids,
    owners,
    conv_weight,
    norm_gain,
    norm_bias,
    qkv_weight,
    proj_weight,
    pool_weight,
):
    total, width = points_in.shape
    entries = neighbor_offsets.shape[1]
    nodes = lax.axis_size("pts")
    channels = lax.axis_size("ch")
    inside = [(i, i ^ 1) for i in range(nodes)]
    across = [(i, ((i + 1) ^ 1) - 1) for i in range(1, nodes - 1)]
    offsets, kinds = jnp.transpose(neighbor_offsets), jnp.transpose(kernel_ids)
    args = (
        points_in,
        offsets,
        kinds,
        owners.reshape(1, total),
        conv_weight,
        norm_gain.reshape(1, width),
        norm_bias.reshape(1, width),
        jnp.transpose(qkv_weight, (0, 2, 1)),
        proj_weight,
        pool_weight,
        cluster_ids.reshape(1, total),
    )
    staged = stage(len(args))(*args)
    points, offsets, kinds, own, conv_weight, gain, bias, qkv_weight, proj_weight, pool_weight = staged[:10]
    clusters_here, first, second = staged[10:]
    got_first = lax.ppermute(first, "pts", inside)
    got_second = lax.ppermute(second, "pts", across)
    slots = nodes * HALF_SLOTS
    inner_rows = total - 2 * ROWS
    inner_res, base, place, fetch, partial, top_scale, end_scale = call(
        front_inner,
        (
            shape((inner_rows, width)),
            shape((2 * slots, width)),
            shape((2 * slots, 2 * ROWS)),
            shape((total, 2 * slots)),
            shape((2 * ROWS, width), F32),
            shape((entries // GROUP, GROUP * ROWS, width)),
            shape((entries // GROUP, GROUP * ROWS, width)),
        ),
        scratch=(pltpu.VMEM((inner_rows, width), BF), pltpu.VMEM((2 * slots, inner_rows), BF)),
        flops=10**9,
        nbytes=4 * 10**6,
        name="front_inner",
    )(points, offsets, kinds, own, conv_weight, gain, bias, qkv_weight)
    edge_res, packed, extra_res, extra_fetch, extra_lead = call(
        front_edges,
        (
            shape((2 * ROWS, width)),
            shape((slots, 384)),
            shape((EXTRA, width)),
            shape((EXTRA, slots)),
            shape((EXTRA, 128), F32),
        ),
        flops=10**9,
        nbytes=4 * 10**6,
        name="front_edges",
    )(
        got_first,
        got_second,
        points,
        offsets,
        kinds,
        conv_weight,
        gain,
        bias,
        qkv_weight,
        base,
        place,
        partial,
        top_scale,
        end_scale,
    )
    arrived = lax.all_to_all(
        packed.reshape(nodes, HALF_SLOTS, 384), "pts", split_axis=0, concat_axis=0, tiled=True
    ).reshape(slots, 384)
    attended = call(
        attend,
        shape((slots // 2, 384)),
        scratch=(
            pltpu.VMEM((2 * slots, 128), BF),
            pltpu.VMEM((2 * slots, 128), BF),
            pltpu.VMEM((slots + 8, 128), F32),
        ),
        flops=10**9,
        nbytes=10**6,
        name="attend",
    )(arrived)
    returned = lax.all_to_all(
        attended.reshape(nodes, 2, 384), "pts", split_axis=0, concat_axis=0, tiled=True
    ).reshape(slots // 2, 384)
    rows = call(
        fetch_rows, shape((channels, total // 2 + EXTRA, 128)), flops=10**8, nbytes=10**6, name="fetch_rows"
    )(returned, fetch, extra_fetch)
    gathered = lax.all_to_all(rows, "ch", split_axis=0, concat_axis=0, tiled=True)
    block_out, pooled = call(
        finish,
        (shape((width // channels, total)), shape((total // 4, pool_weight.shape[1]))),
        scratch=(pltpu.VMEM((total, width), BF),),
        flops=10**8,
        nbytes=10**6,
        name="finish",
    )(gathered, edge_res, inner_res, extra_res, extra_lead, proj_weight, pool_weight, clusters_here)
    return jnp.transpose(block_out), pooled


def solution(mesh):
    return jax.shard_map(
        shards,
        mesh=mesh,
        in_specs=(
            P("pts", None),
            P("pts", None),
            P("pts", None),
            P("pts"),
            P("pts"),
            P(),
            P(),
            P(),
            P(None, None, "ch"),
            P(),
            P(None, "ch"),
        ),
        out_specs=(P("pts", "ch"), P("pts", "ch")),
        check_vma=False,
    )
```

```python
import functools
import math

import jax
import jax.numpy as jnp
from jax import lax
from jax.experimental import pallas as pl
from jax.experimental.pallas import tpu as pltpu
from jax.sharding import PartitionSpec as P

HD = 32
G = 128
ROWS = 128
HALF_SLOTS = 4
DEAD = -1e30
LEAD = 8
HALO = G + 2 * LEAD
EXTRA = 16
GROUP = 4
BF = jnp.bfloat16
F32 = jnp.float32
VMEM_BYTES = 24 * 1024 * 1024


def call(body, outs, scratch=(), flops=0, nbytes=0, name=None, out_space=pltpu.VMEM):
    def run(*args):
        return pl.pallas_call(
            body,
            out_shape=outs,
            in_specs=[pl.BlockSpec(memory_space=pltpu.VMEM)] * len(args),
            out_specs=jax.tree.map(lambda _: pl.BlockSpec(memory_space=out_space), outs),
            scratch_shapes=list(scratch),
            compiler_params=pltpu.CompilerParams(vmem_limit_bytes=VMEM_BYTES),
            cost_estimate=pl.CostEstimate(flops=flops, bytes_accessed=nbytes, transcendentals=0),
            name=name,
        )(*args)

    return run


def iota(shape, dim):
    return lax.broadcasted_iota(jnp.int32, shape, dim)


def hot(mask):
    return jnp.where(mask, 1.0, 0.0).astype(BF)


def dot(a, b):
    return lax.dot_general(a, b, (((1,), (0,)), ((), ())), preferred_element_type=F32)


def dot_t(a, b):
    return lax.dot_general(a, b, (((1,), (1,)), ((), ())), preferred_element_type=F32)


def lead_facts(offsets, kinds, owners, clusters, first_cluster):
    own = owners[:, :128]
    lane = iota(own.shape, 1)
    slot = jnp.zeros(own.shape, F32)
    for back in (1, 2):
        same = (own == jnp.concatenate([own[:, 128 - back :], own[:, : 128 - back]], axis=1)) & (lane >= back)
        slot = slot + jnp.where(same, 1.0, 0.0)
    lead = jnp.where(clusters[:, :128] < first_cluster, 1.0, 0.0)
    lines = [
        offsets[:, :128].astype(F32),
        kinds[:, :128].astype(F32),
        jnp.broadcast_to(own.astype(F32), (8, 128)),
        jnp.broadcast_to(slot, (8, 128)),
        jnp.broadcast_to(lead, (8, 128)),
        jnp.zeros((72, 128), F32),
    ]
    return jnp.transpose(jnp.concatenate(lines, axis=0))[:LEAD, :]


def stage(count):
    def body(*refs):
        sources, targets = refs[:count], refs[count : 2 * count]
        first, second, sems = refs[2 * count :]
        copies = [
            pltpu.make_async_copy(a, b, sems.at[n]) for n, (a, b) in enumerate(zip(sources, targets, strict=True))
        ]
        for copy in copies:
            copy.start()
        points, offsets, kinds, owners = targets[:4]
        clusters = targets[-1]
        total, width = points.shape
        index = lax.axis_index("pts")
        even = lax.rem(index, 2) == 0
        for copy in (*copies[1:4], copies[-1]):
            copy.wait()
        facts = lead_facts(offsets[...], kinds[...], owners[...], clusters[...], index * (total // 4))
        facts = jnp.concatenate([facts, jnp.zeros((LEAD, width - 128), F32)], axis=1)
        copies[0].wait()
        head = jnp.concatenate([points[0:G, :].astype(F32), points[G : G + LEAD, :].astype(F32), facts], axis=0)
        tail = jnp.concatenate([points[total - G :, :].astype(F32), jnp.zeros((2 * LEAD, width), F32)], axis=0)
        first[...] = jnp.where(even, tail, head).astype(BF)
        second[...] = jnp.where(even, head, tail).astype(BF)
        for copy in copies[4:-1]:
            copy.wait()

    def run(*args):
        outs = [jax.ShapeDtypeStruct(a.shape, a.dtype) for a in args]
        outs += [jax.ShapeDtypeStruct((HALO, args[0].shape[1]), args[0].dtype)] * 2
        return pl.pallas_call(
            body,
            out_shape=outs,
            in_specs=[pl.BlockSpec(memory_space=pltpu.HBM)] * count,
            out_specs=[pl.BlockSpec(memory_space=pltpu.VMEM)] * (count + 2),
            scratch_shapes=[pltpu.SemaphoreType.DMA((count,))],
            compiler_params=pltpu.CompilerParams(vmem_limit_bytes=VMEM_BYTES),
            name="stage",
        )(*(pltpu.with_memory_space_constraint(a, pltpu.HBM) for a in args))

    return run


def codes(offsets):
    return jnp.transpose(offsets.astype(F32)) + iota((offsets.shape[1], offsets.shape[0]), 0).astype(F32)


def columns(kinds):
    return jnp.transpose(kinds.astype(F32))


def spread(values, keep=None):
    def value_of(n):
        value = jnp.broadcast_to(values[:, n : n + 1], (values.shape[0], 128)).astype(BF)
        if keep is not None:
            keep[n] = value
        return value

    return value_of


def marks_of(value, first, span):
    lane = iota(value.shape, 1).astype(F32)
    one, none = jnp.ones(value.shape, BF), jnp.zeros(value.shape, BF)
    tiles = [jnp.where(value == (lane + (first + lanes)).astype(BF), one, none) for lanes in range(0, span, 128)]
    return tiles[0] if len(tiles) == 1 else jnp.concatenate(tiles, axis=1)


def windowed_sum(value_of, entries, first_row, window, scale_of, between=()):
    span = window.shape[0]
    between = list(between)
    conv = None
    for first in range(0, entries, GROUP):
        picks = [marks_of(value_of(n), first_row - G, span) for n in range(first, first + GROUP)]
        rows = picks[0].shape[0]
        picked = dot(jnp.concatenate(picks, axis=0), window)
        part = picked * scale_of(first // GROUP)
        for n in range(GROUP):
            piece = part[n * rows : (n + 1) * rows]
            conv = piece if conv is None else conv + piece
        if between:
            between.pop(0)()
    for step in between:
        step()
    return conv


def scale_by(weights, kinds, keep=None):
    def scale_of(group):
        marks = [marks_of(spread(kinds)(n), 0, 128) for n in range(group * GROUP, (group + 1) * GROUP)]
        scale = dot(jnp.concatenate(marks, axis=0), weights)
        if keep is not None:
            keep[group] = scale
        return scale

    return scale_of


def kept_scale(kept):
    return lambda group: kept[group]


def normalize(points, conv, gain, bias):
    residual = (points.astype(F32) + conv).astype(BF)
    features = residual.astype(F32)
    average = jnp.mean(features, axis=1, keepdims=True)
    centered = features - average
    variance = jnp.mean(centered * centered, axis=1, keepdims=True)
    normed = (centered * lax.rsqrt(variance + 1e-05) * gain + bias).astype(BF)
    return residual, normed


def padded_weights(conv_weight):
    kinds = conv_weight.shape[0]
    fill = jnp.zeros((128 - kinds, conv_weight.shape[1]), F32)
    return jnp.concatenate([conv_weight.astype(F32), fill], axis=0).astype(BF)


def projected(rows, qkv_weight):
    q, k, v = (qkv_weight[t] for t in range(3))
    none = jnp.zeros(q.shape, BF)
    near = dot_t(rows, jnp.concatenate([q, k, v, none], axis=0))
    far = dot_t(rows, jnp.concatenate([k, q, none, v], axis=0))
    lane = iota(near.shape, 1)
    near = jnp.where(lane >= 192, 1.0, near)
    far = jnp.where((lane >= 128) & (lane < 192), 1.0, far)
    return near.astype(BF), far.astype(BF)


def front_inner(
    points,
    offsets,
    kinds,
    owners,
    conv_weight,
    gain,
    bias,
    qkv_weight,
    residual,
    base,
    place,
    fetch,
    partial,
    top_scale,
    end_scale,
    top_code,
    end_code,
    normed,
    place_inner,
):
    total = points.shape[0]
    weights = padded_weights(conv_weight[...])
    slots = place.shape[0] // 2
    peers = slots // HALF_SLOTS
    own = owners[...]
    match = iota((peers, total), 0) == own
    before = hot(iota((total, total), 0) < iota((total, total), 1))
    earlier = dot(hot(match), before)
    slot = jnp.sum(jnp.where(match, earlier, 0.0), axis=0, keepdims=True).astype(jnp.int32)
    low = own * HALF_SLOTS + (slot & (HALF_SLOTS - 1))
    spot = jnp.where(slot >= HALF_SLOTS, low + slots, low)
    quarter = (slot >> 2) * 2 + (slot & 1)
    back = quarter * (2 * peers) + own * 2 + ((slot & (HALF_SLOTS - 1)) >> 1)
    column = jnp.transpose(jnp.broadcast_to(back, (8, total)))[:, 0:1]
    one, none = jnp.ones((ROWS, 128), BF), jnp.zeros((ROWS, 128), BF)
    tile_row = jnp.broadcast_to((spot >> 7).astype(F32), (ROWS, total)).astype(BF)
    mark_row = hot(iota((ROWS, total), 0) == (spot & 127))
    blank_row = jnp.zeros((ROWS, total), BF)

    def build_place(start):
        for tile in (start // ROWS, (start + slots) // ROWS):
            here = slice(tile * ROWS, (tile + 1) * ROWS)
            mask = jnp.where(tile_row == jnp.full((ROWS, total), tile, BF), mark_row, blank_row)
            place[here, :ROWS] = mask[:, :ROWS]
            place_inner[here, :] = mask[:, ROWS : total - ROWS]
            place[here, ROWS:] = mask[:, total - ROWS :]

    def build_fetch(start):
        rows = slice(start, start + ROWS)
        value = jnp.broadcast_to(column[rows, :], (ROWS, 128))
        mark = jnp.where((value & 127).astype(F32).astype(BF) == iota((ROWS, 128), 1).astype(F32).astype(BF), one, none)
        tile_of = (value >> 7).astype(F32).astype(BF)
        for tile in range(2 * slots // 128):
            fetch[rows, tile * 128 : (tile + 1) * 128] = jnp.where(
                tile_of == jnp.full((ROWS, 128), tile, BF), mark, none
            )

    pieces = [functools.partial(build_place, n) for n in range(0, slots, ROWS)]
    pieces += [functools.partial(build_fetch, n) for n in range(0, total, ROWS)]
    blocks = range(1, total // ROWS - 1)
    share = len(pieces) // (len(blocks) + 2)
    for block in blocks:
        rows = slice(block * ROWS, (block + 1) * ROWS)
        window = points[block * ROWS - G : (block + 1) * ROWS + G, :]
        conv = windowed_sum(
            spread(codes(offsets[:, rows])),
            offsets.shape[0],
            0,
            window,
            scale_by(weights, columns(kinds[:, rows])),
            pieces[(block - 1) * share : block * share],
        )
        res, nor = normalize(points[rows, :], conv, gain[...], bias[...])
        out = slice((block - 1) * ROWS, block * ROWS)
        residual[out, :] = res
        normed[out, :] = nor
    last = total - ROWS
    partial[0:ROWS, :] = windowed_sum(
        spread(codes(offsets[:, :ROWS]), top_code),
        offsets.shape[0],
        G,
        points[0 : ROWS + G, :],
        scale_by(weights, columns(kinds[:, :ROWS]), top_scale),
        pieces[2 * share : 3 * share],
    )
    partial[ROWS:, :] = windowed_sum(
        spread(codes(offsets[:, last:]), end_code),
        offsets.shape[0],
        0,
        points[last - G :, :],
        scale_by(weights, columns(kinds[:, last:]), end_scale),
        pieces[3 * share :],
    )
    near, far = projected(normed[...], qkv_weight)
    base[:slots, :] = dot(place_inner[:slots, :], near).astype(BF)
    base[slots:, :] = dot(place_inner[slots:, :], far).astype(BF)


def front_edges(
    got_first,
    got_second,
    points,
    conv_weight,
    gain,
    bias,
    qkv_weight,
    base,
    place,
    partial,
    top_scale,
    end_scale,
    top_code,
    end_code,
    residual,
    out,
    extra_res,
    extra_fetch,
    extra_lead,
):
    total, width = points.shape
    weights = padded_weights(conv_weight[...])
    last = total - ROWS
    even = lax.rem(lax.axis_index("pts"), 2) == 0
    one, two = got_first[...].astype(F32), got_second[...].astype(F32)
    above = jnp.where(even, two[:G], one[:G]).astype(BF)
    below = jnp.where(even, one, two)
    facts = below[G + LEAD :, :128]
    conv = partial[0:ROWS, :] + windowed_sum(
        lambda n: top_code[n], top_code.shape[0], 0, above, kept_scale(top_scale)
    )
    res, top = normalize(points[0:ROWS, :], conv, gain[...], bias[...])
    residual[0:ROWS, :] = res
    conv = partial[ROWS:, :] + windowed_sum(
        lambda n: end_code[n],
        end_code.shape[0],
        ROWS + G,
        below[:G].astype(BF),
        kept_scale(end_scale),
    )
    res, end = normalize(points[last:, :], conv, gain[...], bias[...])
    residual[ROWS:, :] = res
    slots = out.shape[0]
    near, far = projected(jnp.concatenate([top, end], axis=0), qkv_weight)
    near_half = dot(place[:slots, :], near) + base[:slots, :].astype(F32)
    far_half = dot(place[slots:, :], far) + base[slots:, :].astype(F32)
    left = iota((slots, 128), 1) < 64
    out[:, 0:128] = jnp.where(left, near_half[:, :128], far_half[:, :128]).astype(BF)
    key = jnp.where(left, far_half[:, :128], near_half[:, :128])
    live = jnp.where(left, far_half[:, 128:], near_half[:, 128:])
    out[:, 128:256] = jnp.where(live > 0.5, key, DEAD).astype(BF)
    out[:, 256:] = jnp.where(left, near_half[:, 128:], far_half[:, 128:]).astype(BF)

    near = top_code.shape[0]
    padded = jnp.concatenate([facts, jnp.zeros((EXTRA - LEAD, 128), F32)], axis=0)
    code = padded[:, :near] + jnp.where(iota((EXTRA, near), 0) < LEAD, iota((EXTRA, near), 0), 0).astype(F32)
    reach = below[: G + LEAD]
    fill = jnp.zeros((256 - G - LEAD, width), F32)
    window = jnp.concatenate([points[last:, :], jnp.concatenate([reach, fill], axis=0).astype(BF)], axis=0)
    more = jnp.concatenate([reach[:LEAD], jnp.zeros((EXTRA - LEAD, width), F32)], axis=0)
    conv = windowed_sum(spread(code), near, 0, window, scale_by(weights, padded[:, near : 2 * near]))
    extra_res[...] = (more + conv).astype(BF)
    full = jnp.concatenate([facts, jnp.zeros((EXTRA - LEAD, 128), F32)], axis=0)
    owner, slot, lead = (full[:, 2 * near + 8 * n : 2 * near + 8 * n + 1] for n in range(3))
    index = slot.astype(jnp.int32)
    spot = (index & 1) * (slots // 2) + owner.astype(jnp.int32) * 2 + (index >> 1)
    extra_fetch[...] = hot(spot == iota((EXTRA, slots), 1))
    extra_lead[...] = jnp.broadcast_to(lead, (EXTRA, 128))


def swap_halves(value):
    return jnp.concatenate([value[:, 64:], value[:, :64]], axis=1)


def attend(packed, out, keys, values, kept):
    half = packed.shape[0]
    lane = iota((half, 128), 1)
    q = packed[:, 0:128]
    k = packed[:, 128:256]
    v = packed[:, 256:384]
    qs, ks, vs = (swap_halves(x) for x in (q, k, v))
    zero = jnp.zeros((half, 128), F32)

    def key_rows(kk, flag):
        kf = kk.astype(F32)
        bias = jnp.where((lane == 64) & (flag.astype(F32) < 0.1 * DEAD), DEAD, zero)
        return jnp.where((lane < 64) & (kf > 0.1 * DEAD), kf, bias).astype(BF)

    step = 128
    extra = jnp.where(lane == 64, 1.0, zero)
    keys[:half, :] = key_rows(ks, k)
    keys[half:, :] = key_rows(k, ks)

    def fill_values():
        for part, vv in enumerate((v, vs)):
            rows = slice(part * half, (part + 1) * half)
            values[rows, :] = jnp.where(lane < 64, vv.astype(F32), extra).astype(BF)

    factor = math.log2(math.e) / math.sqrt(HD)
    block_lane = iota((step, 128), 1)

    def scores_of(chunk):
        rows = slice((chunk // 2) * step, (chunk // 2 + 1) * step)
        mine = (q, qs)[chunk % 2][rows].astype(F32)
        pair = []
        for head in range(2):
            inside = (block_lane >= head * HD) & (block_lane < (head + 1) * HD)
            pair.append(jnp.where(inside, mine, extra[:step]).astype(BF))
        return dot_t(jnp.concatenate(pair, axis=0), keys[...])

    def attended_of(scores):
        top = jnp.max(scores, axis=1, keepdims=True)
        soft = jnp.exp2((scores - top) * factor).astype(BF)
        summed = dot(soft, values[...])
        result = summed / summed[:, 64:65]
        return jnp.where(block_lane < HD, result[:step], result[step:])

    chunks = 2 * half // step
    ahead = [scores_of(0)]
    fill_values()
    done = []
    for chunk in range(chunks):
        if chunk + 1 < chunks:
            ahead.append(scores_of(chunk + 1))
        done.append(attended_of(ahead.pop(0)))
        if len(done) == 2:
            first, second = done
            done = []
            moved = jnp.concatenate([second[:, 64:], second[:, :64]], axis=1)
            rows = slice((chunk // 2) * step, (chunk // 2 + 1) * step)
            both = jnp.where(block_lane < 64, first, moved)
            kept[rows, :] = both
    kept[half:, :] = jnp.zeros((8, 128), F32)
    pairs = half // 2
    lane = iota((pairs, 128), 1)
    out[:, :128] = kept[pl.ds(0, pairs, stride=2), :].astype(BF)
    out[:, 128:256] = kept[pl.ds(1, pairs, stride=2), :].astype(BF)
    near, far = kept[pl.ds(HALF_SLOTS, pairs, stride=2), :], kept[pl.ds(HALF_SLOTS + 1, pairs, stride=2), :]
    out[:, 256:] = jnp.where(lane < 64, near, swap_halves(far)).astype(BF)


def fetch_rows(returned, fetch, extra_fetch, out):
    tiles = [returned[:, n * 128 : (n + 1) * 128] for n in range(3)]
    lane = iota(tiles[0].shape, 1)
    zero = jnp.zeros(tiles[0].shape, BF)
    moved = [swap_halves(tile) for tile in tiles]
    order = [tiles[0], tiles[1], moved[0], moved[1]]
    other = [moved[0], moved[1], tiles[0], tiles[1]]
    left = jnp.concatenate([jnp.where(lane < 64, tile, zero) for tile in order], axis=0)
    right = jnp.concatenate([jnp.where(lane < 64, zero, tile) for tile in other], axis=0)
    points = fetch.shape[0] // 2
    rows = (dot(fetch[:points, :], left) + dot(fetch[points:, :], right)).astype(BF)
    extra = dot(extra_fetch[...], jnp.concatenate([tiles[2], moved[2]], axis=0)).astype(BF)
    for peer in range(out.shape[0]):
        out[peer, :points, :] = rows
        out[peer, points:, :] = extra


def finish(
    gathered,
    edge_res,
    inner_res,
    extra_res,
    extra_lead,
    proj_weight,
    pool_weight,
    clusters,
    block_hbm,
    pooled_hbm,
    block,
    block_out,
    pooled,
    sems,
):
    channels = gathered.shape[0]
    width = proj_weight.shape[1]
    part = width // channels
    wide = jnp.concatenate([gathered[c] for c in range(channels)], axis=1)
    proj = proj_weight[...]
    none = jnp.zeros((part, width), BF)
    low, high = [], []
    for c in range(channels):
        piece = proj[c * part : (c + 1) * part, :]
        low += [piece, none]
        high += [none, piece]
    points = block.shape[0] // 2
    last = 2 * points - ROWS
    first = dot(wide, jnp.concatenate(low, axis=0))
    second = dot(wide[:points], jnp.concatenate(high, axis=0))
    block[0:ROWS, :] = (edge_res[0:ROWS, :].astype(F32) + first[0:ROWS]).astype(BF)
    block[ROWS:points, :] = (inner_res[0 : points - ROWS, :].astype(F32) + first[ROWS:points]).astype(BF)
    block[points:last, :] = (inner_res[points - ROWS :, :].astype(F32) + second[: last - points]).astype(BF)
    block[last:, :] = (edge_res[ROWS:, :].astype(F32) + second[last - points :]).astype(BF)
    extra = (extra_res[...].astype(F32) + first[points:]).astype(BF).astype(F32)
    lead = extra_lead[...]
    spill = jnp.sum(jnp.where(lead[:, 0:1] > 0.5, extra, 0.0), axis=0, keepdims=True)
    spill_count = jnp.sum(lead, axis=0, keepdims=True)
    full = block[...]
    channel = lax.axis_index("ch")
    pick = hot(iota((part, width), 1) == iota((part, width), 0) + channel * part)
    block_out[...] = dot_t(pick, full).astype(BF)
    copies = [
        pltpu.make_async_copy(block_out, block_hbm, sems.at[0]),
        pltpu.make_async_copy(pooled, pooled_hbm, sems.at[1]),
    ]
    copies[0].start()
    count = pooled.shape[0]
    base = lax.axis_index("pts") * count
    member = jnp.where(iota((count, 2 * points), 0) == clusters[...] - base, 1.0, 0.0)
    final = iota((count, 1), 0) == count - 1
    value = dot(member.astype(BF), full) + jnp.where(final, spill, 0.0)
    number = jnp.sum(member, axis=1, keepdims=True) + jnp.where(final, spill_count, 0.0)
    upper = value.astype(BF)
    lower = (value - upper.astype(F32)).astype(BF)
    weight = pool_weight[...]
    mean = (dot(upper, weight) + dot(lower, weight)) / number
    pooled[...] = (mean * (1.0 + lax.erf(mean * math.sqrt(0.5))) * 0.5).astype(BF)
    copies[1].start()
    for copy in copies:
        copy.wait()


def shape(dims, kind=BF):
    return jax.ShapeDtypeStruct(dims, kind)


def shards(
    points_in,
    neighbor_offsets,
    kernel_ids,
    cluster_ids,
    owners,
    conv_weight,
    norm_gain,
    norm_bias,
    qkv_weight,
    proj_weight,
    pool_weight,
):
    total, width = points_in.shape
    entries = neighbor_offsets.shape[1]
    nodes = lax.axis_size("pts")
    channels = lax.axis_size("ch")
    inside = [(i, i ^ 1) for i in range(nodes)]
    across = [(i, ((i + 1) ^ 1) - 1) for i in range(1, nodes - 1)]
    offsets, kinds = jnp.transpose(neighbor_offsets), jnp.transpose(kernel_ids)
    args = (
        points_in,
        offsets,
        kinds,
        owners.reshape(1, total),
        conv_weight,
        norm_gain.reshape(1, width),
        norm_bias.reshape(1, width),
        jnp.transpose(qkv_weight, (0, 2, 1)),
        proj_weight,
        pool_weight,
        cluster_ids.reshape(1, total),
    )
    staged = stage(len(args))(*args)
    points, offsets, kinds, own, conv_weight, gain, bias, qkv_weight, proj_weight, pool_weight = staged[:10]
    clusters_here, first, second = staged[10:]
    got_first = lax.ppermute(first, "pts", inside)
    got_second = lax.ppermute(second, "pts", across)
    slots = nodes * HALF_SLOTS
    inner_rows = total - 2 * ROWS
    inner_res, base, place, fetch, partial, top_scale, end_scale, top_code, end_code = call(
        front_inner,
        (
            shape((inner_rows, width)),
            shape((2 * slots, width)),
            shape((2 * slots, 2 * ROWS)),
            shape((total, 2 * slots)),
            shape((2 * ROWS, width), F32),
            shape((entries // GROUP, GROUP * ROWS, width), F32),
            shape((entries // GROUP, GROUP * ROWS, width), F32),
            shape((entries, ROWS, 128)),
            shape((entries, ROWS, 128)),
        ),
        scratch=(pltpu.VMEM((inner_rows, width), BF), pltpu.VMEM((2 * slots, inner_rows), BF)),
        flops=10**9,
        nbytes=4 * 10**6,
        name="front_inner",
    )(points, offsets, kinds, own, conv_weight, gain, bias, qkv_weight)
    edge_res, packed, extra_res, extra_fetch, extra_lead = call(
        front_edges,
        (
            shape((2 * ROWS, width)),
            shape((slots, 384)),
            shape((EXTRA, width)),
            shape((EXTRA, slots)),
            shape((EXTRA, 128), F32),
        ),
        flops=10**9,
        nbytes=4 * 10**6,
        name="front_edges",
    )(
        got_first,
        got_second,
        points,
        conv_weight,
        gain,
        bias,
        qkv_weight,
        base,
        place,
        partial,
        top_scale,
        end_scale,
        top_code,
        end_code,
    )
    arrived = lax.all_to_all(
        packed.reshape(nodes, HALF_SLOTS, 384), "pts", split_axis=0, concat_axis=0, tiled=True
    ).reshape(slots, 384)
    attended = call(
        attend,
        shape((slots // 2, 384)),
        scratch=(
            pltpu.VMEM((2 * slots, 128), BF),
            pltpu.VMEM((2 * slots, 128), BF),
            pltpu.VMEM((slots + 8, 128), F32),
        ),
        flops=10**9,
        nbytes=10**6,
        name="attend",
    )(arrived)
    returned = lax.all_to_all(
        attended.reshape(nodes, 2, 384), "pts", split_axis=0, concat_axis=0, tiled=True
    ).reshape(slots // 2, 384)
    rows = call(
        fetch_rows, shape((channels, total // 2 + EXTRA, 128)), flops=10**8, nbytes=10**6, name="fetch_rows"
    )(returned, fetch, extra_fetch)
    gathered = lax.all_to_all(rows, "ch", split_axis=0, concat_axis=0, tiled=True)
    block_out, pooled = call(
        finish,
        (shape((width // channels, total)), shape((total // 4, pool_weight.shape[1]))),
        scratch=(
            pltpu.VMEM((total, width), BF),
            pltpu.VMEM((width // channels, total), BF),
            pltpu.VMEM((total // 4, pool_weight.shape[1]), BF),
            pltpu.SemaphoreType.DMA((2,)),
        ),
        flops=10**8,
        nbytes=10**6,
        name="finish",
        out_space=pltpu.HBM,
    )(gathered, edge_res, inner_res, extra_res, extra_lead, proj_weight, pool_weight, clusters_here)
    return jnp.transpose(block_out), pooled


def solution(mesh):
    return jax.shard_map(
        shards,
        mesh=mesh,
        in_specs=(
            P("pts", None),
            P("pts", None),
            P("pts", None),
            P("pts"),
            P("pts"),
            P(),
            P(),
            P(),
            P(None, None, "ch"),
            P(),
            P(None, "ch"),
        ),
        out_specs=(P("pts", "ch"), P("pts", "ch")),
        check_vma=False,
    )
```

```python
import functools
import math

import jax
import jax.numpy as jnp
from jax import lax
from jax.experimental import pallas as pl
from jax.experimental.pallas import tpu as pltpu
from jax.sharding import PartitionSpec as P

HD = 32
G = 128
ROWS = 128
HALF_SLOTS = 4
DEAD = -1e30
LEAD = 8
HALO = G + 2 * LEAD
EXTRA = 16
GROUP = 4
BF = jnp.bfloat16
F32 = jnp.float32
VMEM_BYTES = 24 * 1024 * 1024


def call(body, outs, scratch=(), flops=0, nbytes=0, name=None, out_space=pltpu.VMEM):
    def run(*args):
        return pl.pallas_call(
            body,
            out_shape=outs,
            in_specs=[pl.BlockSpec(memory_space=pltpu.VMEM)] * len(args),
            out_specs=jax.tree.map(lambda _: pl.BlockSpec(memory_space=out_space), outs),
            scratch_shapes=list(scratch),
            compiler_params=pltpu.CompilerParams(vmem_limit_bytes=VMEM_BYTES),
            cost_estimate=pl.CostEstimate(flops=flops, bytes_accessed=nbytes, transcendentals=0),
            name=name,
        )(*args)

    return run


def iota(shape, dim):
    return lax.broadcasted_iota(jnp.int32, shape, dim)


def hot(mask):
    return jnp.where(mask, 1.0, 0.0).astype(BF)


def dot(a, b):
    return lax.dot_general(a, b, (((1,), (0,)), ((), ())), preferred_element_type=F32)


def dot_t(a, b):
    return lax.dot_general(a, b, (((1,), (1,)), ((), ())), preferred_element_type=F32)


def lead_facts(offsets, kinds, owners, clusters, first_cluster):
    own = owners[:, :128]
    lane = iota(own.shape, 1)
    slot = jnp.zeros(own.shape, F32)
    for back in (1, 2):
        same = (own == jnp.concatenate([own[:, 128 - back :], own[:, : 128 - back]], axis=1)) & (lane >= back)
        slot = slot + jnp.where(same, 1.0, 0.0)
    lead = jnp.where(clusters[:, :128] < first_cluster, 1.0, 0.0)
    lines = [
        offsets[:, :128].astype(F32),
        kinds[:, :128].astype(F32),
        jnp.broadcast_to(own.astype(F32), (8, 128)),
        jnp.broadcast_to(slot, (8, 128)),
        jnp.broadcast_to(lead, (8, 128)),
        jnp.zeros((72, 128), F32),
    ]
    return jnp.transpose(jnp.concatenate(lines, axis=0))[:LEAD, :]


def stage(count):
    def body(*refs):
        sources, targets = refs[:count], refs[count : 2 * count]
        first, second, sems = refs[2 * count :]
        copies = [
            pltpu.make_async_copy(a, b, sems.at[n]) for n, (a, b) in enumerate(zip(sources, targets, strict=True))
        ]
        for copy in copies:
            copy.start()
        points, offsets, kinds, owners = targets[:4]
        clusters = targets[-1]
        total, width = points.shape
        index = lax.axis_index("pts")
        even = lax.rem(index, 2) == 0
        for copy in (*copies[1:4], copies[-1]):
            copy.wait()
        facts = lead_facts(offsets[...], kinds[...], owners[...], clusters[...], index * (total // 4))
        facts = jnp.concatenate([facts, jnp.zeros((LEAD, width - 128), F32)], axis=1)
        copies[0].wait()
        head = jnp.concatenate([points[0:G, :].astype(F32), points[G : G + LEAD, :].astype(F32), facts], axis=0)
        tail = jnp.concatenate([points[total - G :, :].astype(F32), jnp.zeros((2 * LEAD, width), F32)], axis=0)
        first[...] = jnp.where(even, tail, head).astype(BF)
        second[...] = jnp.where(even, head, tail).astype(BF)
        for copy in copies[4:-1]:
            copy.wait()

    def run(*args):
        outs = [jax.ShapeDtypeStruct(a.shape, a.dtype) for a in args]
        outs += [jax.ShapeDtypeStruct((HALO, args[0].shape[1]), args[0].dtype)] * 2
        return pl.pallas_call(
            body,
            out_shape=outs,
            in_specs=[pl.BlockSpec(memory_space=pltpu.HBM)] * count,
            out_specs=[pl.BlockSpec(memory_space=pltpu.VMEM)] * (count + 2),
            scratch_shapes=[pltpu.SemaphoreType.DMA((count,))],
            compiler_params=pltpu.CompilerParams(vmem_limit_bytes=VMEM_BYTES),
            name="stage",
        )(*(pltpu.with_memory_space_constraint(a, pltpu.HBM) for a in args))

    return run


def codes(offsets):
    return jnp.transpose(offsets.astype(F32)) + iota((offsets.shape[1], offsets.shape[0]), 0).astype(F32)


def columns(kinds):
    return jnp.transpose(kinds.astype(F32))


def spread(values, keep=None):
    def value_of(n):
        value = jnp.broadcast_to(values[:, n : n + 1], (values.shape[0], 128)).astype(BF)
        if keep is not None:
            keep[n] = value
        return value

    return value_of


def marks_of(value, first, span):
    lane = iota(value.shape, 1).astype(F32)
    one, none = jnp.ones(value.shape, BF), jnp.zeros(value.shape, BF)
    tiles = [jnp.where(value == (lane + (first + lanes)).astype(BF), one, none) for lanes in range(0, span, 128)]
    return tiles[0] if len(tiles) == 1 else jnp.concatenate(tiles, axis=1)


def windowed_sum(value_of, entries, first_row, window, scale_of, between=()):
    span = window.shape[0]
    between = list(between)
    conv = None
    for first in range(0, entries, GROUP):
        picks = [marks_of(value_of(n), first_row - G, span) for n in range(first, first + GROUP)]
        rows = picks[0].shape[0]
        picked = dot(jnp.concatenate(picks, axis=0), window)
        part = picked * scale_of(first // GROUP)
        for n in range(GROUP):
            piece = part[n * rows : (n + 1) * rows]
            conv = piece if conv is None else conv + piece
        if between:
            between.pop(0)()
    for step in between:
        step()
    return conv


def scale_by(weights, kinds, keep=None):
    def scale_of(group):
        marks = [marks_of(spread(kinds)(n), 0, 128) for n in range(group * GROUP, (group + 1) * GROUP)]
        scale = dot(jnp.concatenate(marks, axis=0), weights)
        if keep is not None:
            keep[group] = scale
        return scale

    return scale_of


def kept_scale(kept):
    return lambda group: kept[group]


def normalize(points, conv, gain, bias):
    residual = (points.astype(F32) + conv).astype(BF)
    features = residual.astype(F32)
    average = jnp.mean(features, axis=1, keepdims=True)
    centered = features - average
    variance = jnp.mean(centered * centered, axis=1, keepdims=True)
    normed = (centered * lax.rsqrt(variance + 1e-05) * gain + bias).astype(BF)
    return residual, normed


def padded_weights(conv_weight):
    kinds = conv_weight.shape[0]
    fill = jnp.zeros((128 - kinds, conv_weight.shape[1]), F32)
    return jnp.concatenate([conv_weight.astype(F32), fill], axis=0).astype(BF)


def projected(rows, qkv_weight):
    q, k, v = (qkv_weight[t] for t in range(3))
    none = jnp.zeros(q.shape, BF)
    near = dot_t(rows, jnp.concatenate([q, k, v, none], axis=0))
    far = dot_t(rows, jnp.concatenate([k, q, none, v], axis=0))
    lane = iota(near.shape, 1)
    near = jnp.where(lane >= 192, 1.0, near)
    far = jnp.where((lane >= 128) & (lane < 192), 1.0, far)
    return near.astype(BF), far.astype(BF)


def front_inner(
    points,
    offsets,
    kinds,
    owners,
    conv_weight,
    gain,
    bias,
    qkv_weight,
    residual,
    base,
    place,
    fetch,
    partial,
    top_scale,
    end_scale,
    top_code,
    end_code,
    normed,
    place_inner,
):
    total = points.shape[0]
    weights = padded_weights(conv_weight[...])
    slots = place.shape[0] // 2
    peers = slots // HALF_SLOTS
    own = owners[...]
    match = iota((peers, total), 0) == own
    before = hot(iota((total, total), 0) < iota((total, total), 1))
    earlier = dot(hot(match), before)
    slot = jnp.sum(jnp.where(match, earlier, 0.0), axis=0, keepdims=True).astype(jnp.int32)
    low = own * HALF_SLOTS + (slot & (HALF_SLOTS - 1))
    spot = jnp.where(slot >= HALF_SLOTS, low + slots, low)
    quarter = (slot >> 2) * 2 + (slot & 1)
    back = quarter * (2 * peers) + own * 2 + ((slot & (HALF_SLOTS - 1)) >> 1)
    column = jnp.transpose(jnp.broadcast_to(back, (8, total)))[:, 0:1]
    one, none = jnp.ones((ROWS, 128), BF), jnp.zeros((ROWS, 128), BF)
    tile_row = jnp.broadcast_to((spot >> 7).astype(F32), (ROWS, total)).astype(BF)
    mark_row = hot(iota((ROWS, total), 0) == (spot & 127))
    blank_row = jnp.zeros((ROWS, total), BF)

    def build_place(start):
        for tile in (start // ROWS, (start + slots) // ROWS):
            here = slice(tile * ROWS, (tile + 1) * ROWS)
            mask = jnp.where(tile_row == jnp.full((ROWS, total), tile, BF), mark_row, blank_row)
            place[here, :ROWS] = mask[:, :ROWS]
            place_inner[here, :] = mask[:, ROWS : total - ROWS]
            place[here, ROWS:] = mask[:, total - ROWS :]

    def build_fetch(start):
        rows = slice(start, start + ROWS)
        value = jnp.broadcast_to(column[rows, :], (ROWS, 128))
        mark = jnp.where((value & 127).astype(F32).astype(BF) == iota((ROWS, 128), 1).astype(F32).astype(BF), one, none)
        tile_of = (value >> 7).astype(F32).astype(BF)
        for tile in range(2 * slots // 128):
            fetch[rows, tile * 128 : (tile + 1) * 128] = jnp.where(
                tile_of == jnp.full((ROWS, 128), tile, BF), mark, none
            )

    pieces = [functools.partial(build_place, n) for n in range(0, slots, ROWS)]
    pieces += [functools.partial(build_fetch, n) for n in range(0, total, ROWS)]
    blocks = range(1, total // ROWS - 1)
    share = len(pieces) // (len(blocks) + 2)
    for block in blocks:
        rows = slice(block * ROWS, (block + 1) * ROWS)
        window = points[block * ROWS - G : (block + 1) * ROWS + G, :]
        conv = windowed_sum(
            spread(codes(offsets[:, rows])),
            offsets.shape[0],
            0,
            window,
            scale_by(weights, columns(kinds[:, rows])),
            pieces[(block - 1) * share : block * share],
        )
        res, nor = normalize(points[rows, :], conv, gain[...], bias[...])
        out = slice((block - 1) * ROWS, block * ROWS)
        residual[out, :] = res
        normed[out, :] = nor
    last = total - ROWS
    partial[0:ROWS, :] = windowed_sum(
        spread(codes(offsets[:, :ROWS]), top_code),
        offsets.shape[0],
        G,
        points[0 : ROWS + G, :],
        scale_by(weights, columns(kinds[:, :ROWS]), top_scale),
        pieces[2 * share : 3 * share],
    )
    partial[ROWS:, :] = windowed_sum(
        spread(codes(offsets[:, last:]), end_code),
        offsets.shape[0],
        0,
        points[last - G :, :],
        scale_by(weights, columns(kinds[:, last:]), end_scale),
        pieces[3 * share :],
    )
    near, far = projected(normed[...], qkv_weight)
    base[:slots, :] = dot(place_inner[:slots, :], near).astype(BF)
    base[slots:, :] = dot(place_inner[slots:, :], far).astype(BF)


def front_edges(
    got_first,
    got_second,
    points,
    conv_weight,
    gain,
    bias,
    qkv_weight,
    base,
    place,
    partial,
    top_scale,
    end_scale,
    top_code,
    end_code,
    residual,
    out,
    extra_res,
    extra_fetch,
    extra_lead,
):
    total, width = points.shape
    weights = padded_weights(conv_weight[...])
    last = total - ROWS
    even = lax.rem(lax.axis_index("pts"), 2) == 0
    one, two = got_first[...].astype(F32), got_second[...].astype(F32)
    above = jnp.where(even, two[:G], one[:G]).astype(BF)
    below = jnp.where(even, one, two)
    facts = below[G + LEAD :, :128]
    conv = partial[0:ROWS, :] + windowed_sum(
        lambda n: top_code[n], top_code.shape[0], 0, above, kept_scale(top_scale)
    )
    res, top = normalize(points[0:ROWS, :], conv, gain[...], bias[...])
    residual[0:ROWS, :] = res
    conv = partial[ROWS:, :] + windowed_sum(
        lambda n: end_code[n],
        end_code.shape[0],
        ROWS + G,
        below[:G].astype(BF),
        kept_scale(end_scale),
    )
    res, end = normalize(points[last:, :], conv, gain[...], bias[...])
    residual[ROWS:, :] = res
    slots = out.shape[0]
    near, far = projected(jnp.concatenate([top, end], axis=0), qkv_weight)
    near_half = dot(place[:slots, :], near) + base[:slots, :].astype(F32)
    far_half = dot(place[slots:, :], far) + base[slots:, :].astype(F32)
    left = iota((slots, 128), 1) < 64
    out[:, 0:128] = jnp.where(left, near_half[:, :128], far_half[:, :128]).astype(BF)
    key = jnp.where(left, far_half[:, :128], near_half[:, :128])
    live = jnp.where(left, far_half[:, 128:], near_half[:, 128:])
    out[:, 128:256] = jnp.where(live > 0.5, key, DEAD).astype(BF)
    out[:, 256:] = jnp.where(left, near_half[:, 128:], far_half[:, 128:]).astype(BF)

    near = top_code.shape[0]
    padded = jnp.concatenate([facts, jnp.zeros((EXTRA - LEAD, 128), F32)], axis=0)
    code = padded[:, :near] + jnp.where(iota((EXTRA, near), 0) < LEAD, iota((EXTRA, near), 0), 0).astype(F32)
    reach = below[: G + LEAD]
    fill = jnp.zeros((256 - G - LEAD, width), F32)
    window = jnp.concatenate([points[last:, :], jnp.concatenate([reach, fill], axis=0).astype(BF)], axis=0)
    more = jnp.concatenate([reach[:LEAD], jnp.zeros((EXTRA - LEAD, width), F32)], axis=0)
    conv = windowed_sum(spread(code), near, 0, window, scale_by(weights, padded[:, near : 2 * near]))
    extra_res[...] = (more + conv).astype(BF)
    full = jnp.concatenate([facts, jnp.zeros((EXTRA - LEAD, 128), F32)], axis=0)
    owner, slot, lead = (full[:, 2 * near + 8 * n : 2 * near + 8 * n + 1] for n in range(3))
    index = slot.astype(jnp.int32)
    spot = (index & 1) * (slots // 2) + owner.astype(jnp.int32) * 2 + (index >> 1)
    extra_fetch[...] = hot(spot == iota((EXTRA, slots), 1))
    extra_lead[...] = jnp.broadcast_to(lead, (EXTRA, 128))


def swap_halves(value):
    return jnp.concatenate([value[:, 64:], value[:, :64]], axis=1)


def attend(packed, out, keys, values, kept):
    half = packed.shape[0]
    step = 128
    q = packed[:, 0:128]
    k = packed[:, 128:256]
    v = packed[:, 256:384]
    qs, ks, vs = (swap_halves(x) for x in (q, k, v))

    def lanes(rows):
        return iota((rows, 128), 1).astype(F32).astype(BF)

    def full(value, like):
        return jnp.full(like.shape, value, BF)

    lane = lanes(half)
    zero = full(0.0, lane)
    extra = jnp.where(lane == full(64, lane), full(1.0, lane), zero)
    low = lane < full(64, lane)

    def key_rows(kk, flag):
        alive = jnp.where(kk > full(0.1 * DEAD, lane), kk, zero)
        bias = jnp.where(flag < full(0.1 * DEAD, lane), full(DEAD, lane), zero)
        return jnp.where(low, alive, jnp.where(lane == full(64, lane), bias, zero))

    keys[:half, :] = key_rows(ks, k)
    keys[half:, :] = key_rows(k, ks)

    def fill_values():
        values[:half, :] = jnp.where(low, v, extra)
        values[half:, :] = jnp.where(low, vs, extra)

    factor = math.log2(math.e) / math.sqrt(HD)
    block_lane = iota((step, 128), 1)

    def scores_of(chunk):
        rows = slice((chunk // 2) * step, (chunk // 2 + 1) * step)
        mine, here = (q, qs)[chunk % 2][rows], lanes(step)
        first = jnp.where(here < full(HD, here), mine, extra[:step])
        second = jnp.where(here < full(HD, here), full(0.0, here), jnp.where(here < full(2 * HD, here), mine, extra[:step]))
        return dot_t(jnp.concatenate([first, second], axis=0), keys[...])

    def attended_of(scores):
        top = jnp.max(scores, axis=1, keepdims=True)
        soft = jnp.exp2((scores - top) * factor).astype(BF)
        summed = dot(soft, values[...])
        result = summed / summed[:, 64:65]
        return jnp.where(block_lane < HD, result[:step], result[step:])

    pairs = step // 2

    def store_own(block):
        rows = slice(block * pairs, (block + 1) * pairs)
        out[rows, :128] = kept[pl.ds(block * step, pairs, stride=2), :].astype(BF)
        out[rows, 128:256] = kept[pl.ds(block * step + 1, pairs, stride=2), :].astype(BF)

    def store_next(block):
        near = kept[pl.ds(block * step + HALF_SLOTS, pairs, stride=2), :]
        far = kept[pl.ds(block * step + HALF_SLOTS + 1, pairs, stride=2), :]
        rows = slice(block * pairs, (block + 1) * pairs)
        out[rows, 256:] = jnp.where(iota((pairs, 128), 1) < 64, near, swap_halves(far)).astype(BF)

    chunks = 2 * half // step
    ahead = [scores_of(0)]
    fill_values()
    done = []
    for chunk in range(chunks):
        if chunk + 1 < chunks:
            ahead.append(scores_of(chunk + 1))
        done.append(attended_of(ahead.pop(0)))
        if len(done) == 2:
            first, second = done
            done = []
            moved = jnp.concatenate([second[:, 64:], second[:, :64]], axis=1)
            rows = slice((chunk // 2) * step, (chunk // 2 + 1) * step)
            both = jnp.where(block_lane < 64, first, moved)
            kept[rows, :] = both
            store_own(chunk // 2)
            if chunk > 2:
                store_next(chunk // 2 - 1)
    kept[half:, :] = jnp.zeros((8, 128), F32)
    store_next(half // step - 1)


def fetch_rows(returned, fetch, extra_fetch, out):
    tiles = [returned[:, n * 128 : (n + 1) * 128] for n in range(3)]
    lane = iota(tiles[0].shape, 1)
    zero = jnp.zeros(tiles[0].shape, BF)
    moved = [swap_halves(tile) for tile in tiles]
    order = [tiles[0], tiles[1], moved[0], moved[1]]
    other = [moved[0], moved[1], tiles[0], tiles[1]]
    left = jnp.concatenate([jnp.where(lane < 64, tile, zero) for tile in order], axis=0)
    right = jnp.concatenate([jnp.where(lane < 64, zero, tile) for tile in other], axis=0)
    points = fetch.shape[0] // 2
    rows = (dot(fetch[:points, :], left) + dot(fetch[points:, :], right)).astype(BF)
    extra = dot(extra_fetch[...], jnp.concatenate([tiles[2], moved[2]], axis=0)).astype(BF)
    for peer in range(out.shape[0]):
        out[peer, :points, :] = rows
        out[peer, points:, :] = extra


def finish(
    gathered,
    edge_res,
    inner_res,
    extra_res,
    extra_lead,
    proj_weight,
    pool_weight,
    clusters,
    block_hbm,
    pooled_hbm,
    block,
    block_out,
    pooled,
    sems,
):
    channels = gathered.shape[0]
    width = proj_weight.shape[1]
    part = width // channels
    wide = jnp.concatenate([gathered[c] for c in range(channels)], axis=1)
    proj = proj_weight[...]
    none = jnp.zeros((part, width), BF)
    low, high = [], []
    for c in range(channels):
        piece = proj[c * part : (c + 1) * part, :]
        low += [piece, none]
        high += [none, piece]
    points = block.shape[0] // 2
    last = 2 * points - ROWS
    first = dot(wide, jnp.concatenate(low, axis=0))
    second = dot(wide[:points], jnp.concatenate(high, axis=0))
    block[0:ROWS, :] = (edge_res[0:ROWS, :].astype(F32) + first[0:ROWS]).astype(BF)
    block[ROWS:points, :] = (inner_res[0 : points - ROWS, :].astype(F32) + first[ROWS:points]).astype(BF)
    block[points:last, :] = (inner_res[points - ROWS :, :].astype(F32) + second[: last - points]).astype(BF)
    block[last:, :] = (edge_res[ROWS:, :].astype(F32) + second[last - points :]).astype(BF)
    extra = (extra_res[...].astype(F32) + first[points:]).astype(BF).astype(F32)
    lead = extra_lead[...]
    spill = jnp.sum(jnp.where(lead[:, 0:1] > 0.5, extra, 0.0), axis=0, keepdims=True)
    spill_count = jnp.sum(lead, axis=0, keepdims=True)
    full = block[...]
    channel = lax.axis_index("ch")
    pick = hot(iota((part, width), 1) == iota((part, width), 0) + channel * part)
    block_out[...] = dot_t(pick, full).astype(BF)
    copies = [
        pltpu.make_async_copy(block_out, block_hbm, sems.at[0]),
        pltpu.make_async_copy(pooled, pooled_hbm, sems.at[1]),
    ]
    copies[0].start()
    count = pooled.shape[0]
    base = lax.axis_index("pts") * count
    member = jnp.where(iota((count, 2 * points), 0) == clusters[...] - base, 1.0, 0.0)
    final = iota((count, 1), 0) == count - 1
    value = dot(member.astype(BF), full) + jnp.where(final, spill, 0.0)
    number = jnp.sum(member, axis=1, keepdims=True) + jnp.where(final, spill_count, 0.0)
    upper = value.astype(BF)
    lower = (value - upper.astype(F32)).astype(BF)
    weight = pool_weight[...]
    mean = (dot(upper, weight) + dot(lower, weight)) / number
    pooled[...] = (mean * (1.0 + lax.erf(mean * math.sqrt(0.5))) * 0.5).astype(BF)
    copies[1].start()
    for copy in copies:
        copy.wait()


def shape(dims, kind=BF):
    return jax.ShapeDtypeStruct(dims, kind)


def shards(
    points_in,
    neighbor_offsets,
    kernel_ids,
    cluster_ids,
    owners,
    conv_weight,
    norm_gain,
    norm_bias,
    qkv_weight,
    proj_weight,
    pool_weight,
):
    total, width = points_in.shape
    entries = neighbor_offsets.shape[1]
    nodes = lax.axis_size("pts")
    channels = lax.axis_size("ch")
    inside = [(i, i ^ 1) for i in range(nodes)]
    across = [(i, ((i + 1) ^ 1) - 1) for i in range(1, nodes - 1)]
    offsets, kinds = jnp.transpose(neighbor_offsets), jnp.transpose(kernel_ids)
    args = (
        points_in,
        offsets,
        kinds,
        owners.reshape(1, total),
        conv_weight,
        norm_gain.reshape(1, width),
        norm_bias.reshape(1, width),
        jnp.transpose(qkv_weight, (0, 2, 1)),
        proj_weight,
        pool_weight,
        cluster_ids.reshape(1, total),
    )
    staged = stage(len(args))(*args)
    points, offsets, kinds, own, conv_weight, gain, bias, qkv_weight, proj_weight, pool_weight = staged[:10]
    clusters_here, first, second = staged[10:]
    got_second = lax.ppermute(second, "pts", across)
    got_first = lax.ppermute(first, "pts", inside)
    slots = nodes * HALF_SLOTS
    inner_rows = total - 2 * ROWS
    inner_res, base, place, fetch, partial, top_scale, end_scale, top_code, end_code = call(
        front_inner,
        (
            shape((inner_rows, width)),
            shape((2 * slots, width)),
            shape((2 * slots, 2 * ROWS)),
            shape((total, 2 * slots)),
            shape((2 * ROWS, width), F32),
            shape((entries // GROUP, GROUP * ROWS, width), F32),
            shape((entries // GROUP, GROUP * ROWS, width), F32),
            shape((entries, ROWS, 128)),
            shape((entries, ROWS, 128)),
        ),
        scratch=(pltpu.VMEM((inner_rows, width), BF), pltpu.VMEM((2 * slots, inner_rows), BF)),
        flops=10**9,
        nbytes=4 * 10**6,
        name="front_inner",
    )(points, offsets, kinds, own, conv_weight, gain, bias, qkv_weight)
    edge_res, packed, extra_res, extra_fetch, extra_lead = call(
        front_edges,
        (
            shape((2 * ROWS, width)),
            shape((slots, 384)),
            shape((EXTRA, width)),
            shape((EXTRA, slots)),
            shape((EXTRA, 128), F32),
        ),
        flops=10**9,
        nbytes=4 * 10**6,
        name="front_edges",
    )(
        got_first,
        got_second,
        points,
        conv_weight,
        gain,
        bias,
        qkv_weight,
        base,
        place,
        partial,
        top_scale,
        end_scale,
        top_code,
        end_code,
    )
    arrived = lax.all_to_all(
        packed.reshape(nodes, HALF_SLOTS, 384), "pts", split_axis=0, concat_axis=0, tiled=True
    ).reshape(slots, 384)
    attended = call(
        attend,
        shape((slots // 2, 384)),
        scratch=(
            pltpu.VMEM((2 * slots, 128), BF),
            pltpu.VMEM((2 * slots, 128), BF),
            pltpu.VMEM((slots + 8, 128), F32),
        ),
        flops=10**9,
        nbytes=10**6,
        name="attend",
    )(arrived)
    returned = lax.all_to_all(
        attended.reshape(nodes, 2, 384), "pts", split_axis=0, concat_axis=0, tiled=True
    ).reshape(slots // 2, 384)
    rows = call(
        fetch_rows, shape((channels, total // 2 + EXTRA, 128)), flops=10**8, nbytes=10**6, name="fetch_rows"
    )(returned, fetch, extra_fetch)
    gathered = lax.all_to_all(rows, "ch", split_axis=0, concat_axis=0, tiled=True)
    block_out, pooled = call(
        finish,
        (shape((width // channels, total)), shape((total // 4, pool_weight.shape[1]))),
        scratch=(
            pltpu.VMEM((total, width), BF),
            pltpu.VMEM((width // channels, total), BF),
            pltpu.VMEM((total // 4, pool_weight.shape[1]), BF),
            pltpu.SemaphoreType.DMA((2,)),
        ),
        flops=10**8,
        nbytes=10**6,
        name="finish",
        out_space=pltpu.HBM,
    )(gathered, edge_res, inner_res, extra_res, extra_lead, proj_weight, pool_weight, clusters_here)
    return jnp.transpose(block_out), pooled


def solution(mesh):
    return jax.shard_map(
        shards,
        mesh=mesh,
        in_specs=(
            P("pts", None),
            P("pts", None),
            P("pts", None),
            P("pts"),
            P("pts"),
            P(),
            P(),
            P(),
            P(None, None, "ch"),
            P(),
            P(None, "ch"),
        ),
        out_specs=(P("pts", "ch"), P("pts", "ch")),
        check_vma=False,
    )
```

```python
import functools
import math

import jax
import jax.numpy as jnp
from jax import lax
from jax.experimental import pallas as pl
from jax.experimental.pallas import tpu as pltpu
from jax.sharding import PartitionSpec as P


HD = 32
G = 128
ROWS = 128
HALF_SLOTS = 4
DEAD = -1e30
LEAD = 8
HALO = G + 2 * LEAD
EXTRA = 16
GROUP = 4
BF = jnp.bfloat16
F32 = jnp.float32
VMEM_BYTES = 24 * 1024 * 1024


def call(body, outs, scratch=(), flops=0, nbytes=0, out_space=pltpu.VMEM):
    def run(*args):
        return pl.pallas_call(
            body,
            out_shape=outs,
            in_specs=[pl.BlockSpec(memory_space=pltpu.VMEM)] * len(args),
            out_specs=jax.tree.map(lambda _: pl.BlockSpec(memory_space=out_space), outs),
            scratch_shapes=list(scratch),
            compiler_params=pltpu.CompilerParams(vmem_limit_bytes=VMEM_BYTES),
            cost_estimate=pl.CostEstimate(flops=flops, bytes_accessed=nbytes, transcendentals=0),
        )(*args)

    return run


def iota(shape, dim):
    return lax.broadcasted_iota(jnp.int32, shape, dim)


def hot(mask):
    return jnp.where(mask, 1.0, 0.0).astype(BF)


def dot(a, b):
    return lax.dot_general(a, b, (((1,), (0,)), ((), ())), preferred_element_type=F32)


def dot_t(a, b):
    return lax.dot_general(a, b, (((1,), (1,)), ((), ())), preferred_element_type=F32)


def lead_facts(offsets, kinds, owners, clusters, first_cluster):
    own = owners[:, :128]
    lane = iota(own.shape, 1)
    slot = jnp.zeros(own.shape, F32)
    for back in (1, 2):
        same = (own == jnp.concatenate([own[:, 128 - back :], own[:, : 128 - back]], axis=1)) & (lane >= back)
        slot = slot + jnp.where(same, 1.0, 0.0)
    lead = jnp.where(clusters[:, :128] < first_cluster, 1.0, 0.0)
    lines = [
        offsets[:, :128].astype(F32),
        kinds[:, :128].astype(F32),
        jnp.broadcast_to(own.astype(F32), (8, 128)),
        jnp.broadcast_to(slot, (8, 128)),
        jnp.broadcast_to(lead, (8, 128)),
        jnp.zeros((72, 128), F32),
    ]
    return jnp.transpose(jnp.concatenate(lines, axis=0))[:LEAD, :]


def stage(count):
    def body(*refs):
        sources, targets = refs[:count], refs[count : 2 * count]
        first, second, sems = refs[2 * count :]
        copies = [
            pltpu.make_async_copy(a, b, sems.at[n]) for n, (a, b) in enumerate(zip(sources, targets, strict=True))
        ]
        for copy in copies:
            copy.start()
        points, offsets, kinds, owners = targets[:4]
        clusters = targets[-1]
        total, width = points.shape
        index = lax.axis_index("pts")
        even = lax.rem(index, 2) == 0
        for copy in (*copies[1:4], copies[-1]):
            copy.wait()
        facts = lead_facts(offsets[...], kinds[...], owners[...], clusters[...], index * (total // 4))
        facts = jnp.concatenate([facts, jnp.zeros((LEAD, width - 128), F32)], axis=1)
        copies[0].wait()
        head = jnp.concatenate([points[0:G, :].astype(F32), points[G : G + LEAD, :].astype(F32), facts], axis=0)
        tail = jnp.concatenate([points[total - G :, :].astype(F32), jnp.zeros((2 * LEAD, width), F32)], axis=0)
        first[...] = jnp.where(even, tail, head).astype(BF)
        second[...] = jnp.where(even, head, tail).astype(BF)
        for copy in copies[4:-1]:
            copy.wait()

    def run(*args):
        outs = [jax.ShapeDtypeStruct(a.shape, a.dtype) for a in args]
        outs += [jax.ShapeDtypeStruct((HALO, args[0].shape[1]), args[0].dtype)] * 2
        return pl.pallas_call(
            body,
            out_shape=outs,
            in_specs=[pl.BlockSpec(memory_space=pltpu.HBM)] * count,
            out_specs=[pl.BlockSpec(memory_space=pltpu.VMEM)] * (count + 2),
            scratch_shapes=[pltpu.SemaphoreType.DMA((count,))],
            compiler_params=pltpu.CompilerParams(vmem_limit_bytes=VMEM_BYTES),
            name="stage",
        )(*(pltpu.with_memory_space_constraint(a, pltpu.HBM) for a in args))

    return run


def codes(offsets):
    return jnp.transpose(offsets.astype(F32)) + iota((offsets.shape[1], offsets.shape[0]), 0).astype(F32)


def columns(kinds):
    return jnp.transpose(kinds.astype(F32))


def spread(values, keep=None):
    def value_of(n):
        value = jnp.broadcast_to(values[:, n : n + 1], (values.shape[0], 128)).astype(BF)
        if keep is not None:
            keep[n] = value
        return value

    return value_of


def marks_of(value, first, span):
    lane = iota(value.shape, 1).astype(F32)
    one, none = jnp.ones(value.shape, BF), jnp.zeros(value.shape, BF)
    tiles = [jnp.where(value == (lane + (first + lanes)).astype(BF), one, none) for lanes in range(0, span, 128)]
    return tiles[0] if len(tiles) == 1 else jnp.concatenate(tiles, axis=1)


def windowed_sum(value_of, entries, first_row, window, scale_of, between=()):
    span = window.shape[0]
    between = list(between)
    conv = None
    for first in range(0, entries, GROUP):
        picks = [marks_of(value_of(n), first_row - G, span) for n in range(first, first + GROUP)]
        rows = picks[0].shape[0]
        picked = dot(jnp.concatenate(picks, axis=0), window)
        part = picked * scale_of(first // GROUP)
        for n in range(GROUP):
            piece = part[n * rows : (n + 1) * rows]
            conv = piece if conv is None else conv + piece
        if between:
            between.pop(0)()
    for step in between:
        step()
    return conv


def scale_by(weights, kinds, keep=None):
    def scale_of(group):
        marks = [marks_of(spread(kinds)(n), 0, 128) for n in range(group * GROUP, (group + 1) * GROUP)]
        scale = dot(jnp.concatenate(marks, axis=0), weights)
        if keep is not None:
            keep[group] = scale
        return scale

    return scale_of


def kept_scale(kept):
    return lambda group: kept[group]


def normalize(points, conv, gain, bias):
    residual = (points.astype(F32) + conv).astype(BF)
    features = residual.astype(F32)
    average = jnp.mean(features, axis=1, keepdims=True)
    centered = features - average
    variance = jnp.mean(centered * centered, axis=1, keepdims=True)
    normed = (centered * lax.rsqrt(variance + 1e-05) * gain + bias).astype(BF)
    return residual, normed


def padded_weights(conv_weight):
    kinds = conv_weight.shape[0]
    fill = jnp.zeros((128 - kinds, conv_weight.shape[1]), F32)
    return jnp.concatenate([conv_weight.astype(F32), fill], axis=0).astype(BF)


def projected(rows, qkv_weight):
    q, k, v = (qkv_weight[t] for t in range(3))
    none = jnp.zeros(q.shape, BF)
    near = dot_t(rows, jnp.concatenate([q, k, v, none], axis=0))
    far = dot_t(rows, jnp.concatenate([k, q, none, v], axis=0))
    lane = iota(near.shape, 1)
    near = jnp.where(lane >= 192, 1.0, near)
    far = jnp.where((lane >= 128) & (lane < 192), 1.0, far)
    return near.astype(BF), far.astype(BF)


def front_inner(
    points,
    offsets,
    kinds,
    owners,
    conv_weight,
    gain,
    bias,
    qkv_weight,
    residual,
    base,
    place,
    fetch,
    partial,
    top_scale,
    end_scale,
    top_code,
    end_code,
    normed,
    place_inner,
):
    total = points.shape[0]
    weights = padded_weights(conv_weight[...])
    slots = place.shape[0] // 2
    peers = slots // HALF_SLOTS
    own = owners[...]
    match = iota((peers, total), 0) == own
    before = hot(iota((total, total), 0) < iota((total, total), 1))
    earlier = dot(hot(match), before)
    slot = jnp.sum(jnp.where(match, earlier, 0.0), axis=0, keepdims=True).astype(jnp.int32)
    low = own * HALF_SLOTS + (slot & (HALF_SLOTS - 1))
    spot = jnp.where(slot >= HALF_SLOTS, low + slots, low)
    quarter = (slot >> 2) * 2 + (slot & 1)
    back = quarter * (2 * peers) + own * 2 + ((slot & (HALF_SLOTS - 1)) >> 1)
    column = jnp.transpose(jnp.broadcast_to(back, (8, total)))[:, 0:1]
    one, none = jnp.ones((ROWS, 128), BF), jnp.zeros((ROWS, 128), BF)
    tile_row = jnp.broadcast_to((spot >> 7).astype(F32), (ROWS, total)).astype(BF)
    mark_row = hot(iota((ROWS, total), 0) == (spot & 127))
    blank_row = jnp.zeros((ROWS, total), BF)

    def build_place(start):
        for tile in (start // ROWS, (start + slots) // ROWS):
            here = slice(tile * ROWS, (tile + 1) * ROWS)
            mask = jnp.where(tile_row == jnp.full((ROWS, total), tile, BF), mark_row, blank_row)
            place[here, :ROWS] = mask[:, :ROWS]
            place_inner[here, :] = mask[:, ROWS : total - ROWS]
            place[here, ROWS:] = mask[:, total - ROWS :]

    def build_fetch(start):
        rows = slice(start, start + ROWS)
        value = jnp.broadcast_to(column[rows, :], (ROWS, 128))
        mark = jnp.where((value & 127).astype(F32).astype(BF) == iota((ROWS, 128), 1).astype(F32).astype(BF), one, none)
        tile_of = (value >> 7).astype(F32).astype(BF)
        for tile in range(2 * slots // 128):
            fetch[rows, tile * 128 : (tile + 1) * 128] = jnp.where(
                tile_of == jnp.full((ROWS, 128), tile, BF), mark, none
            )

    pieces = [functools.partial(build_place, n) for n in range(0, slots, ROWS)]
    pieces += [functools.partial(build_fetch, n) for n in range(0, total, ROWS)]
    blocks = range(1, total // ROWS - 1)
    share = len(pieces) // (len(blocks) + 2)
    for block in blocks:
        rows = slice(block * ROWS, (block + 1) * ROWS)
        window = points[block * ROWS - G : (block + 1) * ROWS + G, :]
        conv = windowed_sum(
            spread(codes(offsets[:, rows])),
            offsets.shape[0],
            0,
            window,
            scale_by(weights, columns(kinds[:, rows])),
            pieces[(block - 1) * share : block * share],
        )
        res, nor = normalize(points[rows, :], conv, gain[...], bias[...])
        out = slice((block - 1) * ROWS, block * ROWS)
        residual[out, :] = res
        normed[out, :] = nor
    last = total - ROWS
    partial[0:ROWS, :] = windowed_sum(
        spread(codes(offsets[:, :ROWS]), top_code),
        offsets.shape[0],
        G,
        points[0 : ROWS + G, :],
        scale_by(weights, columns(kinds[:, :ROWS]), top_scale),
        pieces[2 * share : 3 * share],
    )
    partial[ROWS:, :] = windowed_sum(
        spread(codes(offsets[:, last:]), end_code),
        offsets.shape[0],
        0,
        points[last - G :, :],
        scale_by(weights, columns(kinds[:, last:]), end_scale),
        pieces[3 * share :],
    )
    near, far = projected(normed[...], qkv_weight)
    base[:slots, :] = dot(place_inner[:slots, :], near).astype(BF)
    base[slots:, :] = dot(place_inner[slots:, :], far).astype(BF)


def front_edges(
    got_first,
    got_second,
    points,
    conv_weight,
    gain,
    bias,
    qkv_weight,
    base,
    place,
    partial,
    top_scale,
    end_scale,
    top_code,
    end_code,
    residual,
    out,
    extra_res,
    extra_fetch,
    extra_lead,
):
    total, width = points.shape
    weights = padded_weights(conv_weight[...])
    last = total - ROWS
    even = lax.rem(lax.axis_index("pts"), 2) == 0
    one, two = got_first[...].astype(F32), got_second[...].astype(F32)
    above = jnp.where(even, two[:G], one[:G]).astype(BF)
    below = jnp.where(even, one, two)
    facts = below[G + LEAD :, :128]
    conv = partial[0:ROWS, :] + windowed_sum(
        lambda n: top_code[n], top_code.shape[0], 0, above, kept_scale(top_scale)
    )
    res, top = normalize(points[0:ROWS, :], conv, gain[...], bias[...])
    residual[0:ROWS, :] = res
    conv = partial[ROWS:, :] + windowed_sum(
        lambda n: end_code[n],
        end_code.shape[0],
        ROWS + G,
        below[:G].astype(BF),
        kept_scale(end_scale),
    )
    res, end = normalize(points[last:, :], conv, gain[...], bias[...])
    residual[ROWS:, :] = res
    slots = out.shape[0]
    near, far = projected(jnp.concatenate([top, end], axis=0), qkv_weight)
    near_half = dot(place[:slots, :], near) + base[:slots, :].astype(F32)
    far_half = dot(place[slots:, :], far) + base[slots:, :].astype(F32)
    left = iota((slots, 128), 1) < 64
    out[:, 0:128] = jnp.where(left, near_half[:, :128], far_half[:, :128]).astype(BF)
    key = jnp.where(left, far_half[:, :128], near_half[:, :128])
    live = jnp.where(left, far_half[:, 128:], near_half[:, 128:])
    out[:, 128:256] = jnp.where(live > 0.5, key, DEAD).astype(BF)
    out[:, 256:] = jnp.where(left, near_half[:, 128:], far_half[:, 128:]).astype(BF)

    near = top_code.shape[0]
    padded = jnp.concatenate([facts, jnp.zeros((EXTRA - LEAD, 128), F32)], axis=0)
    code = padded[:, :near] + jnp.where(iota((EXTRA, near), 0) < LEAD, iota((EXTRA, near), 0), 0).astype(F32)
    reach = below[: G + LEAD]
    fill = jnp.zeros((256 - G - LEAD, width), F32)
    window = jnp.concatenate([points[last:, :], jnp.concatenate([reach, fill], axis=0).astype(BF)], axis=0)
    more = jnp.concatenate([reach[:LEAD], jnp.zeros((EXTRA - LEAD, width), F32)], axis=0)
    conv = windowed_sum(spread(code), near, 0, window, scale_by(weights, padded[:, near : 2 * near]))
    extra_res[...] = (more + conv).astype(BF)
    full = jnp.concatenate([facts, jnp.zeros((EXTRA - LEAD, 128), F32)], axis=0)
    owner, slot, lead = (full[:, 2 * near + 8 * n : 2 * near + 8 * n + 1] for n in range(3))
    index = slot.astype(jnp.int32)
    spot = (index & 1) * (slots // 2) + owner.astype(jnp.int32) * 2 + (index >> 1)
    extra_fetch[...] = hot(spot == iota((EXTRA, slots), 1))
    extra_lead[...] = jnp.broadcast_to(lead, (EXTRA, 128))


def swap_halves(value):
    return jnp.concatenate([value[:, 64:], value[:, :64]], axis=1)


def attend(packed, out, keys, values, kept):
    half = packed.shape[0]
    step = 128
    q = packed[:, 0:128]
    k = packed[:, 128:256]
    v = packed[:, 256:384]
    qs, ks, vs = (swap_halves(x) for x in (q, k, v))

    def lanes(rows):
        return iota((rows, 128), 1).astype(F32).astype(BF)

    def full(value, like):
        return jnp.full(like.shape, value, BF)

    lane = lanes(half)
    zero = full(0.0, lane)
    extra = jnp.where(lane == full(64, lane), full(1.0, lane), zero)
    low = lane < full(64, lane)

    def key_rows(kk, flag):
        alive = jnp.where(kk > full(0.1 * DEAD, lane), kk, zero)
        bias = jnp.where(flag < full(0.1 * DEAD, lane), full(DEAD, lane), zero)
        return jnp.where(low, alive, jnp.where(lane == full(64, lane), bias, zero))

    keys[:half, :] = key_rows(ks, k)
    keys[half:, :] = key_rows(k, ks)

    def fill_values():
        values[:half, :] = jnp.where(low, v, extra)
        values[half:, :] = jnp.where(low, vs, extra)

    factor = math.log2(math.e) / math.sqrt(HD)
    block_lane = iota((step, 128), 1)

    def scores_of(chunk):
        rows = slice((chunk // 2) * step, (chunk // 2 + 1) * step)
        mine, here = (q, qs)[chunk % 2][rows], lanes(step)
        first = jnp.where(here < full(HD, here), mine, extra[:step])
        second = jnp.where(here < full(HD, here), full(0.0, here), jnp.where(here < full(2 * HD, here), mine, extra[:step]))
        return dot_t(jnp.concatenate([first, second], axis=0), keys[...])

    def attended_of(scores):
        top = jnp.max(scores, axis=1, keepdims=True)
        soft = jnp.exp2((scores - top) * factor).astype(BF)
        summed = dot(soft, values[...])
        result = summed / summed[:, 64:65]
        return jnp.where(block_lane < HD, result[:step], result[step:])

    pairs = step // 2

    def store_own(block):
        rows = slice(block * pairs, (block + 1) * pairs)
        out[rows, :128] = kept[pl.ds(block * step, pairs, stride=2), :].astype(BF)
        out[rows, 128:256] = kept[pl.ds(block * step + 1, pairs, stride=2), :].astype(BF)

    def store_next(block):
        near = kept[pl.ds(block * step + HALF_SLOTS, pairs, stride=2), :]
        far = kept[pl.ds(block * step + HALF_SLOTS + 1, pairs, stride=2), :]
        rows = slice(block * pairs, (block + 1) * pairs)
        out[rows, 256:] = jnp.where(iota((pairs, 128), 1) < 64, near, swap_halves(far)).astype(BF)

    chunks = 2 * half // step
    ahead = [scores_of(0)]
    fill_values()
    done = []
    for chunk in range(chunks):
        if chunk + 1 < chunks:
            ahead.append(scores_of(chunk + 1))
        done.append(attended_of(ahead.pop(0)))
        if len(done) == 2:
            first, second = done
            done = []
            moved = jnp.concatenate([second[:, 64:], second[:, :64]], axis=1)
            rows = slice((chunk // 2) * step, (chunk // 2 + 1) * step)
            both = jnp.where(block_lane < 64, first, moved)
            kept[rows, :] = both
            store_own(chunk // 2)
            if chunk > 2:
                store_next(chunk // 2 - 1)
    kept[half:, :] = jnp.zeros((8, 128), F32)
    store_next(half // step - 1)


def fetch_rows(returned, fetch, extra_fetch, out):
    tiles = [returned[:, n * 128 : (n + 1) * 128] for n in range(3)]
    lane = iota(tiles[0].shape, 1)
    zero = jnp.zeros(tiles[0].shape, BF)
    moved = [swap_halves(tile) for tile in tiles]
    order = [tiles[0], tiles[1], moved[0], moved[1]]
    other = [moved[0], moved[1], tiles[0], tiles[1]]
    left = jnp.concatenate([jnp.where(lane < 64, tile, zero) for tile in order], axis=0)
    right = jnp.concatenate([jnp.where(lane < 64, zero, tile) for tile in other], axis=0)
    points = fetch.shape[0] // 2
    rows = (dot(fetch[:points, :], left) + dot(fetch[points:, :], right)).astype(BF)
    extra = dot(extra_fetch[...], jnp.concatenate([tiles[2], moved[2]], axis=0)).astype(BF)
    for peer in range(out.shape[0]):
        out[peer, :points, :] = rows
        out[peer, points:, :] = extra


def finish(
    gathered,
    edge_res,
    inner_res,
    extra_res,
    extra_lead,
    proj_weight,
    pool_weight,
    clusters,
    block_hbm,
    pooled_hbm,
    block,
    block_out,
    pooled,
    sems,
):
    channels = gathered.shape[0]
    width = proj_weight.shape[1]
    part = width // channels
    wide = jnp.concatenate([gathered[c] for c in range(channels)], axis=1)
    proj = proj_weight[...]
    none = jnp.zeros((part, width), BF)
    low, high = [], []
    for c in range(channels):
        piece = proj[c * part : (c + 1) * part, :]
        low += [piece, none]
        high += [none, piece]
    points = block.shape[0] // 2
    last = 2 * points - ROWS
    first = dot(wide, jnp.concatenate(low, axis=0))
    second = dot(wide[:points], jnp.concatenate(high, axis=0))
    block[0:ROWS, :] = (edge_res[0:ROWS, :].astype(F32) + first[0:ROWS]).astype(BF)
    block[ROWS:points, :] = (inner_res[0 : points - ROWS, :].astype(F32) + first[ROWS:points]).astype(BF)
    block[points:last, :] = (inner_res[points - ROWS :, :].astype(F32) + second[: last - points]).astype(BF)
    block[last:, :] = (edge_res[ROWS:, :].astype(F32) + second[last - points :]).astype(BF)
    extra = (extra_res[...].astype(F32) + first[points:]).astype(BF).astype(F32)
    lead = extra_lead[...]
    spill = jnp.sum(jnp.where(lead[:, 0:1] > 0.5, extra, 0.0), axis=0, keepdims=True)
    spill_count = jnp.sum(lead, axis=0, keepdims=True)
    full = block[...]
    channel = lax.axis_index("ch")
    pick = hot(iota((part, width), 1) == iota((part, width), 0) + channel * part)
    block_out[...] = dot_t(pick, full).astype(BF)
    copies = [
        pltpu.make_async_copy(block_out, block_hbm, sems.at[0]),
        pltpu.make_async_copy(pooled, pooled_hbm, sems.at[1]),
    ]
    copies[0].start()
    count = pooled.shape[0]
    base = lax.axis_index("pts") * count
    member = jnp.where(iota((count, 2 * points), 0) == clusters[...] - base, 1.0, 0.0)
    final = iota((count, 1), 0) == count - 1
    value = dot(member.astype(BF), full) + jnp.where(final, spill, 0.0)
    number = jnp.sum(member, axis=1, keepdims=True) + jnp.where(final, spill_count, 0.0)
    upper = value.astype(BF)
    lower = (value - upper.astype(F32)).astype(BF)
    weight = pool_weight[...]
    mean = (dot(upper, weight) + dot(lower, weight)) / number
    pooled[...] = (mean * (1.0 + lax.erf(mean * math.sqrt(0.5))) * 0.5).astype(BF)
    copies[1].start()
    for copy in copies:
        copy.wait()


def shape(dims, kind=BF):
    return jax.ShapeDtypeStruct(dims, kind)


def shards(
    points_in,
    neighbor_offsets,
    kernel_ids,
    cluster_ids,
    owners,
    conv_weight,
    norm_gain,
    norm_bias,
    qkv_weight,
    proj_weight,
    pool_weight,
):
    total, width = points_in.shape
    entries = neighbor_offsets.shape[1]
    nodes = lax.axis_size("pts")
    channels = lax.axis_size("ch")
    inside = [(i, i ^ 1) for i in range(nodes)]
    across = [(i, ((i + 1) ^ 1) - 1) for i in range(1, nodes - 1)]
    offsets, kinds = jnp.transpose(neighbor_offsets), jnp.transpose(kernel_ids)
    args = (
        points_in,
        offsets,
        kinds,
        owners.reshape(1, total),
        conv_weight,
        norm_gain.reshape(1, width),
        norm_bias.reshape(1, width),
        jnp.transpose(qkv_weight, (0, 2, 1)),
        proj_weight,
        pool_weight,
        cluster_ids.reshape(1, total),
    )
    staged = stage(len(args))(*args)
    points, offsets, kinds, own, conv_weight, gain, bias, qkv_weight, proj_weight, pool_weight = staged[:10]
    clusters_here, first, second = staged[10:]
    got_second = lax.ppermute(second, "pts", across)
    got_first = lax.ppermute(first, "pts", inside)
    slots = nodes * HALF_SLOTS
    inner_rows = total - 2 * ROWS
    inner_res, base, place, fetch, partial, top_scale, end_scale, top_code, end_code = call(
        front_inner,
        (
            shape((inner_rows, width)),
            shape((2 * slots, width)),
            shape((2 * slots, 2 * ROWS)),
            shape((total, 2 * slots)),
            shape((2 * ROWS, width), F32),
            shape((entries // GROUP, GROUP * ROWS, width), F32),
            shape((entries // GROUP, GROUP * ROWS, width), F32),
            shape((entries, ROWS, 128)),
            shape((entries, ROWS, 128)),
        ),
        scratch=(pltpu.VMEM((inner_rows, width), BF), pltpu.VMEM((2 * slots, inner_rows), BF)),
        flops=10**9,
        nbytes=4 * 10**6,
    )(points, offsets, kinds, own, conv_weight, gain, bias, qkv_weight)
    edge_res, packed, extra_res, extra_fetch, extra_lead = call(
        front_edges,
        (
            shape((2 * ROWS, width)),
            shape((slots, 384)),
            shape((EXTRA, width)),
            shape((EXTRA, slots)),
            shape((EXTRA, 128), F32),
        ),
        flops=10**9,
        nbytes=4 * 10**6,
    )(
        got_first,
        got_second,
        points,
        conv_weight,
        gain,
        bias,
        qkv_weight,
        base,
        place,
        partial,
        top_scale,
        end_scale,
        top_code,
        end_code,
    )
    arrived = lax.all_to_all(
        packed.reshape(nodes, HALF_SLOTS, 384), "pts", split_axis=0, concat_axis=0, tiled=True
    ).reshape(slots, 384)
    attended = call(
        attend,
        shape((slots // 2, 384)),
        scratch=(
            pltpu.VMEM((2 * slots, 128), BF),
            pltpu.VMEM((2 * slots, 128), BF),
            pltpu.VMEM((slots + 8, 128), F32),
        ),
        flops=10**9,
        nbytes=10**6,
    )(arrived)
    returned = lax.all_to_all(
        attended.reshape(nodes, 2, 384), "pts", split_axis=0, concat_axis=0, tiled=True
    ).reshape(slots // 2, 384)
    rows = call(
        fetch_rows, shape((channels, total // 2 + EXTRA, 128)), flops=10**8, nbytes=10**6
    )(returned, fetch, extra_fetch)
    gathered = lax.all_to_all(rows, "ch", split_axis=0, concat_axis=0, tiled=True)
    block_out, pooled = call(
        finish,
        (shape((width // channels, total)), shape((total // 4, pool_weight.shape[1]))),
        scratch=(
            pltpu.VMEM((total, width), BF),
            pltpu.VMEM((width // channels, total), BF),
            pltpu.VMEM((total // 4, pool_weight.shape[1]), BF),
            pltpu.SemaphoreType.DMA((2,)),
        ),
        flops=10**8,
        nbytes=10**6,
        out_space=pltpu.HBM,
    )(gathered, edge_res, inner_res, extra_res, extra_lead, proj_weight, pool_weight, clusters_here)
    return jnp.transpose(block_out), pooled


def solution(mesh):
    return jax.shard_map(
        shards,
        mesh=mesh,
        in_specs=(
            P("pts", None),
            P("pts", None),
            P("pts", None),
            P("pts"),
            P("pts"),
            P(),
            P(),
            P(),
            P(None, None, "ch"),
            P(),
            P(None, "ch"),
        ),
        out_specs=(P("pts", "ch"), P("pts", "ch")),
        check_vma=False,
    )
```
